32 devices in a mesh: req: 4 (over y, x), tok: 8 (over z, core).
Axes of the slice: x: 2, y: 2, z: 4, core: 2. Of those that a mesh axis runs over, the one named last changes fastest.
Arguments:
- activations: bfloat16 [4, 128, 2048], P('req', 'tok'), may hold values from -4 to 4
- cache_entries: bfloat16 [4, 512, 4096], P('req', 'tok'), may hold values from -162 to 162
- cache_lengths: int32 [4], P('req'), may hold values from 128 to 512, as said below
- attention_gain: float32 [2048], replicated, may hold values from 0.5 to 1.5
- feedforward_gain: float32 [2048], replicated, may hold values from 0.5 to 1.5
- key_value_weight: bfloat16 [2048, 4096], P('tok', 'req'), may hold values from -0.125 to 0.125
- attention_router: bfloat16 [2048, 8], replicated, may hold values from -0.125 to 0.125
- attention_routes: int32 [4, 128, 2], P('req', 'tok'), may hold values from 0 to 7, all different within a row; in each aligned block of 16 rows (0 to 15, 16 to 31, ..., all dimensions but the last counted through in order) at most 6 rows name the same one
- query_weight: bfloat16 [8, 2048, 2048], P('tok'), may hold values from -0.125 to 0.125
- output_weight: bfloat16 [8, 2048, 2048], P('tok'), may hold values from -0.125 to 0.125
- feedforward_router: bfloat16 [2048, 8], replicated, may hold values from -0.125 to 0.125
- feedforward_routes: int32 [4, 128, 2], P('req', 'tok'), may hold values from 0 to 7, all different within a row; in each aligned block of 16 rows (0 to 15, 16 to 31, ..., all dimensions but the last counted through in order) at most 6 rows name the same one
- gate_up: bfloat16 [8, 2048, 11264], P('tok'), may hold values from -0.125 to 0.125
- down_weight: bfloat16 [8, 5632, 2048], P('tok'), may hold values from -0.078125 to 0.078125
Outputs:
- layer_output: bfloat16 [4, 128, 2048], P('req', 'tok')
- new_keys_values: bfloat16 [4, 128, 4096], P('req', 'tok')
The draws below stay inside these ranges and needn't reach their ends.
Inputs may be any that keep to these rules, and one draw needn't show every extreme that they name: `cache_lengths`: some request's cache is full. `attention_routes`: each row names 2 different experts; in the rows of one device (aligned blocks of 16 rows, requests and tokens taken together in order) no expert is named by more than 6 rows, a bound that some block reaches. `feedforward_routes`: as for attention_routes.
All inputs are finite; a program needn't handle non-finite values.
Results may differ from the reference program's by a relative error of at most 0.015.
The reference program's roundings to bfloat16 on the way count: a program that leaves them out, or rounds other values in their place, can miss the bound.
Values may be sent and summed in bfloat16 or wider, within the bound.
No kernel may reach another device: no remote copies, remote signals or barrier semaphores. Data moves between devices by JAX's collectives and lax.ppermute only.
A program may use at most 192 MiB of HBM per device.

```python
import math
import jax
import jax.numpy as jnp
import numpy as np
from jax import lax

D = 2048
HEADS = 16
HEAD_DIM = 128
EXPERTS = 8
FF = 5632
TOPK = 2
QB = 16
CAP = 6
HG = 16
HS = 5632
KVW = 4096
SLOTS = 8
REQ = 4
NEW_TOKENS = 128
CACHE = 512
N_TOK = 8


def draw_cache_lengths(key, part):
    lowest = CACHE // 4
    lengths = jax.random.randint(jax.random.fold_in(key, 11), (REQ,), lowest, CACHE + 1)
    full_request = jax.random.randint(jax.random.fold_in(key, 12), (), 0, REQ)
    return jnp.where(jnp.arange(REQ) == full_request, CACHE, lengths).astype(jnp.int32)


def draw_cache_entries(key, part):
    base = jnp.clip(jax.random.normal(jax.random.fold_in(key, 21), (REQ, CACHE, KVW), jnp.float32), -6.0, 6.0)
    return base.astype(jnp.bfloat16)


def level_of(rng, extent, pieces, least, top_value):
    def one(dim, shards_of):
        draws = jax.random.uniform(jax.random.fold_in(jax.random.fold_in(rng, 6), dim), (shards_of,), jnp.float32, least / len(pieces), top_value / len(pieces))
        return jnp.repeat(jnp.exp(draws), extent[dim] // shards_of).reshape((-1,) + (1,) * (len(extent) - dim - 1))

    factor_of = one(*pieces[0])
    for cut in pieces[1:]:
        factor_of = factor_of * one(*cut)
    return factor_of


def deal_out(key, own, number, rows, count, top, limit, skew):
    ranking = jax.random.permutation(key, count)
    heavy_load, ordinary = load_shares(count, rows * top, limit, skew, True), load_shares(count, rows * top, limit, skew, False)
    places = jnp.arange(count)

    def named(sizes, offset_by):
        used = int((sizes > 0).sum())
        fixed = max(1, used // 4)
        shifted = fixed + (places - fixed + offset_by * (used - fixed)) % max(1, count - fixed)
        return jnp.zeros((count,), jnp.int32).at[ranking[jnp.where(places < fixed, places, shifted)]].set(jnp.asarray(sizes, jnp.int32))

    sizes = jnp.where(number % 4 == 0, named(heavy_load, number // 4), named(ordinary, number - number // 4 - 1))
    mixed = jax.random.permutation(jax.random.fold_in(own, 3), count)
    source_of, sink = mixed[0:count // 2 * 2:2], mixed[1:count // 2 * 2:2]
    room = jnp.minimum(sizes[source_of] - 1, limit - sizes[sink]) // 2
    room = jnp.where((source_of == ranking[0]) | (sink == ranking[0]) | (sizes[sink] == 0), 0, jnp.maximum(room, 0))
    shifted = jax.random.randint(jax.random.fold_in(own, 4), (count // 2,), 0, 1 << 20) % (room + 1)
    sizes = sizes.at[source_of].add(-shifted).at[sink].add(shifted)
    items = jnp.searchsorted(jnp.cumsum(sizes), jnp.arange(rows * top), side="right").astype(jnp.int32)
    grid = items.reshape(top, rows).T
    grid = grid[jax.random.permutation(jax.random.fold_in(own, 1), rows)]
    offset_by = jax.random.randint(jax.random.fold_in(own, 2), (rows, 1), 0, top)
    return jnp.take_along_axis(grid, (jnp.arange(top)[None, :] + offset_by) % top, axis=1)


def load_shares(count, total, most, skew, full):
    loads = [(1 << 20) // math.isqrt(rank ** skew) + 1 for rank in range(1, count + 1)]
    largest = most if full else min(most, max(-(-total // count), total * loads[0] // sum(loads)))
    least = 1 if total - largest >= count - 1 else 0
    given, surplus = [largest] + [least] * (count - 1), total - largest - least * (count - 1)
    while surplus > 0:
        free = [i for i in range(1, count) if given[i] < largest] or [i for i in range(1, count) if given[i] < most]
        whole, left = sum([loads[i] for i in free]), surplus
        for i in free:
            extra = min(most - given[i], max(1, left * loads[i] // whole), surplus)
            given[i] = given[i] + extra
            surplus = surplus - extra
    return np.array(given)


def noise(key, shape, scale, reach, split=(), kind=jnp.bfloat16):
    values = jax.random.normal(key, shape, jnp.float32) * scale
    if len(split) > 0:
        values = level_of(key, shape, split, -0.22, 0.18) * values
    return jnp.clip(values, min=-reach, max=reach).astype(kind)


def setup_inputs(seed: int = 0) -> dict:
    key_list = jax.random.split(jax.random.key(seed), 15)
    activations = noise(key_list[0], (REQ, NEW_TOKENS, D), 0.5, 4.0, ((0, 4), (1, 8)))
    cache_entries = draw_cache_entries(jax.random.fold_in(key_list[14], 71), 0)
    cache_lengths = draw_cache_lengths(jax.random.fold_in(key_list[14], 71), 0)
    attention_gain = jnp.clip(1.0 + 0.1 * jax.random.normal(key_list[3], (D,), jnp.float32), 0.5, 1.5)
    feedforward_gain = jnp.clip(1.0 + 0.1 * jax.random.normal(key_list[4], (D,), jnp.float32), 0.5, 1.5)
    key_value_weight = noise(key_list[5], (D, KVW), D ** -0.5, 0.125, ((0, 8), (1, 4)))
    attention_router = noise(key_list[6], (D, EXPERTS), D ** -0.5, 0.125)
    attention_routes_keys = jax.random.split(jax.random.fold_in(key_list[7], 1), REQ * NEW_TOKENS // QB)
    attention_routes_turns = jax.random.permutation(jax.random.fold_in(key_list[7], 3), REQ * NEW_TOKENS // QB)
    attention_routes = jax.vmap(lambda own, number: deal_out(jax.random.fold_in(key_list[7], 2), own, number, QB, EXPERTS, TOPK, CAP, 1))(attention_routes_keys, attention_routes_turns).reshape((REQ, NEW_TOKENS, TOPK))
    query_weight = noise(key_list[8], (SLOTS, D, HG * HEAD_DIM), D ** -0.5, 0.125, ((0, 8),))
    output_weight = noise(key_list[9], (SLOTS, HG * HEAD_DIM, D), (HEADS * HEAD_DIM) ** -0.5, 0.125, ((0, 8),))
    feedforward_router = noise(key_list[10], (D, EXPERTS), D ** -0.5, 0.125)
    feedforward_routes_keys = jax.random.split(jax.random.fold_in(key_list[11], 1), REQ * NEW_TOKENS // QB)
    feedforward_routes_turns = jax.random.permutation(jax.random.fold_in(key_list[11], 3), REQ * NEW_TOKENS // QB)
    feedforward_routes = jax.vmap(lambda own, number: deal_out(jax.random.fold_in(key_list[11], 2), own, number, QB, EXPERTS, TOPK, CAP, 1))(feedforward_routes_keys, feedforward_routes_turns).reshape((REQ, NEW_TOKENS, TOPK))
    gate_up = noise(key_list[12], (SLOTS, D, 2 * HS), D ** -0.5, 0.125, ((0, 8),))
    down_weight = noise(key_list[13], (SLOTS, HS, D), FF ** -0.5, 0.078125, ((0, 8),))
    return {"activations": activations, "cache_entries": cache_entries, "cache_lengths": cache_lengths, "attention_gain": attention_gain, "feedforward_gain": feedforward_gain, "key_value_weight": key_value_weight, "attention_router": attention_router, "attention_routes": attention_routes, "query_weight": query_weight, "output_weight": output_weight, "feedforward_router": feedforward_router, "feedforward_routes": feedforward_routes, "gate_up": gate_up, "down_weight": down_weight}


def normed(values, gain):
    scale_rows = lax.rsqrt(lax.optimization_barrier(jnp.mean(values * values, axis=-1, keepdims=True)) + 1e-06)
    return values * scale_rows * gain

def slot_index(routes):
    labels = jnp.arange(EXPERTS, dtype=jnp.int32)
    onehot = (routes[:, :, None] == labels[None, None, :]).astype(jnp.int32)
    blocks = onehot.reshape(N_TOK, QB * TOPK, EXPERTS)
    before = (jnp.cumsum(blocks, axis=1) - blocks).astype(jnp.int32)
    within = lax.optimization_barrier(jnp.sum(before * blocks, axis=-1)).astype(jnp.int32).reshape(NEW_TOKENS, TOPK)
    block_of = jnp.arange(NEW_TOKENS, dtype=jnp.int32) // QB
    return (block_of[:, None] * CAP + within).astype(jnp.int32)

def slot_table(routes, slots):
    pair_ids = jnp.arange(NEW_TOKENS * TOPK, dtype=jnp.int32).reshape(NEW_TOKENS, TOPK)
    table = jnp.full((EXPERTS, N_TOK * CAP), NEW_TOKENS * TOPK, dtype=jnp.int32)
    return table.at[routes, slots].set(pair_ids)

def gate_of(hidden, router, routes):
    logits = jnp.dot(hidden, router, preferred_element_type=jnp.float32)
    picked = jnp.take_along_axis(logits, routes, axis=1)
    return jax.nn.sigmoid(2.0 * picked - lax.optimization_barrier(jnp.sum(picked, axis=1, keepdims=True)))

def attend(queries, keys, values, usable):
    scores = jnp.dot(queries, keys.T, preferred_element_type=jnp.float32) * (1.0 / math.sqrt(HEAD_DIM))
    scores = jnp.where(usable, scores, -1e+30)
    row_max = lax.optimization_barrier(jnp.max(scores, axis=-1, keepdims=True))
    weights = jnp.where(usable, jnp.exp(scores - row_max), 0.0).astype(jnp.bfloat16)
    row_sums = lax.optimization_barrier(jnp.sum(weights.astype(jnp.float32), axis=-1, keepdims=True))
    return (jnp.dot(weights, values, preferred_element_type=jnp.float32) / row_sums).astype(jnp.bfloat16)

def reference(activations, cache_entries, cache_lengths, attention_gain, feedforward_gain, key_value_weight, attention_router, attention_routes, query_weight, output_weight, feedforward_router, feedforward_routes, gate_up, down_weight):
    groups = N_TOK // EXPERTS
    width = HEADS * HEAD_DIM
    residual_in = activations.astype(jnp.float32)
    hidden = normed(residual_in, attention_gain).astype(jnp.bfloat16)
    new_keys_values = jnp.dot(hidden.reshape(REQ * NEW_TOKENS, D), key_value_weight, preferred_element_type=jnp.float32).astype(jnp.bfloat16).reshape(REQ, NEW_TOKENS, KVW)
    query_full = query_weight.reshape(EXPERTS, groups, D, HG * HEAD_DIM).transpose(0, 2, 1, 3).reshape(EXPERTS, D, width)
    output_full = output_weight.reshape(EXPERTS, groups, HG * HEAD_DIM, D)
    gate_full = gate_up.reshape(EXPERTS, groups, D, 2 * HS)
    down_full = down_weight.reshape(EXPERTS, groups, HS, D)
    pair_token = jnp.arange(NEW_TOKENS * TOPK, dtype=jnp.int32) // TOPK
    key_slot = jnp.arange(CACHE + NEW_TOKENS, dtype=jnp.int32)

    def request_layer(item):
        hidden_r, residual_r, cache_r, length_r, fresh_r, attn_routes, ffn_routes = item
        attn_gate = gate_of(hidden_r, attention_router, attn_routes)
        attn_slots = slot_index(attn_routes)
        attn_table = slot_table(attn_routes, attn_slots)
        padded_hidden = jnp.concatenate([hidden_r, jnp.zeros((1, D), jnp.bfloat16)], axis=0)
        slot_rows = padded_hidden[attn_table // TOPK]

        def project_query(pair):
            return jnp.dot(pair[0], pair[1], preferred_element_type=jnp.float32).astype(jnp.bfloat16)
        query_rows = lax.map(project_query, (slot_rows, query_full))
        queries = query_rows[attn_routes, attn_slots].reshape(NEW_TOKENS * TOPK, HEADS, HEAD_DIM)
        keys = jnp.concatenate([cache_r[:, :width], fresh_r[:, :width]], axis=0).reshape(CACHE + NEW_TOKENS, HEADS, HEAD_DIM)
        values = jnp.concatenate([cache_r[:, width:], fresh_r[:, width:]], axis=0).reshape(CACHE + NEW_TOKENS, HEADS, HEAD_DIM)
        usable = jnp.where(key_slot[None, :] < CACHE, (key_slot < length_r)[None, :], (key_slot - CACHE)[None, :] <= pair_token[:, None])

        def per_head(triple):
            return attend(triple[0], triple[1], triple[2], usable)
        attended = lax.map(per_head, (queries.transpose(1, 0, 2), keys.transpose(1, 0, 2), values.transpose(1, 0, 2)))
        attended = attended.transpose(1, 0, 2).reshape(NEW_TOKENS * TOPK, width)
        padded_attended = jnp.concatenate([attended, jnp.zeros((1, width), jnp.bfloat16)], axis=0)
        attended_rows = padded_attended[attn_table]

        def project_output(pair):
            rows_e, weight_e = pair
            parts = jnp.einsum('rgf,gfd->grd', rows_e.reshape(N_TOK * CAP, groups, HG * HEAD_DIM).astype(jnp.float32), weight_e.astype(jnp.float32), precision=lax.Precision.HIGHEST)
            return lax.optimization_barrier(jnp.sum(lax.optimization_barrier(parts.astype(jnp.bfloat16)).astype(jnp.float32), axis=0))
        output_rows = lax.map(project_output, (attended_rows, output_full))
        attn_out = lax.optimization_barrier(jnp.sum(attn_gate[:, :, None] * output_rows[attn_routes, attn_slots], axis=1))
        mixed_rows = (residual_r + attn_out).astype(jnp.bfloat16)
        hidden_two = normed(mixed_rows.astype(jnp.float32), feedforward_gain).astype(jnp.bfloat16)
        ffn_gate = gate_of(hidden_two, feedforward_router, ffn_routes)
        ffn_slots = slot_index(ffn_routes)
        ffn_table = slot_table(ffn_routes, ffn_slots)
        padded_two = jnp.concatenate([hidden_two, jnp.zeros((1, D), jnp.bfloat16)], axis=0)
        slot_rows_two = padded_two[ffn_table // TOPK]

        def project_expert(triple):
            rows_e, gate_e, down_e = triple

            def shard_part(pair):
                projected = jnp.dot(rows_e, pair[0], preferred_element_type=jnp.float32)
                active = (jax.nn.silu(projected[:, :HS]) * projected[:, HS:]).astype(jnp.bfloat16)
                return lax.optimization_barrier(jnp.dot(active, pair[1], preferred_element_type=jnp.float32).astype(jnp.bfloat16)).astype(jnp.float32)
            return lax.optimization_barrier(jnp.sum(lax.map(shard_part, (gate_e, down_e)), axis=0))
        expert_rows = lax.map(project_expert, (slot_rows_two, gate_full, down_full))
        ffn_out = lax.optimization_barrier(jnp.sum(ffn_gate[:, :, None] * expert_rows[ffn_routes, ffn_slots], axis=1))
        return (mixed_rows.astype(jnp.float32) + ffn_out).astype(jnp.bfloat16)
    layer_output = lax.map(request_layer, (hidden, residual_in, cache_entries, cache_lengths, new_keys_values, attention_routes, feedforward_routes))
    return (layer_output, new_keys_values)
```

```python
import math

import jax
import jax.numpy as jnp
from jax import lax
from jax.experimental import pallas as pl
from jax.experimental.pallas import tpu as pltpu
from jax.sharding import PartitionSpec as P

HEADS = 16
HEAD_DIM = 128
CAP = 6


def normed(values, gain):
    scale_rows = lax.rsqrt(jnp.mean(values * values, axis=-1, keepdims=True) + 1e-06)
    return values * scale_rows * gain


def slot_matrix(routes, experts, capacity):
    row_count, top_count = routes.shape
    labels = jnp.arange(experts, dtype=jnp.int32)
    onehot = (routes.reshape(row_count * top_count, 1) == labels[None, :]).astype(jnp.int32)
    before = jnp.cumsum(onehot, axis=0) - onehot
    within = jnp.sum(before * onehot, axis=1)
    placed = routes.reshape(row_count * top_count) * capacity + within
    columns = jnp.arange(experts * capacity, dtype=jnp.int32)
    return (placed[:, None] == columns[None, :]).astype(jnp.float32)


def router_gates(hidden, router, routes):
    logits = jnp.dot(hidden, router, preferred_element_type=jnp.float32)
    picked = jnp.take_along_axis(logits, routes, axis=1)
    return jax.nn.sigmoid(2.0 * picked - jnp.sum(picked, axis=1, keepdims=True))


def token_matrices(pair_slots, gates, top_count):
    row_count = gates.shape[0]
    per_token = pair_slots.reshape(row_count, top_count, -1)
    picked = jnp.sum(per_token, axis=1)
    weighted = jnp.sum(per_token * gates[:, :, None], axis=1)
    return (picked, weighted)


def spread_slots(slot_rows, experts, groups, capacity):
    feat_width = slot_rows.shape[-1]
    shaped = slot_rows.reshape(experts, 1, capacity, feat_width)
    return jnp.broadcast_to(shaped, (experts, groups, capacity, feat_width)).reshape(
        experts * groups, capacity, feat_width
    )


def head_groups(rows, experts, groups, group_width):
    row_count = rows.shape[0]
    shaped = (
        rows.reshape(row_count, 2, groups, group_width)
        .transpose(2, 0, 1, 3)
        .reshape(groups, row_count, 2 * group_width)
    )
    return jnp.broadcast_to(shaped[None], (experts, groups, row_count, 2 * group_width)).reshape(
        experts * groups, row_count, 2 * group_width
    )


def group_sum(received, experts, groups, capacity):
    feat_width = received.shape[-1]
    summed = jnp.sum(
        received.reshape(experts, groups, capacity, feat_width).astype(jnp.float32), axis=1
    )
    return summed.reshape(experts * capacity, feat_width)


def expert_feedforward(received, gate_piece, down_piece):
    units = down_piece.shape[0]
    projected = jnp.einsum("scd,df->scf", received, gate_piece, preferred_element_type=jnp.float32)
    active = (jax.nn.silu(projected[..., :units]) * projected[..., units:]).astype(jnp.bfloat16)
    return jnp.einsum("scf,fd->scd", active, down_piece, preferred_element_type=jnp.float32).astype(
        jnp.bfloat16
    )


def local(
    activations,
    cache_entries,
    cache_lengths,
    attention_gain,
    feedforward_gain,
    key_value_weight,
    attention_router,
    attention_routes,
    query_weight,
    output_weight,
    feedforward_router,
    feedforward_routes,
    gate_up,
    down_weight,
):
    tok_count = lax.axis_size("tok")
    tok_index = lax.axis_index("tok")
    experts = attention_router.shape[1]
    groups = tok_count // experts
    query_rows = activations.shape[1]
    cache_rows = cache_entries.shape[1]
    top_count = attention_routes.shape[2]
    model_width = activations.shape[2]
    head_count = HEADS // groups
    group_width = head_count * HEAD_DIM
    block_span = cache_rows + query_rows
    score_scale = 1.0 / math.sqrt(HEAD_DIM)
    cache_part = cache_entries[0]
    residual_in = activations[0].astype(jnp.float32)
    hidden = normed(residual_in, attention_gain).astype(jnp.bfloat16)
    stacked = lax.all_gather(hidden, "req", axis=0, tiled=True)
    projected_part = jnp.dot(
        stacked,
        lax.all_gather(key_value_weight, "tok", axis=0, tiled=True),
        preferred_element_type=jnp.float32,
    )
    new_keys_values = lax.all_to_all(
        projected_part.astype(jnp.bfloat16), "req", split_axis=0, concat_axis=1, tiled=True
    )
    combined = jnp.concatenate([cache_part, new_keys_values], axis=0)
    group_keys = lax.all_to_all(
        head_groups(combined, experts, groups, group_width),
        "tok",
        split_axis=0,
        concat_axis=0,
        tiled=True,
    )
    attn_routes = attention_routes[0]
    attn_pairs = slot_matrix(attn_routes, experts, CAP)
    attn_gate = router_gates(hidden, attention_router, attn_routes)
    attn_pick, attn_weights = token_matrices(attn_pairs, attn_gate, top_count)
    slot_inputs = jnp.dot(
        attn_pick.T.astype(jnp.bfloat16), hidden, preferred_element_type=jnp.float32
    ).astype(jnp.bfloat16)
    token_place = tok_index * query_rows + jnp.arange(query_rows, dtype=jnp.int32)
    slot_place = jnp.sum(attn_pick.astype(jnp.int32) * token_place[:, None], axis=0)
    query_send = spread_slots(slot_inputs, experts, groups, CAP)
    place_send = jnp.broadcast_to(
        slot_place.reshape(experts, 1, CAP), (experts, groups, CAP)
    ).reshape(tok_count, CAP)
    length = cache_lengths[0]
    source = jnp.arange(tok_count, dtype=jnp.int32).reshape(groups, experts, 1)
    offset = jnp.arange(block_span, dtype=jnp.int32).reshape(1, 1, block_span)
    turn_shape = (groups, experts * block_span)
    cached = jnp.broadcast_to(offset < cache_rows, (groups, experts, block_span)).reshape(
        turn_shape
    )
    cache_usable = (source * cache_rows + offset < length).reshape(turn_shape)
    fresh_place = (source * query_rows + offset - cache_rows).reshape(turn_shape)
    key_turns = group_keys.reshape(groups, experts * block_span, 2, head_count, HEAD_DIM)
    slot_rows = lax.all_to_all(query_send, "tok", split_axis=0, concat_axis=0, tiled=True)
    slot_places = lax.all_to_all(place_send, "tok", split_axis=0, concat_axis=0, tiled=True)
    items = slot_rows.shape[1]
    query_three = (
        jnp.einsum("scd,df->scf", slot_rows, query_weight[0], preferred_element_type=jnp.float32)
        .astype(jnp.bfloat16)
        .reshape(tok_count * items, head_count, HEAD_DIM)
    )
    query_place = slot_places.reshape(tok_count * items)

    def one_turn(state_in, turn_data):
        row_max, row_sums, weighted = state_in
        keys_values, cached_turn, usable_turn, place_turn = turn_data
        usable = jnp.where(
            cached_turn[None, :], usable_turn[None, :], place_turn[None, :] <= query_place[:, None]
        )[None]
        scores = (
            jnp.einsum(
                "phd,khd->hpk", query_three, keys_values[:, 0], preferred_element_type=jnp.float32
            )
            * score_scale
        )
        scores = jnp.where(usable, scores, -1e30)
        new_max = jnp.maximum(row_max, jnp.max(scores, axis=-1))
        weights = jnp.where(usable, jnp.exp(scores - new_max[..., None]), 0.0).astype(jnp.bfloat16)
        factor = jnp.exp(row_max - new_max)
        row_sums = row_sums * factor + jnp.sum(weights.astype(jnp.float32), axis=-1)
        weighted = weighted * factor[..., None] + jnp.einsum(
            "hpk,khd->hpd", weights, keys_values[:, 1], preferred_element_type=jnp.float32
        )
        return ((new_max, row_sums, weighted), None)

    query_total = tok_count * items
    initial = (
        jnp.full((head_count, query_total), -1e30, jnp.float32),
        jnp.zeros((head_count, query_total), jnp.float32),
        jnp.zeros((head_count, query_total, HEAD_DIM), jnp.float32),
    )
    final_state, _ = lax.scan(one_turn, initial, (key_turns, cached, cache_usable, fresh_place))
    row_max, row_sums, weighted = final_state
    attended = (
        (weighted / row_sums[..., None])
        .astype(jnp.bfloat16)
        .transpose(1, 0, 2)
        .reshape(tok_count, items, group_width)
    )
    parts = jnp.einsum(
        "scf,fd->scd", attended, output_weight[0], preferred_element_type=jnp.float32
    ).astype(jnp.bfloat16)
    output_back = lax.all_to_all(parts, "tok", split_axis=0, concat_axis=0, tiled=True)
    output_sums = group_sum(output_back, experts, groups, CAP)
    mixed_rows = (
        residual_in + jnp.dot(attn_weights, output_sums, precision=lax.Precision.HIGHEST)
    ).astype(jnp.bfloat16)
    hidden_two = normed(mixed_rows.astype(jnp.float32), feedforward_gain).astype(jnp.bfloat16)
    ffn_routes = feedforward_routes[0]
    ffn_pairs = slot_matrix(ffn_routes, experts, CAP)
    ffn_gate = router_gates(hidden_two, feedforward_router, ffn_routes)
    ffn_pick, ffn_weights = token_matrices(ffn_pairs, ffn_gate, top_count)
    every_rows, every_routes = (
        lax.all_gather(hidden_two, "tok", axis=0, tiled=True),
        lax.all_gather(ffn_routes, "tok", axis=0, tiled=True),
    )
    routes_all = every_routes.reshape(tok_count, query_rows, top_count)

    def source_slots(routes_block):
        return slot_matrix(routes_block, experts, CAP)

    per_source = jax.vmap(source_slots)(routes_all)
    per_token = jnp.sum(per_source.reshape(tok_count, query_rows, top_count, experts, CAP), axis=2)
    expert_mask = (jnp.arange(experts, dtype=jnp.int32) == tok_index // groups).astype(jnp.float32)
    picked = jnp.einsum("sqec,e->sqc", per_token, expert_mask)
    received = jnp.einsum(
        "sqc,sqd->scd",
        picked.astype(jnp.bfloat16),
        every_rows.reshape(tok_count, query_rows, model_width),
        preferred_element_type=jnp.float32,
    ).astype(jnp.bfloat16)
    expert_parts = expert_feedforward(received, gate_up[0], down_weight[0])
    expert_back = lax.all_to_all(expert_parts, "tok", split_axis=0, concat_axis=0, tiled=True)
    expert_sums = group_sum(expert_back, experts, groups, CAP)
    layer_output = (
        mixed_rows.astype(jnp.float32)
        + jnp.dot(ffn_weights, expert_sums, precision=lax.Precision.HIGHEST)
    ).astype(jnp.bfloat16)
    return (layer_output[None], new_keys_values[None])


PAD = 8
LANES = 128


def permute(values, axis, pairs):
    return lax.ppermute(values, axis, pairs)


def swap_all(values, axis):
    return lax.all_to_all(values, axis, split_axis=0, concat_axis=0, tiled=True)


def whole_spec():
    return pl.BlockSpec(memory_space=pltpu.VMEM)


def index_spec():
    return pl.BlockSpec(memory_space=pltpu.SMEM)


def iota(shape, axis):
    return lax.broadcasted_iota(jnp.int32, shape, axis)


def padded_picks(routes, experts):
    row_count = routes.shape[0]
    shape = (row_count, experts * PAD)
    column = iota(shape, 1)
    expert, slot = column // PAD, column % PAD
    first, second = routes[:, 0:1] == expert, routes[:, 1:2] == expert
    named = jnp.where(first, 1.0, 0.0) + jnp.where(second, 1.0, 0.0)
    earlier = (iota((row_count, row_count), 1) < iota((row_count, row_count), 0)).astype(
        jnp.bfloat16
    )
    before = jnp.dot(
        earlier, named.astype(jnp.bfloat16), preferred_element_type=jnp.float32
    ).astype(jnp.int32)
    here = (before == slot) & (slot < CAP)
    return named * here.astype(jnp.float32), first


def gate_weights(hidden, router, routes, picks, first):
    experts = router.shape[1]
    logits = jnp.dot(hidden, router, preferred_element_type=jnp.float32)
    label = iota(logits.shape, 1)
    one = jnp.sum(jnp.where(routes[:, 0:1] == label, logits, 0.0), axis=1, keepdims=True)
    two = jnp.sum(jnp.where(routes[:, 1:2] == label, logits, 0.0), axis=1, keepdims=True)
    gate_one = 1.0 / (1.0 + jnp.exp(two - one))
    gate_two = 1.0 / (1.0 + jnp.exp(one - two))
    return picks * jnp.where(first, gate_one, gate_two)


def row_norm(values, gain):
    mean = jnp.mean(values * values, axis=-1, keepdims=True)
    return (values * lax.rsqrt(mean + 1e-06) * gain).astype(jnp.bfloat16)


def pick_rows(picks, rows):
    return lax.dot_general(
        picks.astype(jnp.bfloat16),
        rows,
        (((0,), (0,)), ((), ())),
        preferred_element_type=jnp.float32,
    )


def compact(rows):
    count = rows.shape[0] // PAD * CAP
    one, two = iota((count, rows.shape[0]), 0), iota((count, rows.shape[0]), 1)
    chosen = ((one // CAP) * PAD + one % CAP == two).astype(jnp.bfloat16)
    return jnp.dot(chosen, rows, preferred_element_type=jnp.float32)


def spread(rows):
    count = rows.shape[0] // CAP * PAD
    one, two = iota((count, rows.shape[0]), 0), iota((count, rows.shape[0]), 1)
    chosen = ((two // CAP) * PAD + two % CAP == one).astype(jnp.bfloat16)
    return jnp.dot(chosen, rows, preferred_element_type=jnp.float32)


def exact_mix(weights, rows):
    high = weights.astype(jnp.bfloat16)
    rest = weights - high.astype(jnp.float32)
    middle = rest.astype(jnp.bfloat16)
    low = (rest - middle.astype(jnp.float32)).astype(jnp.bfloat16)
    count = weights.shape[0]
    stacked = jnp.dot(
        jnp.concatenate([high, middle, low], axis=0), rows, preferred_element_type=jnp.float32
    )
    return stacked[:count] + (stacked[count : 2 * count] + stacked[2 * count :])


def prepare(activations, gain, router, routes, tok_count):
    rows, width = activations.shape
    experts = router.shape[1]
    span = width // tok_count
    half = rows // 2
    per_row = width // (2 * span)

    def body(act_ref, gain_ref, router_ref, route_ref, out_ref, weight_ref, wide, copy):
        route = route_ref[...]
        hidden = row_norm(act_ref[...].astype(jnp.float32), gain_ref[...])
        picks, first = padded_picks(route, experts)
        wide[...] = pick_rows(picks, hidden)
        copy[...] = hidden.astype(jnp.float32)
        for dest in range(tok_count):
            chip, core = dest // 2, dest % 2
            for place in range(half):
                row = dest * PAD + CAP + place // per_row
                for side in range(2):
                    column = (place % per_row) * 2 * span + side * span
                    source = (2 * chip + (core ^ side)) * span
                    wide[row : row + 1, column : column + span] = copy[
                        core * half + place : core * half + place + 1, source : source + span
                    ]
        out_ref[:, :, :width] = (
            wide[...].astype(jnp.bfloat16).reshape(tok_count, PAD, width)
        )
        number = iota((rows, LANES), 0).astype(jnp.float32).astype(jnp.bfloat16)
        out_ref[:, :, width:] = (
            pick_rows(picks, number).astype(jnp.bfloat16).reshape(tok_count, PAD, LANES)
        )
        weight_ref[...] = gate_weights(hidden, router_ref[...], route, picks, first)

    return pl.pallas_call(
        body,
        in_specs=[whole_spec()] * 4,
        out_specs=[whole_spec()] * 2,
        out_shape=[
            jax.ShapeDtypeStruct((tok_count, PAD, width + LANES), jnp.bfloat16),
            jax.ShapeDtypeStruct((rows, tok_count * PAD), jnp.float32),
        ],
        scratch_shapes=[
            pltpu.VMEM((tok_count * PAD, width), jnp.float32),
            pltpu.VMEM((rows, width), jnp.float32),
        ],
        compiler_params=pltpu.CompilerParams(vmem_limit_bytes=6 << 20),
        name="prepare",
    )(activations, gain.reshape(1, width), router, routes)


def own_tokens(arrived, tok_count, width):
    span = width // tok_count
    per_row = width // (2 * span)
    extra = PAD - CAP

    def body(in_ref, out_ref, wide):
        for source in range(tok_count):
            rows = in_ref[source, :, :width].astype(jnp.float32)
            for part in range(extra):
                for place in range(per_row):
                    row = source * extra * per_row + part * per_row + place
                    wide[row : row + 1, :] = rows[
                        CAP + part : CAP + part + 1, place * 2 * span : (place + 1) * 2 * span
                    ]
        out_ref[...] = wide[...].astype(jnp.bfloat16)

    count = tok_count * extra * per_row
    return pl.pallas_call(
        body,
        in_specs=[whole_spec()],
        out_specs=whole_spec(),
        out_shape=jax.ShapeDtypeStruct((count, 2 * span), jnp.bfloat16),
        scratch_shapes=[pltpu.VMEM((count, 2 * span), jnp.float32)],
        compiler_params=pltpu.CompilerParams(vmem_limit_bytes=4 << 20),
        name="own_tokens",
    )(arrived)


def query_project(arrived, weight, cache_part, tok_count):
    width = weight.shape[0]
    span = width // tok_count
    slots = tok_count * CAP
    cache_rows = cache_part.shape[0]
    height = slots + 2 * cache_rows + PAD
    tile = 2 * span

    def body(in_ref, weight_ref, key_ref, value_ref, out_ref, rows, places):
        step = pl.program_id(0)

        @pl.when(step == 0)
        def _():
            every = compact(in_ref[...].reshape(tok_count * PAD, width + LANES))
            rows[...] = every[:, :width].astype(jnp.bfloat16)
            local = every[:, width : width + LANES]
            mine = iota(local.shape, 0)
            placed = local + ((mine // CAP) * (2 * PAD)).astype(jnp.float32)
            placed = jnp.where(mine == iota(local.shape, 1), placed, 0.0)
            places[...] = jnp.broadcast_to(
                jnp.sum(placed, axis=0, keepdims=True), places.shape
            )

        query = jnp.dot(rows[...], weight_ref[...], preferred_element_type=jnp.float32).astype(
            jnp.bfloat16
        )
        line = places[...].astype(jnp.bfloat16)
        for one in range(tile // span):
            cols = slice(one * span, (one + 1) * span)
            out_ref[one, :slots, :] = query[:, cols]
            out_ref[one, slots : slots + cache_rows, :] = key_ref[:, cols]
            out_ref[one, slots + cache_rows : slots + 2 * cache_rows, :] = value_ref[:, cols]
            out_ref[one, slots + 2 * cache_rows :, :] = jnp.concatenate(
                [line] * (span // LANES), axis=1
            )

    steps = width // tile
    return pl.pallas_call(
        body,
        grid=(steps,),
        in_specs=[
            pl.BlockSpec(arrived.shape, lambda step: (0, 0, 0)),
            pl.BlockSpec((width, tile), lambda step: (0, step)),
            pl.BlockSpec((cache_rows, tile), lambda step: (0, step)),
            pl.BlockSpec((cache_rows, tile), lambda step: (0, step + steps)),
        ],
        out_specs=pl.BlockSpec((tile // span, height, span), lambda step: (step, 0, 0)),
        out_shape=jax.ShapeDtypeStruct((tok_count, height, span), jnp.bfloat16),
        scratch_shapes=[
            pltpu.VMEM((slots, width), jnp.bfloat16),
            pltpu.VMEM((PAD, LANES), jnp.float32),
        ],
        compiler_params=pltpu.CompilerParams(vmem_limit_bytes=8 << 20),
        name="query_project",
    )(arrived, weight, cache_part, cache_part)


def key_value_parts(tokens, weight, sibling, chip):
    rows, depth = tokens[0].shape
    half = depth // 2
    quarter = weight.shape[1] // 4
    count = len(tokens)

    def body(chip_ref, *refs):
        token_refs, weight_ref, sibling_ref = refs[:count], refs[count], refs[count + 1]
        outs = refs[count + 2 :]
        stacked = jnp.concatenate([one[...] for one in token_refs], axis=0)
        for turn in range(4):
            start = pl.multiple_of((chip_ref[0] ^ turn) * quarter, quarter)
            part = jnp.dot(
                stacked[:, :half],
                weight_ref[:, pl.ds(start, quarter)],
                preferred_element_type=jnp.float32,
            ) + jnp.dot(
                stacked[:, half:],
                sibling_ref[:, pl.ds(start, quarter)],
                preferred_element_type=jnp.float32,
            )
            outs[turn][...] = part.astype(outs[turn].dtype)

    shapes = [
        jax.ShapeDtypeStruct((count * rows, quarter), jnp.float32 if turn == 0 else jnp.bfloat16)
        for turn in range(4)
    ]
    return pl.pallas_call(
        body,
        in_specs=[index_spec()] + [whole_spec()] * (count + 2),
        out_specs=[whole_spec()] * 4,
        out_shape=shapes,
        compiler_params=pltpu.CompilerParams(vmem_limit_bytes=8 << 20),
        name="key_value_parts",
    )(chip.reshape(1), *tokens, weight, sibling)


def key_value_sum(parts, own_req, core):
    rows, quarter = parts[0].shape
    block = rows // 4

    def body(place_ref, *refs):
        ins, outs = refs[:4], refs[4:]
        source = (place_ref[0] // 2) * 2 + place_ref[1]
        for turn in range(4):
            start = pl.multiple_of((place_ref[0] ^ source ^ turn) * block, block)
            total = ins[0][pl.ds(start, block), :]
            for one in ins[1:]:
                total = total + one[pl.ds(start, block), :].astype(jnp.float32)
            outs[turn][...] = total.astype(jnp.bfloat16)

    return pl.pallas_call(
        body,
        in_specs=[index_spec()] + [whole_spec()] * 4,
        out_specs=[whole_spec()] * 4,
        out_shape=[jax.ShapeDtypeStruct((block, quarter), jnp.bfloat16)] * 4,
        compiler_params=pltpu.CompilerParams(vmem_limit_bytes=4 << 20),
        name="key_value_sum",
    )(jnp.stack([own_req, core]), *parts)


def attention(message, scalars, fresh_blocks, cache_rows):
    blocks, _, span = message.shape
    heads = span // HEAD_DIM
    slots = blocks * CAP
    fresh_rows = fresh_blocks[0].shape[0]
    half = fresh_rows // blocks
    height = slots + 2 * 2 * half * 2
    scale = 1.0 / math.sqrt(HEAD_DIM)
    contract = (((1,), (1,)), ((), ()))

    def body(scalar_ref, in_ref, *refs):
        fresh_refs, out_ref = refs[:4], refs[4]
        limit, req = scalar_ref[0], scalar_ref[1]
        pieces = []
        for source in range(4):
            picked = fresh_refs[3][...]
            for turn in range(3):
                picked = jnp.where((req ^ source) == turn, fresh_refs[turn][...], picked)
            pieces.append(picked)
        new_keys = jnp.concatenate(pieces[:2], axis=0)
        new_values = jnp.concatenate(pieces[2:], axis=0)
        cache_usable = iota((1, blocks * cache_rows), 1) < limit
        new_row = iota((1, 2 * fresh_rows), 1)
        within = new_row % fresh_rows
        new_place = (within // half) * (2 * half) + (new_row // fresh_rows) * half + within % half
        places = []
        for expert in range(blocks):
            line = in_ref[expert, slots + 2 * cache_rows :, :LANES].astype(jnp.float32)[0:1]
            chosen = iota((slots, LANES), 0) == iota((slots, LANES), 1)
            places.append(jnp.sum(jnp.where(chosen, line, 0.0), axis=1, keepdims=True))
        new_usable = new_place <= jnp.concatenate(places, axis=0).astype(jnp.int32)
        flat = in_ref[:, :slots, :].reshape(blocks * slots, span)
        keys = in_ref[:, slots : slots + cache_rows, :].reshape(blocks * cache_rows, span)
        values = in_ref[:, slots + cache_rows : slots + 2 * cache_rows, :].reshape(
            blocks * cache_rows, span
        )
        for head in range(heads):
            cols = slice(head * HEAD_DIM, (head + 1) * HEAD_DIM)
            query = flat[:, cols]
            first = lax.dot_general(
                query, keys[:, cols], contract, preferred_element_type=jnp.float32
            )
            second = lax.dot_general(
                query, new_keys[:, cols], contract, preferred_element_type=jnp.float32
            )
            first = jnp.where(cache_usable, first * scale, -1e30)
            second = jnp.where(new_usable, second * scale, -1e30)
            top = jnp.maximum(
                jnp.max(first, axis=-1, keepdims=True), jnp.max(second, axis=-1, keepdims=True)
            )
            first = jnp.exp(first - top).astype(jnp.bfloat16)
            second = jnp.exp(second - top).astype(jnp.bfloat16)
            sums = jnp.sum(first.astype(jnp.float32), axis=-1, keepdims=True) + jnp.sum(
                second.astype(jnp.float32), axis=-1, keepdims=True
            )
            mixed = jnp.dot(first, values[:, cols], preferred_element_type=jnp.float32) + jnp.dot(
                second, new_values[:, cols], preferred_element_type=jnp.float32
            )
            out_ref[:, :slots, cols] = (
                (mixed / sums).astype(jnp.bfloat16).reshape(blocks, slots, HEAD_DIM)
            )
        for kind in range(2):
            for part in range(2):
                start = slots + kind * 2 * half + part * half
                out_ref[:, start : start + half, :] = pieces[2 * kind + part].reshape(
                    blocks, half, span
                )

    return pl.pallas_call(
        body,
        in_specs=[index_spec()] + [whole_spec()] * 5,
        out_specs=whole_spec(),
        out_shape=jax.ShapeDtypeStruct((blocks, slots + 4 * half, span), jnp.bfloat16),
        compiler_params=pltpu.CompilerParams(vmem_limit_bytes=14 << 20),
        name="attention",
    )(scalars, message, *fresh_blocks)


def output_project(arrived, weight, query_rows):
    blocks, height, span = arrived.shape
    slots = blocks * CAP
    width = weight.shape[1]
    tile = width // 4

    def body(in_ref, weight_ref, out_ref, fresh_ref, rows):
        @pl.when(pl.program_id(0) == 0)
        def _():
            for block in range(blocks):
                cols = slice(block * span, (block + 1) * span)
                rows[:, cols] = spread(in_ref[block, :slots, :]).astype(jnp.bfloat16)
                fresh_ref[:, cols] = in_ref[block, slots : slots + query_rows, :]
                fresh_ref[:, block * span + width : (block + 1) * span + width] = in_ref[
                    block, slots + query_rows :, :
                ]

        part = jnp.dot(rows[...], weight_ref[...], preferred_element_type=jnp.float32)
        out_ref[...] = part.astype(jnp.bfloat16).reshape(blocks, PAD, tile)

    return pl.pallas_call(
        body,
        grid=(width // tile,),
        in_specs=[
            pl.BlockSpec(arrived.shape, lambda step: (0, 0, 0)),
            pl.BlockSpec((blocks * span, tile), lambda step: (0, step)),
        ],
        out_specs=[
            pl.BlockSpec((blocks, PAD, tile), lambda step: (0, 0, step)),
            pl.BlockSpec((query_rows, 2 * width), lambda step: (0, 0)),
        ],
        out_shape=[
            jax.ShapeDtypeStruct((blocks, PAD, width), jnp.bfloat16),
            jax.ShapeDtypeStruct((query_rows, 2 * width), jnp.bfloat16),
        ],
        scratch_shapes=[pltpu.VMEM((blocks * PAD, blocks * span), jnp.bfloat16)],
        compiler_params=pltpu.CompilerParams(vmem_limit_bytes=8 << 20),
        name="output_project",
    )(arrived, weight)


def middle(activations, arrived, weights, gain, router, routes):
    rows, width = activations.shape
    blocks = arrived.shape[0]
    experts = router.shape[1]

    def body(act_ref, in_ref, old_ref, gain_ref, router_ref, route_ref, out_ref, mix_ref, new_ref):
        route = route_ref[...]
        added = exact_mix(old_ref[...], in_ref[...].reshape(blocks * PAD, width))
        mixed = (act_ref[...].astype(jnp.float32) + added).astype(jnp.bfloat16)
        mix_ref[...] = mixed
        hidden = row_norm(mixed.astype(jnp.float32), gain_ref[...])
        picks, first = padded_picks(route, experts)
        out_ref[...] = (
            pick_rows(picks, hidden).astype(jnp.bfloat16).reshape(blocks, PAD, width)
        )
        new_ref[...] = gate_weights(hidden, router_ref[...], route, picks, first)

    return pl.pallas_call(
        body,
        in_specs=[whole_spec()] * 6,
        out_specs=[whole_spec()] * 3,
        out_shape=[
            jax.ShapeDtypeStruct((blocks, PAD, width), jnp.bfloat16),
            jax.ShapeDtypeStruct((rows, width), jnp.bfloat16),
            jax.ShapeDtypeStruct((rows, blocks * PAD), jnp.float32),
        ],
        compiler_params=pltpu.CompilerParams(vmem_limit_bytes=6 << 20),
        name="middle",
    )(activations, arrived, weights, gain.reshape(1, width), router, routes)


def finish(mixed, arrived, weights):
    rows, width = mixed.shape

    def body(mix_ref, in_ref, weight_ref, out_ref):
        added = exact_mix(weight_ref[...], in_ref[...].reshape(-1, width))
        out_ref[...] = (mix_ref[...].astype(jnp.float32) + added).astype(jnp.bfloat16)

    return pl.pallas_call(
        body,
        in_specs=[whole_spec()] * 3,
        out_specs=whole_spec(),
        out_shape=jax.ShapeDtypeStruct((rows, width), jnp.bfloat16),
        compiler_params=pltpu.CompilerParams(vmem_limit_bytes=4 << 20),
        name="finish",
    )(mixed, arrived, weights)


def feedforward(arrived, gate_piece, down_piece):
    blocks, _, width = arrived.shape
    count = blocks * CAP
    units = down_piece.shape[0]
    tile = 512
    steps = units // tile

    def body(in_ref, gate_ref, up_ref, down_ref, out_ref, rows, total):
        step = pl.program_id(0)

        @pl.when(step == 0)
        def _():
            total[...] = jnp.zeros_like(total)
            rows[...] = compact(in_ref[...].reshape(blocks * PAD, width)).astype(jnp.bfloat16)

        row = rows[...]
        gate = jnp.dot(row, gate_ref[...], preferred_element_type=jnp.float32)
        up = jnp.dot(row, up_ref[...], preferred_element_type=jnp.float32)
        active = (gate / (1.0 + jnp.exp(-gate)) * up).astype(jnp.bfloat16)
        total[...] += jnp.dot(active, down_ref[...], preferred_element_type=jnp.float32)

        @pl.when(step == steps - 1)
        def _():
            out_ref[...] = (
                spread(total[...].astype(jnp.bfloat16))
                .astype(jnp.bfloat16)
                .reshape(blocks, PAD, width)
            )

    return pl.pallas_call(
        body,
        grid=(steps,),
        in_specs=[
            pl.BlockSpec(arrived.shape, lambda step: (0, 0, 0)),
            pl.BlockSpec((width, tile), lambda step: (0, step)),
            pl.BlockSpec((width, tile), lambda step: (0, step + steps)),
            pl.BlockSpec((tile, width), lambda step: (step, 0)),
        ],
        out_specs=pl.BlockSpec(arrived.shape, lambda step: (0, 0, 0)),
        out_shape=jax.ShapeDtypeStruct(arrived.shape, jnp.bfloat16),
        scratch_shapes=[
            pltpu.VMEM((count, width), jnp.bfloat16),
            pltpu.VMEM((count, width), jnp.float32),
        ],
        compiler_params=pltpu.CompilerParams(vmem_limit_bytes=20 << 20),
        cost_estimate=pl.CostEstimate(
            flops=6 * count * width * units,
            transcendentals=count * units,
            bytes_accessed=6 * width * units,
        ),
        name="feedforward",
    )(arrived, gate_piece, gate_piece, down_piece)


def local_heads(
    activations,
    cache_entries,
    cache_lengths,
    attention_gain,
    feedforward_gain,
    key_value_weight,
    attention_router,
    attention_routes,
    query_weight,
    output_weight,
    feedforward_router,
    feedforward_routes,
    gate_up,
    down_weight,
):
    tok_count = lax.axis_size("tok")
    req_count = lax.axis_size("req")
    tok_index = lax.axis_index("tok")
    req_index = lax.axis_index("req")
    chip, core = tok_index // 2, tok_index % 2
    query_rows, width = activations.shape[1:]
    cache_rows = cache_entries.shape[1]

    message, attn_weights = prepare(
        activations[0], attention_gain, attention_router, attention_routes[0], tok_count
    )
    arrived = swap_all(message, "tok")
    sibling = permute(key_value_weight, "tok", [(one, one ^ 1) for one in range(tok_count)])
    mine = own_tokens(arrived, tok_count, width)
    tokens = [mine] + [
        permute(mine, "req", [(one, one ^ turn) for one in range(req_count)])
        for turn in range(1, req_count)
    ]
    queries = query_project(arrived, query_weight[0], cache_entries[0], tok_count)
    queries = swap_all(queries, "tok")
    parts = key_value_parts(tokens, key_value_weight, sibling, chip)
    parts = [parts[0]] + [
        permute(parts[turn], "tok", [(one, one ^ (2 * turn)) for one in range(tok_count)])
        for turn in range(1, 4)
    ]
    sums = key_value_sum(parts, req_index, core)
    fresh_blocks = []
    for turn in range(4):
        pairs = []
        for one in range(req_count * tok_count):
            r, t = one // tok_count, one % tok_count
            dest = ((r // 2) * 2 + t % 2) ^ turn
            pairs.append((one, dest * tok_count + 4 * (r % 2) + t // 2))
        fresh_blocks.append(permute(sums[turn], ("req", "tok"), pairs))
    scalars = jnp.stack([cache_lengths[0], req_index])
    attended = attention(queries, scalars, fresh_blocks, cache_rows)
    attended = swap_all(attended, "tok")
    parts_out, new_keys_values = output_project(attended, output_weight[0], query_rows)
    output_back = swap_all(parts_out, "tok")
    ffn_send, mixed_rows, ffn_weights = middle(
        activations[0],
        output_back,
        attn_weights,
        feedforward_gain,
        feedforward_router,
        feedforward_routes[0],
    )
    received = swap_all(ffn_send, "tok")
    expert_parts = feedforward(received, gate_up[0], down_weight[0])
    expert_back = swap_all(expert_parts, "tok")
    layer_output = finish(mixed_rows, expert_back, ffn_weights)
    return (layer_output[None], new_keys_values[None])


def solution(mesh):
    placed = (
        P("req", "tok", None),
        P("req", "tok", None),
        P("req"),
        P(),
        P(),
        P("tok", "req"),
        P(),
        P("req", "tok", None),
        P("tok", None, None),
        P("tok", None, None),
        P(),
        P("req", "tok", None),
        P("tok", None, None),
        P("tok", None, None),
    )
    sizes = dict(mesh.shape)
    by_heads = sizes["tok"] == 8 and sizes["req"] == 4
    return jax.shard_map(
        local_heads if by_heads else local,
        mesh=mesh,
        in_specs=placed,
        out_specs=(P("req", "tok", None), P("req", "tok", None)),
        check_vma=False,
    )
```

```python
import math

import jax
import jax.numpy as jnp
from jax import lax
from jax.experimental import pallas as pl
from jax.experimental.pallas import tpu as pltpu
from jax.sharding import PartitionSpec as P

HEADS = 16
HEAD_DIM = 128
CAP = 6


def normed(values, gain):
    scale_rows = lax.rsqrt(jnp.mean(values * values, axis=-1, keepdims=True) + 1e-06)
    return values * scale_rows * gain


def slot_matrix(routes, experts, capacity):
    row_count, top_count = routes.shape
    labels = jnp.arange(experts, dtype=jnp.int32)
    onehot = (routes.reshape(row_count * top_count, 1) == labels[None, :]).astype(jnp.int32)
    before = jnp.cumsum(onehot, axis=0) - onehot
    within = jnp.sum(before * onehot, axis=1)
    placed = routes.reshape(row_count * top_count) * capacity + within
    columns = jnp.arange(experts * capacity, dtype=jnp.int32)
    return (placed[:, None] == columns[None, :]).astype(jnp.float32)


def router_gates(hidden, router, routes):
    logits = jnp.dot(hidden, router, preferred_element_type=jnp.float32)
    picked = jnp.take_along_axis(logits, routes, axis=1)
    return jax.nn.sigmoid(2.0 * picked - jnp.sum(picked, axis=1, keepdims=True))


def token_matrices(pair_slots, gates, top_count):
    row_count = gates.shape[0]
    per_token = pair_slots.reshape(row_count, top_count, -1)
    picked = jnp.sum(per_token, axis=1)
    weighted = jnp.sum(per_token * gates[:, :, None], axis=1)
    return (picked, weighted)


def spread_slots(slot_rows, experts, groups, capacity):
    feat_width = slot_rows.shape[-1]
    shaped = slot_rows.reshape(experts, 1, capacity, feat_width)
    return jnp.broadcast_to(shaped, (experts, groups, capacity, feat_width)).reshape(
        experts * groups, capacity, feat_width
    )


def head_groups(rows, experts, groups, group_width):
    row_count = rows.shape[0]
    shaped = (
        rows.reshape(row_count, 2, groups, group_width)
        .transpose(2, 0, 1, 3)
        .reshape(groups, row_count, 2 * group_width)
    )
    return jnp.broadcast_to(shaped[None], (experts, groups, row_count, 2 * group_width)).reshape(
        experts * groups, row_count, 2 * group_width
    )


def group_sum(received, experts, groups, capacity):
    feat_width = received.shape[-1]
    summed = jnp.sum(
        received.reshape(experts, groups, capacity, feat_width).astype(jnp.float32), axis=1
    )
    return summed.reshape(experts * capacity, feat_width)


def expert_feedforward(received, gate_piece, down_piece):
    units = down_piece.shape[0]
    projected = jnp.einsum("scd,df->scf", received, gate_piece, preferred_element_type=jnp.float32)
    active = (jax.nn.silu(projected[..., :units]) * projected[..., units:]).astype(jnp.bfloat16)
    return jnp.einsum("scf,fd->scd", active, down_piece, preferred_element_type=jnp.float32).astype(
        jnp.bfloat16
    )


def local(
    activations,
    cache_entries,
    cache_lengths,
    attention_gain,
    feedforward_gain,
    key_value_weight,
    attention_router,
    attention_routes,
    query_weight,
    output_weight,
    feedforward_router,
    feedforward_routes,
    gate_up,
    down_weight,
):
    tok_count = lax.axis_size("tok")
    tok_index = lax.axis_index("tok")
    experts = attention_router.shape[1]
    groups = tok_count // experts
    query_rows = activations.shape[1]
    cache_rows = cache_entries.shape[1]
    top_count = attention_routes.shape[2]
    model_width = activations.shape[2]
    head_count = HEADS // groups
    group_width = head_count * HEAD_DIM
    block_span = cache_rows + query_rows
    score_scale = 1.0 / math.sqrt(HEAD_DIM)
    cache_part = cache_entries[0]
    residual_in = activations[0].astype(jnp.float32)
    hidden = normed(residual_in, attention_gain).astype(jnp.bfloat16)
    stacked = lax.all_gather(hidden, "req", axis=0, tiled=True)
    projected_part = jnp.dot(
        stacked,
        lax.all_gather(key_value_weight, "tok", axis=0, tiled=True),
        preferred_element_type=jnp.float32,
    )
    new_keys_values = lax.all_to_all(
        projected_part.astype(jnp.bfloat16), "req", split_axis=0, concat_axis=1, tiled=True
    )
    combined = jnp.concatenate([cache_part, new_keys_values], axis=0)
    group_keys = lax.all_to_all(
        head_groups(combined, experts, groups, group_width),
        "tok",
        split_axis=0,
        concat_axis=0,
        tiled=True,
    )
    attn_routes = attention_routes[0]
    attn_pairs = slot_matrix(attn_routes, experts, CAP)
    attn_gate = router_gates(hidden, attention_router, attn_routes)
    attn_pick, attn_weights = token_matrices(attn_pairs, attn_gate, top_count)
    slot_inputs = jnp.dot(
        attn_pick.T.astype(jnp.bfloat16), hidden, preferred_element_type=jnp.float32
    ).astype(jnp.bfloat16)
    token_place = tok_index * query_rows + jnp.arange(query_rows, dtype=jnp.int32)
    slot_place = jnp.sum(attn_pick.astype(jnp.int32) * token_place[:, None], axis=0)
    query_send = spread_slots(slot_inputs, experts, groups, CAP)
    place_send = jnp.broadcast_to(
        slot_place.reshape(experts, 1, CAP), (experts, groups, CAP)
    ).reshape(tok_count, CAP)
    length = cache_lengths[0]
    source = jnp.arange(tok_count, dtype=jnp.int32).reshape(groups, experts, 1)
    offset = jnp.arange(block_span, dtype=jnp.int32).reshape(1, 1, block_span)
    turn_shape = (groups, experts * block_span)
    cached = jnp.broadcast_to(offset < cache_rows, (groups, experts, block_span)).reshape(
        turn_shape
    )
    cache_usable = (source * cache_rows + offset < length).reshape(turn_shape)
    fresh_place = (source * query_rows + offset - cache_rows).reshape(turn_shape)
    key_turns = group_keys.reshape(groups, experts * block_span, 2, head_count, HEAD_DIM)
    slot_rows = lax.all_to_all(query_send, "tok", split_axis=0, concat_axis=0, tiled=True)
    slot_places = lax.all_to_all(place_send, "tok", split_axis=0, concat_axis=0, tiled=True)
    items = slot_rows.shape[1]
    query_three = (
        jnp.einsum("scd,df->scf", slot_rows, query_weight[0], preferred_element_type=jnp.float32)
        .astype(jnp.bfloat16)
        .reshape(tok_count * items, head_count, HEAD_DIM)
    )
    query_place = slot_places.reshape(tok_count * items)

    def one_turn(state_in, turn_data):
        row_max, row_sums, weighted = state_in
        keys_values, cached_turn, usable_turn, place_turn = turn_data
        usable = jnp.where(
            cached_turn[None, :], usable_turn[None, :], place_turn[None, :] <= query_place[:, None]
        )[None]
        scores = (
            jnp.einsum(
                "phd,khd->hpk", query_three, keys_values[:, 0], preferred_element_type=jnp.float32
            )
            * score_scale
        )
        scores = jnp.where(usable, scores, -1e30)
        new_max = jnp.maximum(row_max, jnp.max(scores, axis=-1))
        weights = jnp.where(usable, jnp.exp(scores - new_max[..., None]), 0.0).astype(jnp.bfloat16)
        factor = jnp.exp(row_max - new_max)
        row_sums = row_sums * factor + jnp.sum(weights.astype(jnp.float32), axis=-1)
        weighted = weighted * factor[..., None] + jnp.einsum(
            "hpk,khd->hpd", weights, keys_values[:, 1], preferred_element_type=jnp.float32
        )
        return ((new_max, row_sums, weighted), None)

    query_total = tok_count * items
    initial = (
        jnp.full((head_count, query_total), -1e30, jnp.float32),
        jnp.zeros((head_count, query_total), jnp.float32),
        jnp.zeros((head_count, query_total, HEAD_DIM), jnp.float32),
    )
    final_state, _ = lax.scan(one_turn, initial, (key_turns, cached, cache_usable, fresh_place))
    row_max, row_sums, weighted = final_state
    attended = (
        (weighted / row_sums[..., None])
        .astype(jnp.bfloat16)
        .transpose(1, 0, 2)
        .reshape(tok_count, items, group_width)
    )
    parts = jnp.einsum(
        "scf,fd->scd", attended, output_weight[0], preferred_element_type=jnp.float32
    ).astype(jnp.bfloat16)
    output_back = lax.all_to_all(parts, "tok", split_axis=0, concat_axis=0, tiled=True)
    output_sums = group_sum(output_back, experts, groups, CAP)
    mixed_rows = (
        residual_in + jnp.dot(attn_weights, output_sums, precision=lax.Precision.HIGHEST)
    ).astype(jnp.bfloat16)
    hidden_two = normed(mixed_rows.astype(jnp.float32), feedforward_gain).astype(jnp.bfloat16)
    ffn_routes = feedforward_routes[0]
    ffn_pairs = slot_matrix(ffn_routes, experts, CAP)
    ffn_gate = router_gates(hidden_two, feedforward_router, ffn_routes)
    ffn_pick, ffn_weights = token_matrices(ffn_pairs, ffn_gate, top_count)
    every_rows, every_routes = (
        lax.all_gather(hidden_two, "tok", axis=0, tiled=True),
        lax.all_gather(ffn_routes, "tok", axis=0, tiled=True),
    )
    routes_all = every_routes.reshape(tok_count, query_rows, top_count)

    def source_slots(routes_block):
        return slot_matrix(routes_block, experts, CAP)

    per_source = jax.vmap(source_slots)(routes_all)
    per_token = jnp.sum(per_source.reshape(tok_count, query_rows, top_count, experts, CAP), axis=2)
    expert_mask = (jnp.arange(experts, dtype=jnp.int32) == tok_index // groups).astype(jnp.float32)
    picked = jnp.einsum("sqec,e->sqc", per_token, expert_mask)
    received = jnp.einsum(
        "sqc,sqd->scd",
        picked.astype(jnp.bfloat16),
        every_rows.reshape(tok_count, query_rows, model_width),
        preferred_element_type=jnp.float32,
    ).astype(jnp.bfloat16)
    expert_parts = expert_feedforward(received, gate_up[0], down_weight[0])
    expert_back = lax.all_to_all(expert_parts, "tok", split_axis=0, concat_axis=0, tiled=True)
    expert_sums = group_sum(expert_back, experts, groups, CAP)
    layer_output = (
        mixed_rows.astype(jnp.float32)
        + jnp.dot(ffn_weights, expert_sums, precision=lax.Precision.HIGHEST)
    ).astype(jnp.bfloat16)
    return (layer_output[None], new_keys_values[None])


PAD = 8
LANES = 128
FF_TILE = 512


def column_stream(source, buffers, sems, tile):
    return [
        pltpu.make_async_copy(
            source.at[:, pl.ds(step * tile, tile)], buffers.at[step], sems.at[step]
        )
        for step in range(buffers.shape[0])
    ]


def permute(values, axis, pairs):
    return lax.ppermute(values, axis, pairs)


def swap_all(values, axis):
    return lax.all_to_all(values, axis, split_axis=0, concat_axis=0, tiled=True)


def whole_spec():
    return pl.BlockSpec(memory_space=pltpu.VMEM)


def index_spec():
    return pl.BlockSpec(memory_space=pltpu.SMEM)


def iota(shape, axis):
    return lax.broadcasted_iota(jnp.int32, shape, axis)


def any_spec():
    return pl.BlockSpec(memory_space=pl.ANY)


def in_hbm(*arrays):
    return [pltpu.with_memory_space_constraint(one, pltpu.HBM) for one in arrays]


def in_vmem(*arrays):
    return [pltpu.with_memory_space_constraint(one, pltpu.VMEM) for one in arrays]


def load_all(pairs, sems):
    copies = [
        pltpu.make_async_copy(source, target, sems.at[number])
        for number, (source, target) in enumerate(pairs)
    ]
    for one in copies:
        one.start()
    for one in copies:
        one.wait()


def padded_picks(routes, experts):
    row_count = routes.shape[1]
    row = iota((experts * PAD, row_count), 0)
    expert, slot = row // PAD, row % PAD
    first, second = routes[0:1, :] == expert, routes[1:2, :] == expert
    named = jnp.where(first, 1.0, 0.0) + jnp.where(second, 1.0, 0.0)
    earlier = (iota((row_count, row_count), 0) < iota((row_count, row_count), 1)).astype(
        jnp.bfloat16
    )
    before = jnp.dot(
        named.astype(jnp.bfloat16), earlier, preferred_element_type=jnp.float32
    ).astype(jnp.int32)
    here = (before == slot) & (slot < CAP)
    return named * here.astype(jnp.float32), first


def gate_weights(hidden, router, routes, picks, first):
    logits = lax.dot_general(
        router, hidden, (((1,), (1,)), ((), ())), preferred_element_type=jnp.float32
    )
    label = iota(logits.shape, 0)
    one = jnp.sum(jnp.where(routes[0:1, :] == label, logits, 0.0), axis=0, keepdims=True)
    two = jnp.sum(jnp.where(routes[1:2, :] == label, logits, 0.0), axis=0, keepdims=True)
    gate_one = 1.0 / (1.0 + jnp.exp(two - one))
    gate_two = 1.0 / (1.0 + jnp.exp(one - two))
    return picks * jnp.where(first, gate_one, gate_two)


def row_norm(values, gain):
    mean = jnp.mean(values * values, axis=-1, keepdims=True)
    return (values * lax.rsqrt(mean + 1e-06) * gain).astype(jnp.bfloat16)


def pick_rows(picks, rows):
    return jnp.dot(picks.astype(jnp.bfloat16), rows, preferred_element_type=jnp.float32)


def compact(rows):
    count = rows.shape[0] // PAD * CAP
    one, two = iota((count, rows.shape[0]), 0), iota((count, rows.shape[0]), 1)
    chosen = ((one // CAP) * PAD + one % CAP == two).astype(jnp.bfloat16)
    return jnp.dot(chosen, rows, preferred_element_type=jnp.float32)


def spread(rows):
    count = rows.shape[0] // CAP * PAD
    one, two = iota((count, rows.shape[0]), 0), iota((count, rows.shape[0]), 1)
    chosen = ((two // CAP) * PAD + two % CAP == one).astype(jnp.bfloat16)
    return jnp.dot(chosen, rows, preferred_element_type=jnp.float32)


def exact_mix(weights, rows):
    high = weights.astype(jnp.bfloat16)
    rest = weights - high.astype(jnp.float32)
    middle = rest.astype(jnp.bfloat16)
    low = (rest - middle.astype(jnp.float32)).astype(jnp.bfloat16)
    count = weights.shape[1]
    stacked = lax.dot_general(
        jnp.concatenate([high, middle, low], axis=1),
        rows,
        (((0,), (0,)), ((), ())),
        preferred_element_type=jnp.float32,
    )
    return stacked[:count] + (stacked[count : 2 * count] + stacked[2 * count :])


def prepare(activations, gain, router, routes, place, tok_count):
    rows, width = activations.shape
    experts = router.shape[0]
    span = width // tok_count
    half = rows // 2
    per_row = width // (2 * span)

    def body(
        place_ref, act_in, gain_in, router_in, route_in, out_ref, weight_ref,
        act_ref, gain_ref, router_ref, route_ref, wide, copy, sems,
    ):
        load_all(
            [
                (act_in, act_ref),
                (gain_in, gain_ref),
                (router_in, router_ref),
                (route_in, route_ref),
            ],
            sems,
        )
        route = route_ref[...]
        hidden = row_norm(act_ref[...].astype(jnp.float32), gain_ref[...])
        picks, first = padded_picks(route, experts)
        wide[...] = pick_rows(picks, hidden)
        copy[...] = hidden.astype(jnp.float32)
        for dest in range(tok_count):
            chip, core = dest // 2, dest % 2
            for place in range(half):
                row = dest * PAD + CAP + place // per_row
                for side in range(2):
                    column = (place % per_row) * 2 * span + side * span
                    source = (2 * chip + (core ^ side)) * span
                    wide[row : row + 1, column : column + span] = copy[
                        core * half + place : core * half + place + 1, source : source + span
                    ]
        out_ref[:, :, :width] = wide[...].astype(jnp.bfloat16).reshape(tok_count, PAD, width)
        number = iota((rows, LANES), 0).astype(jnp.float32).astype(jnp.bfloat16)
        out_ref[:, :, width:] = (
            pick_rows(picks, number).astype(jnp.bfloat16).reshape(tok_count, PAD, LANES)
        )
        weight_ref[...] = gate_weights(hidden, router_ref[...], route, picks, first)

    return pl.pallas_call(
        body,
        in_specs=[index_spec()] + [any_spec()] * 4,
        out_specs=[whole_spec()] * 2,
        out_shape=[
            jax.ShapeDtypeStruct((tok_count, PAD, width + LANES), jnp.bfloat16),
            jax.ShapeDtypeStruct((tok_count * PAD, rows), jnp.float32),
        ],
        scratch_shapes=[
            pltpu.VMEM((rows, width), activations.dtype),
            pltpu.VMEM((1, width), gain.dtype),
            pltpu.VMEM(router.shape, router.dtype),
            pltpu.VMEM(routes.shape, routes.dtype),
            pltpu.VMEM((tok_count * PAD, width), jnp.float32),
            pltpu.VMEM((rows, width), jnp.float32),
            pltpu.SemaphoreType.DMA((4,)),
        ],
        compiler_params=pltpu.CompilerParams(vmem_limit_bytes=4 << 20),
        name="prepare",
    )(place, *in_hbm(activations, gain.reshape(1, width), router, routes))


def cache_split(cache_part, place, after):
    rows, width = cache_part.shape
    count = 8
    span = width // 2 // count

    def body(index_ref, cache_ref, after_ref, *outs):
        def piece(other):
            start = pl.multiple_of((index_ref[2] ^ other) * span, span)
            return cache_ref[:, pl.ds(start, span)], cache_ref[:, pl.ds(start + width // 2, span)]

        for turn in range(4):
            for side in range(2):
                keys, values = piece(2 * turn + side)
                if turn:
                    out, base = outs[turn + 1], side * rows
                else:
                    out, base = outs[side], 0
                out[base : base + rows, :span] = keys
                out[base : base + rows, span:] = values

    shapes = [(rows, 2 * span)] * 2 + [(2 * rows, 2 * span)] * 3
    return pl.pallas_call(
        body,
        in_specs=[index_spec(), whole_spec(), any_spec()],
        out_specs=[whole_spec()] * 5,
        out_shape=[jax.ShapeDtypeStruct(one, cache_part.dtype) for one in shapes],
        compiler_params=pltpu.CompilerParams(vmem_limit_bytes=4 << 20),
        name="cache_split",
    )(place, cache_part, after)


def cache_relay(near, turned):
    rows, width = near.shape

    def body(near_ref, *refs):
        out_ref = refs[-1]
        out_ref[:rows, :] = near_ref[...]
        for turn in range(1, 4):
            out_ref[turn * rows : (turn + 1) * rows, :] = refs[turn - 1][rows:, :]

    return pl.pallas_call(
        body,
        in_specs=[whole_spec()] * 4,
        out_specs=whole_spec(),
        out_shape=jax.ShapeDtypeStruct((4 * rows, width), near.dtype),
        compiler_params=pltpu.CompilerParams(vmem_limit_bytes=3 << 20),
        name="cache_relay",
    )(near, *turned)


def own_tokens(arrived, after, tok_count, width):
    span = width // tok_count
    per_row = width // (2 * span)
    extra = PAD - CAP

    def body(in_ref, *rest):
        out_ref, wide = rest[len(after) :]
        for source in range(tok_count):
            rows = in_ref[source, :, :width].astype(jnp.float32)
            for part in range(extra):
                for place in range(per_row):
                    row = source * extra * per_row + part * per_row + place
                    wide[row : row + 1, :] = rows[
                        CAP + part : CAP + part + 1, place * 2 * span : (place + 1) * 2 * span
                    ]
        out_ref[...] = wide[...].astype(jnp.bfloat16)

    count = tok_count * extra * per_row
    return pl.pallas_call(
        body,
        in_specs=[whole_spec()] + [any_spec()] * len(after),
        out_specs=whole_spec(),
        out_shape=jax.ShapeDtypeStruct((count, 2 * span), jnp.bfloat16),
        scratch_shapes=[pltpu.VMEM((count, 2 * span), jnp.float32)],
        compiler_params=pltpu.CompilerParams(vmem_limit_bytes=4 << 20),
        name="own_tokens",
    )(arrived, *after)


def query_project(arrived, weight, after, tok_count):
    width = weight.shape[0]
    span = width // tok_count
    slots = tok_count * CAP
    height = slots + PAD
    tile = 2 * span
    steps = width // tile

    def body(in_ref, weight_ref, *rest):
        out_ref, held, sems = rest[len(after) :]
        copies = column_stream(weight_ref, held, sems, tile)
        for one in copies:
            one.start()
        every = compact(in_ref[...].reshape(tok_count * PAD, width + LANES))
        rows = every[:, :width].astype(jnp.bfloat16)
        local = every[:, width : width + LANES]
        mine = iota(local.shape, 0)
        placed = local + ((mine // CAP) * (2 * PAD)).astype(jnp.float32)
        placed = jnp.where(mine == iota(local.shape, 1), placed, 0.0)
        line = jnp.broadcast_to(jnp.sum(placed, axis=0, keepdims=True), (PAD, LANES))
        line = jnp.concatenate([line] * (span // LANES), axis=1).astype(jnp.bfloat16)
        for step in range(steps):
            copies[step].wait()
            query = jnp.dot(rows, held[step], preferred_element_type=jnp.float32).astype(
                jnp.bfloat16
            )
            for one in range(tile // span):
                place = step * (tile // span) + one
                out_ref[place, :slots, :] = query[:, one * span : (one + 1) * span]
                out_ref[place, slots:, :] = line

    return pl.pallas_call(
        body,
        in_specs=[whole_spec(), any_spec()] + [any_spec()] * len(after),
        out_specs=whole_spec(),
        out_shape=jax.ShapeDtypeStruct((tok_count, height, span), jnp.bfloat16),
        scratch_shapes=[
            pltpu.VMEM((steps, width, tile), jnp.bfloat16),
            pltpu.SemaphoreType.DMA((steps,)),
        ],
        compiler_params=pltpu.CompilerParams(vmem_limit_bytes=14 << 20),
        name="query_project",
    )(arrived, *in_hbm(weight), *after)


def key_value_parts(tokens, weight, sibling, place):
    rows, depth = tokens[0].shape
    half = depth // 2
    quarter = weight.shape[1] // 4
    count = len(tokens)

    def body(place_ref, *refs):
        token_refs, weight_ref, sibling_ref = refs[:count], refs[count], refs[count + 1]
        outs = refs[count + 2 :]
        stacked = jnp.concatenate([one[...] for one in token_refs], axis=0)
        for turn in range(4):
            start = pl.multiple_of(((place_ref[2] // 2) ^ turn) * quarter, quarter)
            part = jnp.dot(
                stacked[:, :half],
                weight_ref[:, pl.ds(start, quarter)],
                preferred_element_type=jnp.float32,
            ) + jnp.dot(
                stacked[:, half:],
                sibling_ref[:, pl.ds(start, quarter)],
                preferred_element_type=jnp.float32,
            )
            outs[turn][...] = part.astype(outs[turn].dtype)

    shapes = [
        jax.ShapeDtypeStruct((count * rows, quarter), jnp.float32 if turn == 0 else jnp.bfloat16)
        for turn in range(4)
    ]
    return pl.pallas_call(
        body,
        in_specs=[index_spec()] + [whole_spec()] * (count + 2),
        out_specs=[whole_spec()] * 4,
        out_shape=shapes,
        compiler_params=pltpu.CompilerParams(vmem_limit_bytes=8 << 20),
        name="key_value_parts",
    )(place, *tokens, weight, sibling)


def key_value_sum(parts, place):
    rows, quarter = parts[0].shape
    block = rows // 4

    def body(place_ref, *refs):
        ins, outs = refs[:4], refs[4:]
        req = place_ref[1]
        source = (req // 2) * 2 + place_ref[2] % 2
        for turn in range(4):
            start = pl.multiple_of((req ^ source ^ turn) * block, block)
            total = ins[0][pl.ds(start, block), :]
            for one in ins[1:]:
                total = total + one[pl.ds(start, block), :].astype(jnp.float32)
            outs[turn][...] = total.astype(jnp.bfloat16)

    return pl.pallas_call(
        body,
        in_specs=[index_spec()] + [whole_spec()] * 4,
        out_specs=[whole_spec()] * 4,
        out_shape=[jax.ShapeDtypeStruct((block, quarter), jnp.bfloat16)] * 4,
        compiler_params=pltpu.CompilerParams(vmem_limit_bytes=4 << 20),
        name="key_value_sum",
    )(place, *parts)


def attention(message, scalars, fresh_blocks, own, turned, relayed):
    blocks, _, span = message.shape
    heads = span // HEAD_DIM
    slots = blocks * CAP
    fresh_rows = fresh_blocks[0].shape[0]
    half = fresh_rows // blocks
    cache_rows = own.shape[0]
    scale = 1.0 / math.sqrt(HEAD_DIM)
    contract = (((1,), (1,)), ((), ()))

    def body(scalar_ref, in_ref, *refs):
        fresh_refs, own_ref, turned_refs, relay_ref = refs[:4], refs[4], refs[5:8], refs[8]
        out_ref = refs[9]
        limit, req, tok = scalar_ref[0], scalar_ref[1], scalar_ref[2]
        pieces = []
        for source in range(4):
            picked = fresh_refs[3][...]
            for turn in range(3):
                picked = jnp.where((req ^ source) == turn, fresh_refs[turn][...], picked)
            pieces.append(picked)
        new_keys = jnp.concatenate(pieces[:2], axis=0)
        new_values = jnp.concatenate(pieces[2:], axis=0)
        key_row = iota((1, blocks * cache_rows), 1)
        key_block = key_row // cache_rows
        key_source = ((key_block % 4) * 2 + key_block // 4) ^ tok
        cache_usable = key_source * cache_rows + key_row % cache_rows < limit
        new_row = iota((1, 2 * fresh_rows), 1)
        within = new_row % fresh_rows
        new_place = (within // half) * (2 * half) + (new_row // fresh_rows) * half + within % half
        places = []
        for expert in range(blocks):
            line = in_ref[expert, slots:, :LANES].astype(jnp.float32)[0:1]
            chosen = iota((slots, LANES), 0) == iota((slots, LANES), 1)
            places.append(jnp.sum(jnp.where(chosen, line, 0.0), axis=1, keepdims=True))
        new_usable = new_place <= jnp.concatenate(places, axis=0).astype(jnp.int32)
        flat = in_ref[:, :slots, :].reshape(blocks * slots, span)
        cached = [own_ref] + [one.at[:cache_rows] for one in turned_refs] + [relay_ref]
        keys = jnp.concatenate([one[:, :span] for one in cached], axis=0)
        values = jnp.concatenate([one[:, span:] for one in cached], axis=0)
        for head in range(heads):
            cols = slice(head * HEAD_DIM, (head + 1) * HEAD_DIM)
            query = flat[:, cols]
            first = lax.dot_general(
                query, keys[:, cols], contract, preferred_element_type=jnp.float32
            )
            second = lax.dot_general(
                query, new_keys[:, cols], contract, preferred_element_type=jnp.float32
            )
            first = jnp.where(cache_usable, first * scale, -1e30)
            second = jnp.where(new_usable, second * scale, -1e30)
            top = jnp.maximum(
                jnp.max(first, axis=-1, keepdims=True), jnp.max(second, axis=-1, keepdims=True)
            )
            first = jnp.exp(first - top).astype(jnp.bfloat16)
            second = jnp.exp(second - top).astype(jnp.bfloat16)
            sums = jnp.sum(first.astype(jnp.float32), axis=-1, keepdims=True) + jnp.sum(
                second.astype(jnp.float32), axis=-1, keepdims=True
            )
            mixed = jnp.dot(first, values[:, cols], preferred_element_type=jnp.float32) + jnp.dot(
                second, new_values[:, cols], preferred_element_type=jnp.float32
            )
            out_ref[:, :slots, cols] = (
                (mixed / sums).astype(jnp.bfloat16).reshape(blocks, slots, HEAD_DIM)
            )
        for kind in range(2):
            for part in range(2):
                start = slots + kind * 2 * half + part * half
                out_ref[:, start : start + half, :] = pieces[2 * kind + part].reshape(
                    blocks, half, span
                )

    return pl.pallas_call(
        body,
        in_specs=[index_spec()] + [whole_spec()] * 10,
        out_specs=whole_spec(),
        out_shape=jax.ShapeDtypeStruct((blocks, slots + 4 * half, span), jnp.bfloat16),
        compiler_params=pltpu.CompilerParams(vmem_limit_bytes=14 << 20),
        name="attention",
    )(scalars, message, *fresh_blocks, own, *turned, relayed)


def output_project(arrived, weight, query_rows):
    blocks, height, span = arrived.shape
    slots = blocks * CAP
    width = weight.shape[1]
    tile = width // 4

    def body(in_ref, weight_ref, out_ref, fresh_ref, held, sems):
        copies = column_stream(weight_ref, held, sems, tile)
        for one in copies:
            one.start()
        rows = []
        for block in range(blocks):
            cols = slice(block * span, (block + 1) * span)
            rows.append(spread(in_ref[block, :slots, :]).astype(jnp.bfloat16))
            fresh_ref[:, cols] = in_ref[block, slots : slots + query_rows, :]
            fresh_ref[:, block * span + width : (block + 1) * span + width] = in_ref[
                block, slots + query_rows :, :
            ]
        rows = jnp.concatenate(rows, axis=1)
        for step in range(width // tile):
            cols = slice(step * tile, (step + 1) * tile)
            copies[step].wait()
            part = jnp.dot(rows, held[step], preferred_element_type=jnp.float32)
            out_ref[:, :, cols] = part.astype(jnp.bfloat16).reshape(blocks, PAD, tile)

    return pl.pallas_call(
        body,
        in_specs=[whole_spec(), any_spec()],
        out_specs=[whole_spec()] * 2,
        out_shape=[
            jax.ShapeDtypeStruct((blocks, PAD, width), jnp.bfloat16),
            jax.ShapeDtypeStruct((query_rows, 2 * width), jnp.bfloat16),
        ],
        scratch_shapes=[
            pltpu.VMEM((width // tile, blocks * span, tile), jnp.bfloat16),
            pltpu.SemaphoreType.DMA((width // tile,)),
        ],
        compiler_params=pltpu.CompilerParams(vmem_limit_bytes=14 << 20),
        name="output_project",
    )(arrived, *in_hbm(weight))


def middle(activations, arrived, weights, gain, router, routes):
    rows, width = activations.shape
    blocks = arrived.shape[0]
    experts = router.shape[0]

    def body(act_ref, in_ref, old_ref, gain_ref, router_ref, route_ref, out_ref, mix_ref, new_ref):
        route = route_ref[...]
        added = exact_mix(old_ref[...], in_ref[...].reshape(blocks * PAD, width))
        mixed = (act_ref[...].astype(jnp.float32) + added).astype(jnp.bfloat16)
        mix_ref[...] = mixed
        hidden = row_norm(mixed.astype(jnp.float32), gain_ref[...])
        picks, first = padded_picks(route, experts)
        out_ref[...] = (
            pick_rows(picks, hidden).astype(jnp.bfloat16).reshape(blocks, PAD, width)
        )
        new_ref[...] = gate_weights(hidden, router_ref[...], route, picks, first)

    return pl.pallas_call(
        body,
        in_specs=[whole_spec()] * 6,
        out_specs=[whole_spec()] * 3,
        out_shape=[
            jax.ShapeDtypeStruct((blocks, PAD, width), jnp.bfloat16),
            jax.ShapeDtypeStruct((rows, width), jnp.bfloat16),
            jax.ShapeDtypeStruct((blocks * PAD, rows), jnp.float32),
        ],
        compiler_params=pltpu.CompilerParams(vmem_limit_bytes=4 << 20),
        name="middle",
    )(activations, arrived, weights, gain.reshape(1, width), router, routes)


def finish(mixed, arrived, weights):
    rows, width = mixed.shape

    def body(mix_ref, in_ref, weight_ref, out_ref):
        added = exact_mix(weight_ref[...], in_ref[...].reshape(-1, width))
        out_ref[...] = (mix_ref[...].astype(jnp.float32) + added).astype(jnp.bfloat16)

    return pl.pallas_call(
        body,
        in_specs=[whole_spec()] * 3,
        out_specs=whole_spec(),
        out_shape=jax.ShapeDtypeStruct((rows, width), jnp.bfloat16),
        compiler_params=pltpu.CompilerParams(vmem_limit_bytes=4 << 20),
        name="finish",
    )(mixed, arrived, weights)


def feedforward(arrived, gate_piece, down_piece):
    blocks, _, width = arrived.shape
    count = blocks * CAP
    units = down_piece.shape[0]
    tile = FF_TILE
    steps = units // tile
    slots = 4

    def body(in_ref, gate_ref, down_ref, out_ref, gates, ups, downs, sems):
        def copies(step):
            slot = step % slots
            return [
                pltpu.make_async_copy(
                    gate_ref.at[:, pl.ds(step * tile, tile)], gates.at[slot], sems.at[slot, 0]
                ),
                pltpu.make_async_copy(
                    gate_ref.at[:, pl.ds(units + step * tile, tile)],
                    ups.at[slot],
                    sems.at[slot, 1],
                ),
                pltpu.make_async_copy(
                    down_ref.at[pl.ds(step * tile, tile), :], downs.at[slot], sems.at[slot, 2]
                ),
            ]

        for step in range(slots):
            for one in copies(step):
                one.start()
        rows = compact(in_ref[...].reshape(blocks * PAD, width)).astype(jnp.bfloat16)
        total = jnp.zeros((count, width), jnp.float32)
        for step in range(steps):
            slot = step % slots
            gate_copy, up_copy, down_copy = copies(step)
            gate_copy.wait()
            gate = jnp.dot(rows, gates[slot], preferred_element_type=jnp.float32)
            up_copy.wait()
            up = jnp.dot(rows, ups[slot], preferred_element_type=jnp.float32)
            active = (gate / (1.0 + jnp.exp(-gate)) * up).astype(jnp.bfloat16)
            down_copy.wait()
            total = total + jnp.dot(active, downs[slot], preferred_element_type=jnp.float32)
            if step + slots < steps:
                for one in copies(step + slots):
                    one.start()
        out_ref[...] = (
            spread(total.astype(jnp.bfloat16)).astype(jnp.bfloat16).reshape(blocks, PAD, width)
        )

    return pl.pallas_call(
        body,
        in_specs=[whole_spec(), any_spec(), any_spec()],
        out_specs=whole_spec(),
        out_shape=jax.ShapeDtypeStruct(arrived.shape, jnp.bfloat16),
        scratch_shapes=[
            pltpu.VMEM((slots, width, tile), jnp.bfloat16),
            pltpu.VMEM((slots, width, tile), jnp.bfloat16),
            pltpu.VMEM((slots, tile, width), jnp.bfloat16),
            pltpu.SemaphoreType.DMA((slots, 3)),
        ],
        compiler_params=pltpu.CompilerParams(vmem_limit_bytes=32 << 20),
        name="feedforward",
    )(arrived, *in_hbm(gate_piece, down_piece))


def local_heads(
    activations,
    cache_entries,
    cache_lengths,
    attention_gain,
    feedforward_gain,
    key_value_weight,
    attention_router,
    attention_routes,
    query_weight,
    output_weight,
    feedforward_router,
    feedforward_routes,
    gate_up,
    down_weight,
):
    tok_count = lax.axis_size("tok")
    req_count = lax.axis_size("req")
    tok_index = lax.axis_index("tok")
    req_index = lax.axis_index("req")
    query_rows, width = activations.shape[1:]

    attn_routes = attention_routes[0].T
    ffn_routes = feedforward_routes[0].T
    place = jnp.stack([cache_lengths[0], req_index, tok_index])
    message, attn_weights = prepare(
        activations[0], attention_gain, attention_router.T, attn_routes, place, tok_count
    )
    arrived = swap_all(message, "tok")
    own_block, near, *turned = cache_split(cache_entries[0], place, attn_weights)
    turned = [
        permute(turned[turn - 1], "tok", [(one, one ^ (2 * turn)) for one in range(tok_count)])
        for turn in range(1, 4)
    ]
    pair = [(one, one ^ 1) for one in range(tok_count)]
    sibling = permute(key_value_weight, "tok", pair)
    projected = query_project(arrived, query_weight[0], [], tok_count)
    projected, *turned = lax.optimization_barrier((projected, *turned))
    queries = swap_all(projected, "tok")
    mine = own_tokens(arrived, [projected], tok_count, width)
    relayed = permute(cache_relay(near, turned), "tok", pair)
    tokens = [mine] + [
        permute(mine, "req", [(one, one ^ turn) for one in range(req_count)])
        for turn in range(1, req_count)
    ]
    parts = key_value_parts(tokens, key_value_weight, sibling, place)
    parts = [parts[0]] + [
        permute(parts[turn], "tok", [(one, one ^ (2 * turn)) for one in range(tok_count)])
        for turn in range(1, 4)
    ]
    sums = key_value_sum(parts, place)
    fresh_blocks = []
    for turn in range(4):
        pairs = []
        for one in range(req_count * tok_count):
            r, t = one // tok_count, one % tok_count
            dest = ((r // 2) * 2 + t % 2) ^ turn
            pairs.append((one, dest * tok_count + 4 * (r % 2) + t // 2))
        fresh_blocks.append(permute(sums[turn], ("req", "tok"), pairs))
    attended = attention(queries, place, fresh_blocks, own_block, turned, relayed)
    attended = swap_all(attended, "tok")
    parts_out, new_keys_values = output_project(attended, output_weight[0], query_rows)
    output_back = swap_all(parts_out, "tok")
    ffn_send, mixed_rows, ffn_weights = middle(
        activations[0],
        output_back,
        attn_weights,
        feedforward_gain,
        feedforward_router.T,
        ffn_routes,
    )
    received = swap_all(ffn_send, "tok")
    expert_parts = feedforward(received, gate_up[0], down_weight[0])
    expert_back = swap_all(expert_parts, "tok")
    layer_output = finish(mixed_rows, expert_back, ffn_weights)
    return (layer_output[None], new_keys_values[None])


def solution(mesh):
    placed = (
        P("req", "tok", None),
        P("req", "tok", None),
        P("req"),
        P(),
        P(),
        P("tok", "req"),
        P(),
        P("req", "tok", None),
        P("tok", None, None),
        P("tok", None, None),
        P(),
        P("req", "tok", None),
        P("tok", None, None),
        P("tok", None, None),
    )
    sizes = dict(mesh.shape)
    by_heads = sizes["tok"] == 8 and sizes["req"] == 4
    return jax.shard_map(
        local_heads if by_heads else local,
        mesh=mesh,
        in_specs=placed,
        out_specs=(P("req", "tok", None), P("req", "tok", None)),
        check_vma=False,
    )
```

```python
import math

import jax
import jax.numpy as jnp
from jax import lax
from jax.experimental import pallas as pl
from jax.experimental.pallas import tpu as pltpu
from jax.sharding import PartitionSpec as P

HEADS = 16
HEAD_DIM = 128
CAP = 6


def normed(values, gain):
    scale_rows = lax.rsqrt(jnp.mean(values * values, axis=-1, keepdims=True) + 1e-06)
    return values * scale_rows * gain


def slot_matrix(routes, experts, capacity):
    row_count, top_count = routes.shape
    labels = jnp.arange(experts, dtype=jnp.int32)
    onehot = (routes.reshape(row_count * top_count, 1) == labels[None, :]).astype(jnp.int32)
    before = jnp.cumsum(onehot, axis=0) - onehot
    within = jnp.sum(before * onehot, axis=1)
    placed = routes.reshape(row_count * top_count) * capacity + within
    columns = jnp.arange(experts * capacity, dtype=jnp.int32)
    return (placed[:, None] == columns[None, :]).astype(jnp.float32)


def router_gates(hidden, router, routes):
    logits = jnp.dot(hidden, router, preferred_element_type=jnp.float32)
    picked = jnp.take_along_axis(logits, routes, axis=1)
    return jax.nn.sigmoid(2.0 * picked - jnp.sum(picked, axis=1, keepdims=True))


def token_matrices(pair_slots, gates, top_count):
    row_count = gates.shape[0]
    per_token = pair_slots.reshape(row_count, top_count, -1)
    picked = jnp.sum(per_token, axis=1)
    weighted = jnp.sum(per_token * gates[:, :, None], axis=1)
    return (picked, weighted)


def spread_slots(slot_rows, experts, groups, capacity):
    feat_width = slot_rows.shape[-1]
    shaped = slot_rows.reshape(experts, 1, capacity, feat_width)
    return jnp.broadcast_to(shaped, (experts, groups, capacity, feat_width)).reshape(
        experts * groups, capacity, feat_width
    )


def head_groups(rows, experts, groups, group_width):
    row_count = rows.shape[0]
    shaped = (
        rows.reshape(row_count, 2, groups, group_width)
        .transpose(2, 0, 1, 3)
        .reshape(groups, row_count, 2 * group_width)
    )
    return jnp.broadcast_to(shaped[None], (experts, groups, row_count, 2 * group_width)).reshape(
        experts * groups, row_count, 2 * group_width
    )


def group_sum(received, experts, groups, capacity):
    feat_width = received.shape[-1]
    summed = jnp.sum(
        received.reshape(experts, groups, capacity, feat_width).astype(jnp.float32), axis=1
    )
    return summed.reshape(experts * capacity, feat_width)


def expert_feedforward(received, gate_piece, down_piece):
    units = down_piece.shape[0]
    projected = jnp.einsum("scd,df->scf", received, gate_piece, preferred_element_type=jnp.float32)
    active = (jax.nn.silu(projected[..., :units]) * projected[..., units:]).astype(jnp.bfloat16)
    return jnp.einsum("scf,fd->scd", active, down_piece, preferred_element_type=jnp.float32).astype(
        jnp.bfloat16
    )


def local(
    activations,
    cache_entries,
    cache_lengths,
    attention_gain,
    feedforward_gain,
    key_value_weight,
    attention_router,
    attention_routes,
    query_weight,
    output_weight,
    feedforward_router,
    feedforward_routes,
    gate_up,
    down_weight,
):
    tok_count = lax.axis_size("tok")
    tok_index = lax.axis_index("tok")
    experts = attention_router.shape[1]
    groups = tok_count // experts
    query_rows = activations.shape[1]
    cache_rows = cache_entries.shape[1]
    top_count = attention_routes.shape[2]
    model_width = activations.shape[2]
    head_count = HEADS // groups
    group_width = head_count * HEAD_DIM
    block_span = cache_rows + query_rows
    score_scale = 1.0 / math.sqrt(HEAD_DIM)
    cache_part = cache_entries[0]
    residual_in = activations[0].astype(jnp.float32)
    hidden = normed(residual_in, attention_gain).astype(jnp.bfloat16)
    stacked = lax.all_gather(hidden, "req", axis=0, tiled=True)
    projected_part = jnp.dot(
        stacked,
        lax.all_gather(key_value_weight, "tok", axis=0, tiled=True),
        preferred_element_type=jnp.float32,
    )
    new_keys_values = lax.all_to_all(
        projected_part.astype(jnp.bfloat16), "req", split_axis=0, concat_axis=1, tiled=True
    )
    combined = jnp.concatenate([cache_part, new_keys_values], axis=0)
    group_keys = lax.all_to_all(
        head_groups(combined, experts, groups, group_width),
        "tok",
        split_axis=0,
        concat_axis=0,
        tiled=True,
    )
    attn_routes = attention_routes[0]
    attn_pairs = slot_matrix(attn_routes, experts, CAP)
    attn_gate = router_gates(hidden, attention_router, attn_routes)
    attn_pick, attn_weights = token_matrices(attn_pairs, attn_gate, top_count)
    slot_inputs = jnp.dot(
        attn_pick.T.astype(jnp.bfloat16), hidden, preferred_element_type=jnp.float32
    ).astype(jnp.bfloat16)
    token_place = tok_index * query_rows + jnp.arange(query_rows, dtype=jnp.int32)
    slot_place = jnp.sum(attn_pick.astype(jnp.int32) * token_place[:, None], axis=0)
    query_send = spread_slots(slot_inputs, experts, groups, CAP)
    place_send = jnp.broadcast_to(
        slot_place.reshape(experts, 1, CAP), (experts, groups, CAP)
    ).reshape(tok_count, CAP)
    length = cache_lengths[0]
    source = jnp.arange(tok_count, dtype=jnp.int32).reshape(groups, experts, 1)
    offset = jnp.arange(block_span, dtype=jnp.int32).reshape(1, 1, block_span)
    turn_shape = (groups, experts * block_span)
    cached = jnp.broadcast_to(offset < cache_rows, (groups, experts, block_span)).reshape(
        turn_shape
    )
    cache_usable = (source * cache_rows + offset < length).reshape(turn_shape)
    fresh_place = (source * query_rows + offset - cache_rows).reshape(turn_shape)
    key_turns = group_keys.reshape(groups, experts * block_span, 2, head_count, HEAD_DIM)
    slot_rows = lax.all_to_all(query_send, "tok", split_axis=0, concat_axis=0, tiled=True)
    slot_places = lax.all_to_all(place_send, "tok", split_axis=0, concat_axis=0, tiled=True)
    items = slot_rows.shape[1]
    query_three = (
        jnp.einsum("scd,df->scf", slot_rows, query_weight[0], preferred_element_type=jnp.float32)
        .astype(jnp.bfloat16)
        .reshape(tok_count * items, head_count, HEAD_DIM)
    )
    query_place = slot_places.reshape(tok_count * items)

    def one_turn(state_in, turn_data):
        row_max, row_sums, weighted = state_in
        keys_values, cached_turn, usable_turn, place_turn = turn_data
        usable = jnp.where(
            cached_turn[None, :], usable_turn[None, :], place_turn[None, :] <= query_place[:, None]
        )[None]
        scores = (
            jnp.einsum(
                "phd,khd->hpk", query_three, keys_values[:, 0], preferred_element_type=jnp.float32
            )
            * score_scale
        )
        scores = jnp.where(usable, scores, -1e30)
        new_max = jnp.maximum(row_max, jnp.max(scores, axis=-1))
        weights = jnp.where(usable, jnp.exp(scores - new_max[..., None]), 0.0).astype(jnp.bfloat16)
        factor = jnp.exp(row_max - new_max)
        row_sums = row_sums * factor + jnp.sum(weights.astype(jnp.float32), axis=-1)
        weighted = weighted * factor[..., None] + jnp.einsum(
            "hpk,khd->hpd", weights, keys_values[:, 1], preferred_element_type=jnp.float32
        )
        return ((new_max, row_sums, weighted), None)

    query_total = tok_count * items
    initial = (
        jnp.full((head_count, query_total), -1e30, jnp.float32),
        jnp.zeros((head_count, query_total), jnp.float32),
        jnp.zeros((head_count, query_total, HEAD_DIM), jnp.float32),
    )
    final_state, _ = lax.scan(one_turn, initial, (key_turns, cached, cache_usable, fresh_place))
    row_max, row_sums, weighted = final_state
    attended = (
        (weighted / row_sums[..., None])
        .astype(jnp.bfloat16)
        .transpose(1, 0, 2)
        .reshape(tok_count, items, group_width)
    )
    parts = jnp.einsum(
        "scf,fd->scd", attended, output_weight[0], preferred_element_type=jnp.float32
    ).astype(jnp.bfloat16)
    output_back = lax.all_to_all(parts, "tok", split_axis=0, concat_axis=0, tiled=True)
    output_sums = group_sum(output_back, experts, groups, CAP)
    mixed_rows = (
        residual_in + jnp.dot(attn_weights, output_sums, precision=lax.Precision.HIGHEST)
    ).astype(jnp.bfloat16)
    hidden_two = normed(mixed_rows.astype(jnp.float32), feedforward_gain).astype(jnp.bfloat16)
    ffn_routes = feedforward_routes[0]
    ffn_pairs = slot_matrix(ffn_routes, experts, CAP)
    ffn_gate = router_gates(hidden_two, feedforward_router, ffn_routes)
    ffn_pick, ffn_weights = token_matrices(ffn_pairs, ffn_gate, top_count)
    every_rows, every_routes = (
        lax.all_gather(hidden_two, "tok", axis=0, tiled=True),
        lax.all_gather(ffn_routes, "tok", axis=0, tiled=True),
    )
    routes_all = every_routes.reshape(tok_count, query_rows, top_count)

    def source_slots(routes_block):
        return slot_matrix(routes_block, experts, CAP)

    per_source = jax.vmap(source_slots)(routes_all)
    per_token = jnp.sum(per_source.reshape(tok_count, query_rows, top_count, experts, CAP), axis=2)
    expert_mask = (jnp.arange(experts, dtype=jnp.int32) == tok_index // groups).astype(jnp.float32)
    picked = jnp.einsum("sqec,e->sqc", per_token, expert_mask)
    received = jnp.einsum(
        "sqc,sqd->scd",
        picked.astype(jnp.bfloat16),
        every_rows.reshape(tok_count, query_rows, model_width),
        preferred_element_type=jnp.float32,
    ).astype(jnp.bfloat16)
    expert_parts = expert_feedforward(received, gate_up[0], down_weight[0])
    expert_back = lax.all_to_all(expert_parts, "tok", split_axis=0, concat_axis=0, tiled=True)
    expert_sums = group_sum(expert_back, experts, groups, CAP)
    layer_output = (
        mixed_rows.astype(jnp.float32)
        + jnp.dot(ffn_weights, expert_sums, precision=lax.Precision.HIGHEST)
    ).astype(jnp.bfloat16)
    return (layer_output[None], new_keys_values[None])


PAD = 8
LANES = 128
FF_TILE = 512


def column_stream(source, buffers, sems, tile):
    return [
        pltpu.make_async_copy(
            source.at[:, pl.ds(step * tile, tile)], buffers.at[step], sems.at[step]
        )
        for step in range(buffers.shape[0])
    ]


def permute(values, axis, pairs):
    return lax.ppermute(values, axis, pairs)


def swap_all(values, axis):
    return lax.all_to_all(values, axis, split_axis=0, concat_axis=0, tiled=True)


def whole_spec():
    return pl.BlockSpec(memory_space=pltpu.VMEM)


def index_spec():
    return pl.BlockSpec(memory_space=pltpu.SMEM)


def iota(shape, axis):
    return lax.broadcasted_iota(jnp.int32, shape, axis)


def any_spec():
    return pl.BlockSpec(memory_space=pl.ANY)


def in_hbm(*arrays):
    return [pltpu.with_memory_space_constraint(one, pltpu.HBM) for one in arrays]


def in_vmem(*arrays):
    return [pltpu.with_memory_space_constraint(one, pltpu.VMEM) for one in arrays]


def load_all(pairs, sems):
    copies = [
        pltpu.make_async_copy(source, target, sems.at[number])
        for number, (source, target) in enumerate(pairs)
    ]
    for one in copies:
        one.start()
    for one in copies:
        one.wait()


def padded_picks(routes, experts):
    row_count = routes.shape[1]
    row = iota((experts * PAD, row_count), 0)
    expert, slot = row // PAD, row % PAD
    first, second = routes[0:1, :] == expert, routes[1:2, :] == expert
    named = jnp.where(first, 1.0, 0.0) + jnp.where(second, 1.0, 0.0)
    earlier = (iota((row_count, row_count), 0) < iota((row_count, row_count), 1)).astype(
        jnp.bfloat16
    )
    before = jnp.dot(
        named.astype(jnp.bfloat16), earlier, preferred_element_type=jnp.float32
    ).astype(jnp.int32)
    here = (before == slot) & (slot < CAP)
    return named * here.astype(jnp.float32), first


def gate_weights(hidden, router, routes, picks, first):
    logits = lax.dot_general(
        router, hidden, (((1,), (1,)), ((), ())), preferred_element_type=jnp.float32
    )
    label = iota(logits.shape, 0)
    one = jnp.sum(jnp.where(routes[0:1, :] == label, logits, 0.0), axis=0, keepdims=True)
    two = jnp.sum(jnp.where(routes[1:2, :] == label, logits, 0.0), axis=0, keepdims=True)
    gate_one = 1.0 / (1.0 + jnp.exp(two - one))
    gate_two = 1.0 / (1.0 + jnp.exp(one - two))
    return picks * jnp.where(first, gate_one, gate_two)


def row_norm(values, gain):
    mean = jnp.mean(values * values, axis=-1, keepdims=True)
    return (values * lax.rsqrt(mean + 1e-06) * gain).astype(jnp.bfloat16)


def pick_rows(picks, rows):
    return jnp.dot(picks.astype(jnp.bfloat16), rows, preferred_element_type=jnp.float32)


def compact(rows):
    count = rows.shape[0] // PAD * CAP
    one, two = iota((count, rows.shape[0]), 0), iota((count, rows.shape[0]), 1)
    chosen = ((one // CAP) * PAD + one % CAP == two).astype(jnp.bfloat16)
    return jnp.dot(chosen, rows, preferred_element_type=jnp.float32)


def spread(rows):
    count = rows.shape[0] // CAP * PAD
    one, two = iota((count, rows.shape[0]), 0), iota((count, rows.shape[0]), 1)
    chosen = ((two // CAP) * PAD + two % CAP == one).astype(jnp.bfloat16)
    return jnp.dot(chosen, rows, preferred_element_type=jnp.float32)


def exact_mix(weights, rows):
    high = weights.astype(jnp.bfloat16)
    rest = weights - high.astype(jnp.float32)
    middle = rest.astype(jnp.bfloat16)
    low = (rest - middle.astype(jnp.float32)).astype(jnp.bfloat16)
    count = weights.shape[1]
    stacked = lax.dot_general(
        jnp.concatenate([high, middle, low], axis=1),
        rows,
        (((0,), (0,)), ((), ())),
        preferred_element_type=jnp.float32,
    )
    return stacked[:count] + (stacked[count : 2 * count] + stacked[2 * count :])


def prepare(activations, gain, router, routes, place, tok_count):
    rows, width = activations.shape
    experts = router.shape[0]
    span = width // tok_count
    half = rows // 2
    per_row = width // (2 * span)

    def body(
        place_ref, act_in, gain_in, router_in, route_in, out_ref, weight_ref,
        act_ref, gain_ref, router_ref, route_ref, wide, copy, sems,
    ):
        load_all(
            [
                (act_in, act_ref),
                (gain_in, gain_ref),
                (router_in, router_ref),
                (route_in, route_ref),
            ],
            sems,
        )
        route = route_ref[...]
        hidden = row_norm(act_ref[...].astype(jnp.float32), gain_ref[...])
        picks, first = padded_picks(route, experts)
        wide[...] = pick_rows(picks, hidden)
        copy[...] = hidden.astype(jnp.float32)
        for dest in range(tok_count):
            chip, core = dest // 2, dest % 2
            for place in range(half):
                row = dest * PAD + CAP + place // per_row
                for side in range(2):
                    column = (place % per_row) * 2 * span + side * span
                    source = (2 * chip + (core ^ side)) * span
                    wide[row : row + 1, column : column + span] = copy[
                        core * half + place : core * half + place + 1, source : source + span
                    ]
        out_ref[:, :, :width] = wide[...].astype(jnp.bfloat16).reshape(tok_count, PAD, width)
        number = iota((rows, LANES), 0).astype(jnp.float32).astype(jnp.bfloat16)
        out_ref[:, :, width:] = (
            pick_rows(picks, number).astype(jnp.bfloat16).reshape(tok_count, PAD, LANES)
        )
        weight_ref[...] = gate_weights(hidden, router_ref[...], route, picks, first)

    return pl.pallas_call(
        body,
        in_specs=[index_spec()] + [any_spec()] * 4,
        out_specs=[whole_spec()] * 2,
        out_shape=[
            jax.ShapeDtypeStruct((tok_count, PAD, width + LANES), jnp.bfloat16),
            jax.ShapeDtypeStruct((tok_count * PAD, rows), jnp.float32),
        ],
        scratch_shapes=[
            pltpu.VMEM((rows, width), activations.dtype),
            pltpu.VMEM((1, width), gain.dtype),
            pltpu.VMEM(router.shape, router.dtype),
            pltpu.VMEM(routes.shape, routes.dtype),
            pltpu.VMEM((tok_count * PAD, width), jnp.float32),
            pltpu.VMEM((rows, width), jnp.float32),
            pltpu.SemaphoreType.DMA((4,)),
        ],
        compiler_params=pltpu.CompilerParams(vmem_limit_bytes=4 << 20),
        name="prepare",
    )(place, *in_hbm(activations, gain.reshape(1, width), router, routes))


def cache_split(cache_part, side, place, after):
    rows, width = cache_part.shape
    count = 8
    span = width // 2 // count

    def body(index_ref, cache_ref, side_ref, after_ref, *refs):
        outs, side_out, sem = refs[:5], refs[5], refs[6]
        side_copy = pltpu.make_async_copy(side_ref, side_out, sem)
        side_copy.start()

        def piece(other):
            start = pl.multiple_of((index_ref[2] ^ other) * span, span)
            return cache_ref[:, pl.ds(start, span)], cache_ref[:, pl.ds(start + width // 2, span)]

        for turn in range(4):
            for side in range(2):
                keys, values = piece(2 * turn + side)
                if turn:
                    out, base = outs[turn + 1], side * rows
                else:
                    out, base = outs[side], 0
                out[base : base + rows, :span] = keys
                out[base : base + rows, span:] = values
        side_copy.wait()

    shapes = [(rows, 2 * span)] * 2 + [(2 * rows, 2 * span)] * 3
    return pl.pallas_call(
        body,
        in_specs=[index_spec(), whole_spec(), any_spec(), any_spec()],
        out_specs=[whole_spec()] * 6,
        out_shape=[jax.ShapeDtypeStruct(one, cache_part.dtype) for one in shapes]
        + [pltpu.VMEM(side.shape, side.dtype)],
        scratch_shapes=[pltpu.SemaphoreType.DMA(())],
        compiler_params=pltpu.CompilerParams(vmem_limit_bytes=4 << 20),
        name="cache_split",
    )(place, cache_part, *in_hbm(side), after)


def cache_relay(near, turned):
    rows, width = near.shape

    def body(near_ref, *refs):
        out_ref = refs[-1]
        out_ref[:rows, :] = near_ref[...]
        for turn in range(1, 4):
            out_ref[turn * rows : (turn + 1) * rows, :] = refs[turn - 1][rows:, :]

    return pl.pallas_call(
        body,
        in_specs=[whole_spec()] * 4,
        out_specs=whole_spec(),
        out_shape=jax.ShapeDtypeStruct((4 * rows, width), near.dtype),
        compiler_params=pltpu.CompilerParams(vmem_limit_bytes=3 << 20),
        name="cache_relay",
    )(near, *turned)


def own_tokens(arrived, after, tok_count, width):
    span = width // tok_count
    per_row = width // (2 * span)
    extra = PAD - CAP

    def body(in_ref, *rest):
        out_ref, wide = rest[len(after) :]
        for source in range(tok_count):
            rows = in_ref[source, :, :width].astype(jnp.float32)
            for part in range(extra):
                for place in range(per_row):
                    row = source * extra * per_row + part * per_row + place
                    wide[row : row + 1, :] = rows[
                        CAP + part : CAP + part + 1, place * 2 * span : (place + 1) * 2 * span
                    ]
        out_ref[...] = wide[...].astype(jnp.bfloat16)

    count = tok_count * extra * per_row
    return pl.pallas_call(
        body,
        in_specs=[whole_spec()] + [any_spec()] * len(after),
        out_specs=whole_spec(),
        out_shape=jax.ShapeDtypeStruct((count, 2 * span), jnp.bfloat16),
        scratch_shapes=[pltpu.VMEM((count, 2 * span), jnp.float32)],
        compiler_params=pltpu.CompilerParams(vmem_limit_bytes=4 << 20),
        name="own_tokens",
    )(arrived, *after)


def query_project(arrived, weight, after, tok_count):
    width = weight.shape[0]
    span = width // tok_count
    slots = tok_count * CAP
    height = slots + PAD
    tile = 2 * span
    steps = width // tile

    def body(in_ref, weight_ref, *rest):
        out_ref, held, sems = rest[len(after) :]
        copies = column_stream(weight_ref, held, sems, tile)
        for one in copies:
            one.start()
        every = compact(in_ref[...].reshape(tok_count * PAD, width + LANES))
        rows = every[:, :width].astype(jnp.bfloat16)
        local = every[:, width : width + LANES]
        mine = iota(local.shape, 0)
        placed = local + ((mine // CAP) * (2 * PAD)).astype(jnp.float32)
        placed = jnp.where(mine == iota(local.shape, 1), placed, 0.0)
        line = jnp.broadcast_to(jnp.sum(placed, axis=0, keepdims=True), (PAD, LANES))
        line = jnp.concatenate([line] * (span // LANES), axis=1).astype(jnp.bfloat16)
        for step in range(steps):
            copies[step].wait()
            query = jnp.dot(rows, held[step], preferred_element_type=jnp.float32).astype(
                jnp.bfloat16
            )
            for one in range(tile // span):
                place = step * (tile // span) + one
                out_ref[place, :slots, :] = query[:, one * span : (one + 1) * span]
                out_ref[place, slots:, :] = line
    return pl.pallas_call(
        body,
        in_specs=[whole_spec(), any_spec()] + [any_spec()] * len(after),
        out_specs=whole_spec(),
        out_shape=jax.ShapeDtypeStruct((tok_count, height, span), jnp.bfloat16),
        scratch_shapes=[
            pltpu.VMEM((steps, width, tile), jnp.bfloat16),
            pltpu.SemaphoreType.DMA((steps,)),
        ],
        compiler_params=pltpu.CompilerParams(vmem_limit_bytes=14 << 20),
        cost_estimate=pl.CostEstimate(flops=0, transcendentals=0, bytes_accessed=40 << 20),
        name="query_project",
    )(arrived, *in_hbm(weight), *after)


def key_value_parts(tokens, weight, sibling, place, after):
    rows, depth = tokens[0].shape
    half = depth // 2
    quarter = weight.shape[1] // 4
    count = len(tokens)

    def body(place_ref, *refs):
        token_refs, weight_ref, sibling_ref = refs[:count], refs[count], refs[count + 1]
        outs = refs[count + 2 + len(after) :]
        stacked = jnp.concatenate([one[...] for one in token_refs], axis=0)
        for turn in range(4):
            start = pl.multiple_of(((place_ref[2] // 2) ^ turn) * quarter, quarter)
            part = jnp.dot(
                stacked[:, :half],
                weight_ref[:, pl.ds(start, quarter)],
                preferred_element_type=jnp.float32,
            ) + jnp.dot(
                stacked[:, half:],
                sibling_ref[:, pl.ds(start, quarter)],
                preferred_element_type=jnp.float32,
            )
            outs[turn][...] = part.astype(outs[turn].dtype)

    shapes = [
        jax.ShapeDtypeStruct((count * rows, quarter), jnp.float32 if turn == 0 else jnp.bfloat16)
        for turn in range(4)
    ]
    return pl.pallas_call(
        body,
        in_specs=[index_spec()] + [whole_spec()] * (count + 2) + [any_spec()] * len(after),
        out_specs=[whole_spec()] * 4,
        out_shape=shapes,
        compiler_params=pltpu.CompilerParams(vmem_limit_bytes=8 << 20),
        name="key_value_parts",
    )(place, *tokens, weight, sibling, *after)


def key_value_sum(parts, place, after):
    rows, quarter = parts[0].shape
    block = rows // 4

    def body(place_ref, *refs):
        ins, outs = refs[:4], refs[5:]
        req = place_ref[1]
        source = (req // 2) * 2 + place_ref[2] % 2
        for turn in range(4):
            start = pl.multiple_of((req ^ source ^ turn) * block, block)
            total = ins[0][pl.ds(start, block), :]
            for one in ins[1:]:
                total = total + one[pl.ds(start, block), :].astype(jnp.float32)
            outs[turn][...] = total.astype(jnp.bfloat16)

    return pl.pallas_call(
        body,
        in_specs=[index_spec()] + [whole_spec()] * 4 + [any_spec()],
        out_specs=[whole_spec()] * 4,
        out_shape=[jax.ShapeDtypeStruct((block, quarter), jnp.bfloat16)] * 4,
        compiler_params=pltpu.CompilerParams(vmem_limit_bytes=4 << 20),
        name="key_value_sum",
    )(place, *parts, after)


def attention(message, scalars, fresh_blocks, own, turned, relayed):
    blocks, _, span = message.shape
    heads = span // HEAD_DIM
    slots = blocks * CAP
    fresh_rows = fresh_blocks[0].shape[0]
    half = fresh_rows // blocks
    cache_rows = own.shape[0]
    scale = 1.0 / math.sqrt(HEAD_DIM)
    contract = (((1,), (1,)), ((), ()))

    def body(scalar_ref, in_ref, *refs):
        fresh_refs, own_ref, turned_refs, relay_ref = refs[:4], refs[4], refs[5:8], refs[8]
        out_ref = refs[9]
        limit, req, tok = scalar_ref[0], scalar_ref[1], scalar_ref[2]
        pieces = []
        for source in range(4):
            picked = fresh_refs[3][...]
            for turn in range(3):
                picked = jnp.where((req ^ source) == turn, fresh_refs[turn][...], picked)
            pieces.append(picked)
        new_keys = jnp.concatenate(pieces[:2], axis=0)
        new_values = jnp.concatenate(pieces[2:], axis=0)
        key_row = iota((1, blocks * cache_rows), 1)
        key_block = key_row // cache_rows
        key_source = ((key_block % 4) * 2 + key_block // 4) ^ tok
        cache_usable = key_source * cache_rows + key_row % cache_rows < limit
        new_row = iota((1, 2 * fresh_rows), 1)
        within = new_row % fresh_rows
        new_place = (within // half) * (2 * half) + (new_row // fresh_rows) * half + within % half
        places = []
        for expert in range(blocks):
            line = in_ref[expert, slots:, :LANES].astype(jnp.float32)[0:1]
            chosen = iota((slots, LANES), 0) == iota((slots, LANES), 1)
            places.append(jnp.sum(jnp.where(chosen, line, 0.0), axis=1, keepdims=True))
        new_usable = new_place <= jnp.concatenate(places, axis=0).astype(jnp.int32)
        flat = in_ref[:, :slots, :].reshape(blocks * slots, span)
        cached = [own_ref] + [one.at[:cache_rows] for one in turned_refs] + [relay_ref]
        keys = jnp.concatenate([one[:, :span] for one in cached], axis=0)
        values = jnp.concatenate([one[:, span:] for one in cached], axis=0)
        for head in range(heads):
            cols = slice(head * HEAD_DIM, (head + 1) * HEAD_DIM)
            query = flat[:, cols]
            first = lax.dot_general(
                query, keys[:, cols], contract, preferred_element_type=jnp.float32
            )
            second = lax.dot_general(
                query, new_keys[:, cols], contract, preferred_element_type=jnp.float32
            )
            first = jnp.where(cache_usable, first * scale, -1e30)
            second = jnp.where(new_usable, second * scale, -1e30)
            top = jnp.maximum(
                jnp.max(first, axis=-1, keepdims=True), jnp.max(second, axis=-1, keepdims=True)
            )
            first = jnp.exp(first - top).astype(jnp.bfloat16)
            second = jnp.exp(second - top).astype(jnp.bfloat16)
            sums = jnp.sum(first.astype(jnp.float32), axis=-1, keepdims=True) + jnp.sum(
                second.astype(jnp.float32), axis=-1, keepdims=True
            )
            mixed = jnp.dot(first, values[:, cols], preferred_element_type=jnp.float32) + jnp.dot(
                second, new_values[:, cols], preferred_element_type=jnp.float32
            )
            out_ref[:, :slots, cols] = (
                (mixed / sums).astype(jnp.bfloat16).reshape(blocks, slots, HEAD_DIM)
            )
        for kind in range(2):
            for part in range(2):
                start = slots + kind * 2 * half + part * half
                out_ref[:, start : start + half, :] = pieces[2 * kind + part].reshape(
                    blocks, half, span
                )

    return pl.pallas_call(
        body,
        in_specs=[index_spec()] + [whole_spec()] * 10,
        out_specs=whole_spec(),
        out_shape=jax.ShapeDtypeStruct((blocks, slots + 4 * half, span), jnp.bfloat16),
        compiler_params=pltpu.CompilerParams(vmem_limit_bytes=14 << 20),
        name="attention",
    )(scalars, message, *fresh_blocks, own, *turned, relayed)


def output_project(arrived, weight, query_rows):
    blocks, height, span = arrived.shape
    slots = blocks * CAP
    width = weight.shape[1]
    tile = width // 4

    def body(in_ref, weight_ref, out_ref, fresh_ref, held, sems):
        copies = column_stream(weight_ref, held, sems, tile)
        for one in copies:
            one.start()
        rows = []
        for block in range(blocks):
            cols = slice(block * span, (block + 1) * span)
            rows.append(spread(in_ref[block, :slots, :]).astype(jnp.bfloat16))
            fresh_ref[:, cols] = in_ref[block, slots : slots + query_rows, :]
            fresh_ref[:, block * span + width : (block + 1) * span + width] = in_ref[
                block, slots + query_rows :, :
            ]
        rows = jnp.concatenate(rows, axis=1)
        for step in range(width // tile):
            cols = slice(step * tile, (step + 1) * tile)
            copies[step].wait()
            part = jnp.dot(rows, held[step], preferred_element_type=jnp.float32)
            out_ref[:, :, cols] = part.astype(jnp.bfloat16).reshape(blocks, PAD, tile)

    return pl.pallas_call(
        body,
        in_specs=[whole_spec(), any_spec()],
        out_specs=[whole_spec()] * 2,
        out_shape=[
            jax.ShapeDtypeStruct((blocks, PAD, width), jnp.bfloat16),
            jax.ShapeDtypeStruct((query_rows, 2 * width), jnp.bfloat16),
        ],
        scratch_shapes=[
            pltpu.VMEM((width // tile, blocks * span, tile), jnp.bfloat16),
            pltpu.SemaphoreType.DMA((width // tile,)),
        ],
        compiler_params=pltpu.CompilerParams(vmem_limit_bytes=14 << 20),
        name="output_project",
    )(arrived, *in_hbm(weight))


def middle(activations, arrived, weights, gain, router, routes):
    rows, width = activations.shape
    blocks = arrived.shape[0]
    experts = router.shape[0]

    def body(act_ref, in_ref, old_ref, gain_ref, router_ref, route_ref, out_ref, mix_ref, new_ref):
        route = route_ref[...]
        added = exact_mix(old_ref[...], in_ref[...].reshape(blocks * PAD, width))
        mixed = (act_ref[...].astype(jnp.float32) + added).astype(jnp.bfloat16)
        mix_ref[...] = mixed
        hidden = row_norm(mixed.astype(jnp.float32), gain_ref[...])
        picks, first = padded_picks(route, experts)
        out_ref[...] = (
            pick_rows(picks, hidden).astype(jnp.bfloat16).reshape(blocks, PAD, width)
        )
        new_ref[...] = gate_weights(hidden, router_ref[...], route, picks, first)

    return pl.pallas_call(
        body,
        in_specs=[whole_spec()] * 6,
        out_specs=[whole_spec()] * 3,
        out_shape=[
            jax.ShapeDtypeStruct((blocks, PAD, width), jnp.bfloat16),
            jax.ShapeDtypeStruct((rows, width), jnp.bfloat16),
            jax.ShapeDtypeStruct((blocks * PAD, rows), jnp.float32),
        ],
        compiler_params=pltpu.CompilerParams(vmem_limit_bytes=4 << 20),
        name="middle",
    )(activations, arrived, weights, gain.reshape(1, width), router, routes)


def finish(mixed, arrived, weights):
    rows, width = mixed.shape

    def body(mix_ref, in_ref, weight_ref, out_ref):
        added = exact_mix(weight_ref[...], in_ref[...].reshape(-1, width))
        out_ref[...] = (mix_ref[...].astype(jnp.float32) + added).astype(jnp.bfloat16)

    return pl.pallas_call(
        body,
        in_specs=[whole_spec()] * 3,
        out_specs=whole_spec(),
        out_shape=jax.ShapeDtypeStruct((rows, width), jnp.bfloat16),
        compiler_params=pltpu.CompilerParams(vmem_limit_bytes=4 << 20),
        name="finish",
    )(mixed, arrived, weights)


def feedforward(arrived, gate_piece, down_piece):
    blocks, _, width = arrived.shape
    count = blocks * CAP
    units = down_piece.shape[0]
    tile = FF_TILE
    steps = units // tile
    slots = 4

    def body(in_ref, gate_ref, down_ref, out_ref, gates, ups, downs, sems):
        def copies(step):
            slot = step % slots
            return [
                pltpu.make_async_copy(
                    gate_ref.at[:, pl.ds(step * tile, tile)], gates.at[slot], sems.at[slot, 0]
                ),
                pltpu.make_async_copy(
                    gate_ref.at[:, pl.ds(units + step * tile, tile)],
                    ups.at[slot],
                    sems.at[slot, 1],
                ),
                pltpu.make_async_copy(
                    down_ref.at[pl.ds(step * tile, tile), :], downs.at[slot], sems.at[slot, 2]
                ),
            ]

        for step in range(slots):
            for one in copies(step):
                one.start()
        rows = compact(in_ref[...].reshape(blocks * PAD, width)).astype(jnp.bfloat16)
        total = jnp.zeros((count, width), jnp.float32)
        for step in range(steps):
            slot = step % slots
            gate_copy, up_copy, down_copy = copies(step)
            gate_copy.wait()
            gate = jnp.dot(rows, gates[slot], preferred_element_type=jnp.float32)
            up_copy.wait()
            up = jnp.dot(rows, ups[slot], preferred_element_type=jnp.float32)
            active = (gate / (1.0 + jnp.exp(-gate)) * up).astype(jnp.bfloat16)
            down_copy.wait()
            total = total + jnp.dot(active, downs[slot], preferred_element_type=jnp.float32)
            if step + slots < steps:
                for one in copies(step + slots):
                    one.start()
        out_ref[...] = (
            spread(total.astype(jnp.bfloat16)).astype(jnp.bfloat16).reshape(blocks, PAD, width)
        )

    return pl.pallas_call(
        body,
        in_specs=[whole_spec(), any_spec(), any_spec()],
        out_specs=whole_spec(),
        out_shape=jax.ShapeDtypeStruct(arrived.shape, jnp.bfloat16),
        scratch_shapes=[
            pltpu.VMEM((slots, width, tile), jnp.bfloat16),
            pltpu.VMEM((slots, width, tile), jnp.bfloat16),
            pltpu.VMEM((slots, tile, width), jnp.bfloat16),
            pltpu.SemaphoreType.DMA((slots, 3)),
        ],
        compiler_params=pltpu.CompilerParams(vmem_limit_bytes=32 << 20),
        name="feedforward",
    )(arrived, *in_hbm(gate_piece, down_piece))


def local_heads(
    activations,
    cache_entries,
    cache_lengths,
    attention_gain,
    feedforward_gain,
    key_value_weight,
    attention_router,
    attention_routes,
    query_weight,
    output_weight,
    feedforward_router,
    feedforward_routes,
    gate_up,
    down_weight,
):
    tok_count = lax.axis_size("tok")
    req_count = lax.axis_size("req")
    tok_index = lax.axis_index("tok")
    req_index = lax.axis_index("req")
    query_rows, width = activations.shape[1:]

    attn_routes = attention_routes[0].T
    ffn_routes = feedforward_routes[0].T
    place = jnp.stack([cache_lengths[0], req_index, tok_index])
    message, attn_weights = prepare(
        activations[0], attention_gain, attention_router.T, attn_routes, place, tok_count
    )
    arrived = swap_all(message, "tok")
    own_block, near, *turned, weight_held = cache_split(
        cache_entries[0], key_value_weight, place, attn_weights
    )
    turned = [
        permute(turned[turn - 1], "tok", [(one, one ^ (2 * turn)) for one in range(tok_count)])
        for turn in range(1, 4)
    ]
    pair = [(one, one ^ 1) for one in range(tok_count)]
    sibling = permute(key_value_weight, "tok", pair)
    mine = own_tokens(arrived, [sibling]+turned[:1], tok_count, width)
    tokens = [mine] + [
        permute(mine, "req", [(one, one ^ turn) for one in range(req_count)])
        for turn in range(1, req_count)
    ]
    parts = key_value_parts(tokens, weight_held, sibling, place, turned)
    projected = query_project(arrived, query_weight[0], parts[:1], tok_count)
    parts = [parts[0]] + [
        permute(parts[turn], "tok", [(one, one ^ (2 * turn)) for one in range(tok_count)])
        for turn in range(1, 4)
    ]
    projected, *gate = lax.optimization_barrier((projected, *parts[1:], *turned))
    parts[1:], turned = gate[:3], gate[3:]
    sums = key_value_sum(parts, place, projected)
    queries = swap_all(projected, "tok")
    relayed = permute(cache_relay(near, turned), "tok", pair)
    fresh_blocks = []
    for turn in range(4):
        pairs = []
        for one in range(req_count * tok_count):
            r, t = one // tok_count, one % tok_count
            dest = ((r // 2) * 2 + t % 2) ^ turn
            pairs.append((one, dest * tok_count + 4 * (r % 2) + t // 2))
        fresh_blocks.append(permute(sums[turn], ("req", "tok"), pairs))
    attended = attention(queries, place, fresh_blocks, own_block, turned, relayed)
    attended = swap_all(attended, "tok")
    parts_out, new_keys_values = output_project(attended, output_weight[0], query_rows)
    output_back = swap_all(parts_out, "tok")
    ffn_send, mixed_rows, ffn_weights = middle(
        activations[0],
        output_back,
        attn_weights,
        feedforward_gain,
        feedforward_router.T,
        ffn_routes,
    )
    received = swap_all(ffn_send, "tok")
    expert_parts = feedforward(received, gate_up[0], down_weight[0])
    expert_back = swap_all(expert_parts, "tok")
    layer_output = finish(mixed_rows, expert_back, ffn_weights)
    return (layer_output[None], new_keys_values[None])


def solution(mesh):
    placed = (
        P("req", "tok", None),
        P("req", "tok", None),
        P("req"),
        P(),
        P(),
        P("tok", "req"),
        P(),
        P("req", "tok", None),
        P("tok", None, None),
        P("tok", None, None),
        P(),
        P("req", "tok", None),
        P("tok", None, None),
        P("tok", None, None),
    )
    sizes = dict(mesh.shape)
    by_heads = sizes["tok"] == 8 and sizes["req"] == 4
    return jax.shard_map(
        local_heads if by_heads else local,
        mesh=mesh,
        in_specs=placed,
        out_specs=(P("req", "tok", None), P("req", "tok", None)),
        check_vma=False,
    )
```

```python
import math

import jax
import jax.numpy as jnp
from jax import lax
from jax.experimental import pallas as pl
from jax.experimental.pallas import tpu as pltpu
from jax.sharding import PartitionSpec as P

HEADS = 16
HEAD_DIM = 128
CAP = 6


def normed(values, gain):
    scale_rows = lax.rsqrt(jnp.mean(values * values, axis=-1, keepdims=True) + 1e-06)
    return values * scale_rows * gain


def slot_matrix(routes, experts, capacity):
    row_count, top_count = routes.shape
    labels = jnp.arange(experts, dtype=jnp.int32)
    onehot = (routes.reshape(row_count * top_count, 1) == labels[None, :]).astype(jnp.int32)
    before = jnp.cumsum(onehot, axis=0) - onehot
    within = jnp.sum(before * onehot, axis=1)
    placed = routes.reshape(row_count * top_count) * capacity + within
    columns = jnp.arange(experts * capacity, dtype=jnp.int32)
    return (placed[:, None] == columns[None, :]).astype(jnp.float32)


def router_gates(hidden, router, routes):
    logits = jnp.dot(hidden, router, preferred_element_type=jnp.float32)
    picked = jnp.take_along_axis(logits, routes, axis=1)
    return jax.nn.sigmoid(2.0 * picked - jnp.sum(picked, axis=1, keepdims=True))


def token_matrices(pair_slots, gates, top_count):
    row_count = gates.shape[0]
    per_token = pair_slots.reshape(row_count, top_count, -1)
    picked = jnp.sum(per_token, axis=1)
    weighted = jnp.sum(per_token * gates[:, :, None], axis=1)
    return (picked, weighted)


def spread_slots(slot_rows, experts, groups, capacity):
    feat_width = slot_rows.shape[-1]
    shaped = slot_rows.reshape(experts, 1, capacity, feat_width)
    return jnp.broadcast_to(shaped, (experts, groups, capacity, feat_width)).reshape(
        experts * groups, capacity, feat_width
    )


def head_groups(rows, experts, groups, group_width):
    row_count = rows.shape[0]
    shaped = (
        rows.reshape(row_count, 2, groups, group_width)
        .transpose(2, 0, 1, 3)
        .reshape(groups, row_count, 2 * group_width)
    )
    return jnp.broadcast_to(shaped[None], (experts, groups, row_count, 2 * group_width)).reshape(
        experts * groups, row_count, 2 * group_width
    )


def group_sum(received, experts, groups, capacity):
    feat_width = received.shape[-1]
    summed = jnp.sum(
        received.reshape(experts, groups, capacity, feat_width).astype(jnp.float32), axis=1
    )
    return summed.reshape(experts * capacity, feat_width)


def expert_feedforward(received, gate_piece, down_piece):
    units = down_piece.shape[0]
    projected = jnp.einsum("scd,df->scf", received, gate_piece, preferred_element_type=jnp.float32)
    active = (jax.nn.silu(projected[..., :units]) * projected[..., units:]).astype(jnp.bfloat16)
    return jnp.einsum("scf,fd->scd", active, down_piece, preferred_element_type=jnp.float32).astype(
        jnp.bfloat16
    )


def local(
    activations,
    cache_entries,
    cache_lengths,
    attention_gain,
    feedforward_gain,
    key_value_weight,
    attention_router,
    attention_routes,
    query_weight,
    output_weight,
    feedforward_router,
    feedforward_routes,
    gate_up,
    down_weight,
):
    tok_count = lax.axis_size("tok")
    tok_index = lax.axis_index("tok")
    experts = attention_router.shape[1]
    groups = tok_count // experts
    query_rows = activations.shape[1]
    cache_rows = cache_entries.shape[1]
    top_count = attention_routes.shape[2]
    model_width = activations.shape[2]
    head_count = HEADS // groups
    group_width = head_count * HEAD_DIM
    block_span = cache_rows + query_rows
    score_scale = 1.0 / math.sqrt(HEAD_DIM)
    cache_part = cache_entries[0]
    residual_in = activations[0].astype(jnp.float32)
    hidden = normed(residual_in, attention_gain).astype(jnp.bfloat16)
    stacked = lax.all_gather(hidden, "req", axis=0, tiled=True)
    projected_part = jnp.dot(
        stacked,
        lax.all_gather(key_value_weight, "tok", axis=0, tiled=True),
        preferred_element_type=jnp.float32,
    )
    new_keys_values = lax.all_to_all(
        projected_part.astype(jnp.bfloat16), "req", split_axis=0, concat_axis=1, tiled=True
    )
    combined = jnp.concatenate([cache_part, new_keys_values], axis=0)
    group_keys = lax.all_to_all(
        head_groups(combined, experts, groups, group_width),
        "tok",
        split_axis=0,
        concat_axis=0,
        tiled=True,
    )
    attn_routes = attention_routes[0]
    attn_pairs = slot_matrix(attn_routes, experts, CAP)
    attn_gate = router_gates(hidden, attention_router, attn_routes)
    attn_pick, attn_weights = token_matrices(attn_pairs, attn_gate, top_count)
    slot_inputs = jnp.dot(
        attn_pick.T.astype(jnp.bfloat16), hidden, preferred_element_type=jnp.float32
    ).astype(jnp.bfloat16)
    token_place = tok_index * query_rows + jnp.arange(query_rows, dtype=jnp.int32)
    slot_place = jnp.sum(attn_pick.astype(jnp.int32) * token_place[:, None], axis=0)
    query_send = spread_slots(slot_inputs, experts, groups, CAP)
    place_send = jnp.broadcast_to(
        slot_place.reshape(experts, 1, CAP), (experts, groups, CAP)
    ).reshape(tok_count, CAP)
    length = cache_lengths[0]
    source = jnp.arange(tok_count, dtype=jnp.int32).reshape(groups, experts, 1)
    offset = jnp.arange(block_span, dtype=jnp.int32).reshape(1, 1, block_span)
    turn_shape = (groups, experts * block_span)
    cached = jnp.broadcast_to(offset < cache_rows, (groups, experts, block_span)).reshape(
        turn_shape
    )
    cache_usable = (source * cache_rows + offset < length).reshape(turn_shape)
    fresh_place = (source * query_rows + offset - cache_rows).reshape(turn_shape)
    key_turns = group_keys.reshape(groups, experts * block_span, 2, head_count, HEAD_DIM)
    slot_rows = lax.all_to_all(query_send, "tok", split_axis=0, concat_axis=0, tiled=True)
    slot_places = lax.all_to_all(place_send, "tok", split_axis=0, concat_axis=0, tiled=True)
    items = slot_rows.shape[1]
    query_three = (
        jnp.einsum("scd,df->scf", slot_rows, query_weight[0], preferred_element_type=jnp.float32)
        .astype(jnp.bfloat16)
        .reshape(tok_count * items, head_count, HEAD_DIM)
    )
    query_place = slot_places.reshape(tok_count * items)

    def one_turn(state_in, turn_data):
        row_max, row_sums, weighted = state_in
        keys_values, cached_turn, usable_turn, place_turn = turn_data
        usable = jnp.where(
            cached_turn[None, :], usable_turn[None, :], place_turn[None, :] <= query_place[:, None]
        )[None]
        scores = (
            jnp.einsum(
                "phd,khd->hpk", query_three, keys_values[:, 0], preferred_element_type=jnp.float32
            )
            * score_scale
        )
        scores = jnp.where(usable, scores, -1e30)
        new_max = jnp.maximum(row_max, jnp.max(scores, axis=-1))
        weights = jnp.where(usable, jnp.exp(scores - new_max[..., None]), 0.0).astype(jnp.bfloat16)
        factor = jnp.exp(row_max - new_max)
        row_sums = row_sums * factor + jnp.sum(weights.astype(jnp.float32), axis=-1)
        weighted = weighted * factor[..., None] + jnp.einsum(
            "hpk,khd->hpd", weights, keys_values[:, 1], preferred_element_type=jnp.float32
        )
        return ((new_max, row_sums, weighted), None)

    query_total = tok_count * items
    initial = (
        jnp.full((head_count, query_total), -1e30, jnp.float32),
        jnp.zeros((head_count, query_total), jnp.float32),
        jnp.zeros((head_count, query_total, HEAD_DIM), jnp.float32),
    )
    final_state, _ = lax.scan(one_turn, initial, (key_turns, cached, cache_usable, fresh_place))
    row_max, row_sums, weighted = final_state
    attended = (
        (weighted / row_sums[..., None])
        .astype(jnp.bfloat16)
        .transpose(1, 0, 2)
        .reshape(tok_count, items, group_width)
    )
    parts = jnp.einsum(
        "scf,fd->scd", attended, output_weight[0], preferred_element_type=jnp.float32
    ).astype(jnp.bfloat16)
    output_back = lax.all_to_all(parts, "tok", split_axis=0, concat_axis=0, tiled=True)
    output_sums = group_sum(output_back, experts, groups, CAP)
    mixed_rows = (
        residual_in + jnp.dot(attn_weights, output_sums, precision=lax.Precision.HIGHEST)
    ).astype(jnp.bfloat16)
    hidden_two = normed(mixed_rows.astype(jnp.float32), feedforward_gain).astype(jnp.bfloat16)
    ffn_routes = feedforward_routes[0]
    ffn_pairs = slot_matrix(ffn_routes, experts, CAP)
    ffn_gate = router_gates(hidden_two, feedforward_router, ffn_routes)
    ffn_pick, ffn_weights = token_matrices(ffn_pairs, ffn_gate, top_count)
    every_rows, every_routes = (
        lax.all_gather(hidden_two, "tok", axis=0, tiled=True),
        lax.all_gather(ffn_routes, "tok", axis=0, tiled=True),
    )
    routes_all = every_routes.reshape(tok_count, query_rows, top_count)

    def source_slots(routes_block):
        return slot_matrix(routes_block, experts, CAP)

    per_source = jax.vmap(source_slots)(routes_all)
    per_token = jnp.sum(per_source.reshape(tok_count, query_rows, top_count, experts, CAP), axis=2)
    expert_mask = (jnp.arange(experts, dtype=jnp.int32) == tok_index // groups).astype(jnp.float32)
    picked = jnp.einsum("sqec,e->sqc", per_token, expert_mask)
    received = jnp.einsum(
        "sqc,sqd->scd",
        picked.astype(jnp.bfloat16),
        every_rows.reshape(tok_count, query_rows, model_width),
        preferred_element_type=jnp.float32,
    ).astype(jnp.bfloat16)
    expert_parts = expert_feedforward(received, gate_up[0], down_weight[0])
    expert_back = lax.all_to_all(expert_parts, "tok", split_axis=0, concat_axis=0, tiled=True)
    expert_sums = group_sum(expert_back, experts, groups, CAP)
    layer_output = (
        mixed_rows.astype(jnp.float32)
        + jnp.dot(ffn_weights, expert_sums, precision=lax.Precision.HIGHEST)
    ).astype(jnp.bfloat16)
    return (layer_output[None], new_keys_values[None])


PAD = 8
LANES = 128
FF_TILE = 512


def column_stream(source, buffers, sems, tile):
    return [
        pltpu.make_async_copy(
            source.at[:, pl.ds(step * tile, tile)], buffers.at[step], sems.at[step]
        )
        for step in range(buffers.shape[0])
    ]


def permute(values, axis, pairs):
    return lax.ppermute(values, axis, pairs)


def swap_all(values, axis):
    return lax.all_to_all(values, axis, split_axis=0, concat_axis=0, tiled=True)


def whole_spec():
    return pl.BlockSpec(memory_space=pltpu.VMEM)


def index_spec():
    return pl.BlockSpec(memory_space=pltpu.SMEM)


def iota(shape, axis):
    return lax.broadcasted_iota(jnp.int32, shape, axis)


def any_spec():
    return pl.BlockSpec(memory_space=pl.ANY)


def in_hbm(*arrays):
    return [pltpu.with_memory_space_constraint(one, pltpu.HBM) for one in arrays]


def in_vmem(*arrays):
    return [pltpu.with_memory_space_constraint(one, pltpu.VMEM) for one in arrays]


def load_all(pairs, sems):
    copies = [
        pltpu.make_async_copy(source, target, sems.at[number])
        for number, (source, target) in enumerate(pairs)
    ]
    for one in copies:
        one.start()
    for one in copies:
        one.wait()


def padded_picks(routes, experts):
    row_count = routes.shape[1]
    row = iota((experts * PAD, row_count), 0)
    expert, slot = row // PAD, row % PAD
    first, second = routes[0:1, :] == expert, routes[1:2, :] == expert
    named = jnp.where(first, 1.0, 0.0) + jnp.where(second, 1.0, 0.0)
    earlier = (iota((row_count, row_count), 0) < iota((row_count, row_count), 1)).astype(
        jnp.bfloat16
    )
    before = jnp.dot(
        named.astype(jnp.bfloat16), earlier, preferred_element_type=jnp.float32
    ).astype(jnp.int32)
    here = (before == slot) & (slot < CAP)
    return named * here.astype(jnp.float32), first


def gate_weights(hidden, router, routes, picks, first):
    logits = lax.dot_general(
        router, hidden, (((1,), (1,)), ((), ())), preferred_element_type=jnp.float32
    )
    label = iota(logits.shape, 0)
    one = jnp.sum(jnp.where(routes[0:1, :] == label, logits, 0.0), axis=0, keepdims=True)
    two = jnp.sum(jnp.where(routes[1:2, :] == label, logits, 0.0), axis=0, keepdims=True)
    gate_one = 1.0 / (1.0 + jnp.exp(two - one))
    gate_two = 1.0 / (1.0 + jnp.exp(one - two))
    return picks * jnp.where(first, gate_one, gate_two)


def row_norm(values, gain):
    mean = jnp.mean(values * values, axis=-1, keepdims=True)
    return (values * lax.rsqrt(mean + 1e-06) * gain).astype(jnp.bfloat16)


def pick_rows(picks, rows):
    return jnp.dot(picks.astype(jnp.bfloat16), rows, preferred_element_type=jnp.float32)


def compact(rows):
    count = rows.shape[0] // PAD * CAP
    one, two = iota((count, rows.shape[0]), 0), iota((count, rows.shape[0]), 1)
    chosen = ((one // CAP) * PAD + one % CAP == two).astype(jnp.bfloat16)
    return jnp.dot(chosen, rows, preferred_element_type=jnp.float32)


def spread(rows):
    count = rows.shape[0] // CAP * PAD
    one, two = iota((count, rows.shape[0]), 0), iota((count, rows.shape[0]), 1)
    chosen = ((two // CAP) * PAD + two % CAP == one).astype(jnp.bfloat16)
    return jnp.dot(chosen, rows, preferred_element_type=jnp.float32)


def exact_mix(weights, rows):
    high = weights.astype(jnp.bfloat16)
    rest = weights - high.astype(jnp.float32)
    middle = rest.astype(jnp.bfloat16)
    low = (rest - middle.astype(jnp.float32)).astype(jnp.bfloat16)
    count = weights.shape[1]
    stacked = lax.dot_general(
        jnp.concatenate([high, middle, low], axis=1),
        rows,
        (((0,), (0,)), ((), ())),
        preferred_element_type=jnp.float32,
    )
    return stacked[:count] + (stacked[count : 2 * count] + stacked[2 * count :])


def prepare(activations, gain, router, routes, tok_count):
    rows, width = activations.shape
    experts = router.shape[0]
    span = width // tok_count
    half = rows // 2
    per_row = width // (2 * span)

    def body(
        act_in, gain_in, router_in, route_in, out_ref, weight_ref,
        act_ref, gain_ref, router_ref, route_ref, wide, copy, sems,
    ):
        load_all(
            [
                (act_in, act_ref),
                (gain_in, gain_ref),
                (router_in, router_ref),
                (route_in, route_ref),
            ],
            sems,
        )
        route = route_ref[...]
        hidden = row_norm(act_ref[...].astype(jnp.float32), gain_ref[...])
        picks, first = padded_picks(route, experts)
        wide[...] = pick_rows(picks, hidden)
        copy[...] = hidden.astype(jnp.float32)
        for dest in range(tok_count):
            chip, core = dest // 2, dest % 2
            for place in range(half):
                row = dest * PAD + CAP + place // per_row
                for side in range(2):
                    column = (place % per_row) * 2 * span + side * span
                    source = (2 * chip + (core ^ side)) * span
                    wide[row : row + 1, column : column + span] = copy[
                        core * half + place : core * half + place + 1, source : source + span
                    ]
        out_ref[:, :, :width] = wide[...].astype(jnp.bfloat16).reshape(tok_count, PAD, width)
        number = iota((rows, LANES), 0).astype(jnp.float32).astype(jnp.bfloat16)
        out_ref[:, :, width:] = (
            pick_rows(picks, number).astype(jnp.bfloat16).reshape(tok_count, PAD, LANES)
        )
        weight_ref[...] = gate_weights(hidden, router_ref[...], route, picks, first)

    return pl.pallas_call(
        body,
        in_specs=[any_spec()] * 4,
        out_specs=[whole_spec()] * 2,
        out_shape=[
            jax.ShapeDtypeStruct((tok_count, PAD, width + LANES), jnp.bfloat16),
            jax.ShapeDtypeStruct((tok_count * PAD, rows), jnp.float32),
        ],
        scratch_shapes=[
            pltpu.VMEM((rows, width), activations.dtype),
            pltpu.VMEM((1, width), gain.dtype),
            pltpu.VMEM(router.shape, router.dtype),
            pltpu.VMEM(routes.shape, routes.dtype),
            pltpu.VMEM((tok_count * PAD, width), jnp.float32),
            pltpu.VMEM((rows, width), jnp.float32),
            pltpu.SemaphoreType.DMA((4,)),
        ],
        compiler_params=pltpu.CompilerParams(vmem_limit_bytes=4 << 20),
        name="prepare",
    )(*in_hbm(activations, gain.reshape(1, width), router, routes))


def cache_split(cache_part, side, place, after):
    rows, width = cache_part.shape
    count = 8
    span = width // 2 // count

    def body(index_ref, cache_ref, side_ref, after_ref, *refs):
        outs, side_out, sems = refs[:5], refs[5], refs[6]
        pairs = []
        for number in range(count):
            turn, side = number // 2, number % 2
            out, base = (outs[turn + 1], side * rows) if turn else (outs[side], 0)
            start = pl.multiple_of((index_ref[2] ^ number) * span, span)
            for kind in range(2):
                pairs.append(
                    (
                        cache_ref.at[:, pl.ds(kind * (width // 2) + start, span)],
                        out.at[base : base + rows, kind * span : (kind + 1) * span],
                    )
                )
        pairs.append((side_ref, side_out))
        load_all(pairs, sems)

    shapes = [(rows, 2 * span)] * 2 + [(2 * rows, 2 * span)] * 3
    return pl.pallas_call(
        body,
        in_specs=[index_spec()] + [any_spec()] * 3,
        out_specs=[whole_spec()] * 6,
        out_shape=[jax.ShapeDtypeStruct(one, cache_part.dtype) for one in shapes]
        + [pltpu.VMEM(side.shape, side.dtype)],
        scratch_shapes=[pltpu.SemaphoreType.DMA((2 * count + 1,))],
        compiler_params=pltpu.CompilerParams(vmem_limit_bytes=4 << 20),
        name="cache_split",
    )(place, *in_hbm(cache_part, side), after)


def cache_relay(near, turned):
    rows, width = near.shape

    def body(near_ref, *refs):
        out_ref = refs[-1]
        out_ref[:rows, :] = near_ref[...]
        for turn in range(1, 4):
            out_ref[turn * rows : (turn + 1) * rows, :] = refs[turn - 1][rows:, :]

    return pl.pallas_call(
        body,
        in_specs=[whole_spec()] * 4,
        out_specs=whole_spec(),
        out_shape=jax.ShapeDtypeStruct((4 * rows, width), near.dtype),
        compiler_params=pltpu.CompilerParams(vmem_limit_bytes=3 << 20),
        name="cache_relay",
    )(near, *turned)


def own_tokens(arrived, after, tok_count, width):
    span = width // tok_count
    per_row = width // (2 * span)
    extra = PAD - CAP

    def body(in_ref, *rest):
        out_ref, wide = rest[len(after) :]
        for source in range(tok_count):
            rows = in_ref[source, :, :width].astype(jnp.float32)
            for part in range(extra):
                for place in range(per_row):
                    row = source * extra * per_row + part * per_row + place
                    wide[row : row + 1, :] = rows[
                        CAP + part : CAP + part + 1, place * 2 * span : (place + 1) * 2 * span
                    ]
        out_ref[...] = wide[...].astype(jnp.bfloat16)

    count = tok_count * extra * per_row
    return pl.pallas_call(
        body,
        in_specs=[whole_spec()] + [any_spec()] * len(after),
        out_specs=whole_spec(),
        out_shape=jax.ShapeDtypeStruct((count, 2 * span), jnp.bfloat16),
        scratch_shapes=[pltpu.VMEM((count, 2 * span), jnp.float32)],
        compiler_params=pltpu.CompilerParams(vmem_limit_bytes=4 << 20),
        name="own_tokens",
    )(arrived, *after)


def query_project(arrived, weight, after, tok_count):
    width = weight.shape[0]
    span = width // tok_count
    slots = tok_count * CAP
    height = slots + PAD
    tile = 2 * span
    steps = width // tile

    def body(in_ref, weight_ref, *rest):
        out_ref, held, sems = rest[len(after) :]
        copies = column_stream(weight_ref, held, sems, tile)
        for one in copies:
            one.start()
        every = compact(in_ref[...].reshape(tok_count * PAD, width + LANES))
        rows = every[:, :width].astype(jnp.bfloat16)
        local = every[:, width : width + LANES]
        mine = iota(local.shape, 0)
        placed = local + ((mine // CAP) * (2 * PAD)).astype(jnp.float32)
        placed = jnp.where(mine == iota(local.shape, 1), placed, 0.0)
        line = jnp.broadcast_to(jnp.sum(placed, axis=0, keepdims=True), (PAD, LANES))
        line = jnp.concatenate([line] * (span // LANES), axis=1).astype(jnp.bfloat16)
        for step in range(steps):
            copies[step].wait()
            query = jnp.dot(rows, held[step], preferred_element_type=jnp.float32).astype(
                jnp.bfloat16
            )
            for one in range(tile // span):
                place = step * (tile // span) + one
                out_ref[place, :slots, :] = query[:, one * span : (one + 1) * span]
                out_ref[place, slots:, :] = line
    return pl.pallas_call(
        body,
        in_specs=[whole_spec(), any_spec()] + [any_spec()] * len(after),
        out_specs=whole_spec(),
        out_shape=jax.ShapeDtypeStruct((tok_count, height, span), jnp.bfloat16),
        scratch_shapes=[
            pltpu.VMEM((steps, width, tile), jnp.bfloat16),
            pltpu.SemaphoreType.DMA((steps,)),
        ],
        compiler_params=pltpu.CompilerParams(vmem_limit_bytes=14 << 20),
        cost_estimate=pl.CostEstimate(flops=0, transcendentals=0, bytes_accessed=40 << 20),
        name="query_project",
    )(arrived, *in_hbm(weight), *after)


def key_value_parts(tokens, weight, sibling, place, after):
    rows, depth = tokens[0].shape
    half = depth // 2
    quarter = weight.shape[1] // 4
    count = len(tokens)

    def body(place_ref, *refs):
        token_refs, weight_ref, sibling_ref = refs[:count], refs[count], refs[count + 1]
        outs = refs[count + 2 + len(after) :]
        stacked = jnp.concatenate([one[...] for one in token_refs], axis=0)
        for turn in range(4):
            start = pl.multiple_of(((place_ref[2] // 2) ^ turn) * quarter, quarter)
            part = jnp.dot(
                stacked[:, :half],
                weight_ref[:, pl.ds(start, quarter)],
                preferred_element_type=jnp.float32,
            ) + jnp.dot(
                stacked[:, half:],
                sibling_ref[:, pl.ds(start, quarter)],
                preferred_element_type=jnp.float32,
            )
            outs[turn][...] = part.astype(outs[turn].dtype)

    shapes = [
        jax.ShapeDtypeStruct((count * rows, quarter), jnp.float32 if turn == 0 else jnp.bfloat16)
        for turn in range(4)
    ]
    return pl.pallas_call(
        body,
        in_specs=[index_spec()] + [whole_spec()] * (count + 2) + [any_spec()] * len(after),
        out_specs=[whole_spec()] * 4,
        out_shape=shapes,
        compiler_params=pltpu.CompilerParams(vmem_limit_bytes=8 << 20),
        name="key_value_parts",
    )(place, *tokens, weight, sibling, *after)


def key_value_sum(parts, place, after):
    rows, quarter = parts[0].shape
    block = rows // 4

    def body(place_ref, *refs):
        ins, outs = refs[:4], refs[5:]
        req = place_ref[1]
        source = (req // 2) * 2 + place_ref[2] % 2
        for turn in range(4):
            start = pl.multiple_of((req ^ source ^ turn) * block, block)
            total = ins[0][pl.ds(start, block), :]
            for one in ins[1:]:
                total = total + one[pl.ds(start, block), :].astype(jnp.float32)
            outs[turn][...] = total.astype(jnp.bfloat16)

    return pl.pallas_call(
        body,
        in_specs=[index_spec()] + [whole_spec()] * 4 + [any_spec()],
        out_specs=[whole_spec()] * 4,
        out_shape=[jax.ShapeDtypeStruct((block, quarter), jnp.bfloat16)] * 4,
        compiler_params=pltpu.CompilerParams(vmem_limit_bytes=4 << 20),
        name="key_value_sum",
    )(place, *parts, after)


def attention(message, scalars, fresh_blocks, own, turned, relayed):
    blocks, _, span = message.shape
    heads = span // HEAD_DIM
    slots = blocks * CAP
    fresh_rows = fresh_blocks[0].shape[0]
    half = fresh_rows // blocks
    cache_rows = own.shape[0]
    scale = 1.0 / math.sqrt(HEAD_DIM)
    contract = (((1,), (1,)), ((), ()))

    def body(scalar_ref, in_ref, *refs):
        fresh_refs, own_ref, turned_refs, relay_ref = refs[:4], refs[4], refs[5:8], refs[8]
        out_ref = refs[9]
        limit, req, tok = scalar_ref[0], scalar_ref[1], scalar_ref[2]
        pieces = []
        for source in range(4):
            picked = fresh_refs[3][...]
            for turn in range(3):
                picked = jnp.where((req ^ source) == turn, fresh_refs[turn][...], picked)
            pieces.append(picked)
        new_keys = jnp.concatenate(pieces[:2], axis=0)
        new_values = jnp.concatenate(pieces[2:], axis=0)
        key_row = iota((1, blocks * cache_rows), 1)
        key_block = key_row // cache_rows
        key_source = ((key_block % 4) * 2 + key_block // 4) ^ tok
        cache_usable = key_source * cache_rows + key_row % cache_rows < limit
        new_row = iota((1, 2 * fresh_rows), 1)
        within = new_row % fresh_rows
        new_place = (within // half) * (2 * half) + (new_row // fresh_rows) * half + within % half
        places = []
        for expert in range(blocks):
            line = in_ref[expert, slots:, :LANES].astype(jnp.float32)[0:1]
            chosen = iota((slots, LANES), 0) == iota((slots, LANES), 1)
            places.append(jnp.sum(jnp.where(chosen, line, 0.0), axis=1, keepdims=True))
        new_usable = new_place <= jnp.concatenate(places, axis=0).astype(jnp.int32)
        flat = in_ref[:, :slots, :].reshape(blocks * slots, span)
        cached = [own_ref] + [one.at[:cache_rows] for one in turned_refs] + [relay_ref]
        keys = jnp.concatenate([one[:, :span] for one in cached], axis=0)
        values = jnp.concatenate([one[:, span:] for one in cached], axis=0)
        for head in range(heads):
            cols = slice(head * HEAD_DIM, (head + 1) * HEAD_DIM)
            query = flat[:, cols]
            first = lax.dot_general(
                query, keys[:, cols], contract, preferred_element_type=jnp.float32
            )
            second = lax.dot_general(
                query, new_keys[:, cols], contract, preferred_element_type=jnp.float32
            )
            first = jnp.where(cache_usable, first * scale, -1e30)
            second = jnp.where(new_usable, second * scale, -1e30)
            top = jnp.maximum(
                jnp.max(first, axis=-1, keepdims=True), jnp.max(second, axis=-1, keepdims=True)
            )
            first = jnp.exp(first - top).astype(jnp.bfloat16)
            second = jnp.exp(second - top).astype(jnp.bfloat16)
            sums = jnp.sum(first.astype(jnp.float32), axis=-1, keepdims=True) + jnp.sum(
                second.astype(jnp.float32), axis=-1, keepdims=True
            )
            mixed = jnp.dot(first, values[:, cols], preferred_element_type=jnp.float32) + jnp.dot(
                second, new_values[:, cols], preferred_element_type=jnp.float32
            )
            out_ref[:, :slots, cols] = (
                (mixed / sums).astype(jnp.bfloat16).reshape(blocks, slots, HEAD_DIM)
            )
        for kind in range(2):
            for part in range(2):
                start = slots + kind * 2 * half + part * half
                out_ref[:, start : start + half, :] = pieces[2 * kind + part].reshape(
                    blocks, half, span
                )

    return pl.pallas_call(
        body,
        in_specs=[index_spec()] + [whole_spec()] * 10,
        out_specs=whole_spec(),
        out_shape=jax.ShapeDtypeStruct((blocks, slots + 4 * half, span), jnp.bfloat16),
        compiler_params=pltpu.CompilerParams(vmem_limit_bytes=14 << 20),
        name="attention",
    )(scalars, message, *fresh_blocks, own, *turned, relayed)


def output_project(arrived, weight, query_rows):
    blocks, height, span = arrived.shape
    slots = blocks * CAP
    width = weight.shape[1]
    tile = width // 4

    def body(in_ref, weight_ref, out_ref, fresh_ref, held, sems):
        copies = column_stream(weight_ref, held, sems, tile)
        for one in copies:
            one.start()
        rows = []
        for block in range(blocks):
            cols = slice(block * span, (block + 1) * span)
            rows.append(spread(in_ref[block, :slots, :]).astype(jnp.bfloat16))
            fresh_ref[:, cols] = in_ref[block, slots : slots + query_rows, :]
            fresh_ref[:, block * span + width : (block + 1) * span + width] = in_ref[
                block, slots + query_rows :, :
            ]
        rows = jnp.concatenate(rows, axis=1)
        for step in range(width // tile):
            cols = slice(step * tile, (step + 1) * tile)
            copies[step].wait()
            part = jnp.dot(rows, held[step], preferred_element_type=jnp.float32)
            out_ref[:, :, cols] = part.astype(jnp.bfloat16).reshape(blocks, PAD, tile)

    return pl.pallas_call(
        body,
        in_specs=[whole_spec(), any_spec()],
        out_specs=[whole_spec()] * 2,
        out_shape=[
            jax.ShapeDtypeStruct((blocks, PAD, width), jnp.bfloat16),
            jax.ShapeDtypeStruct((query_rows, 2 * width), jnp.bfloat16),
        ],
        scratch_shapes=[
            pltpu.VMEM((width // tile, blocks * span, tile), jnp.bfloat16),
            pltpu.SemaphoreType.DMA((width // tile,)),
        ],
        compiler_params=pltpu.CompilerParams(vmem_limit_bytes=14 << 20),
        name="output_project",
    )(arrived, *in_hbm(weight))


def middle(activations, arrived, weights, gain, router, routes):
    rows, width = activations.shape
    blocks = arrived.shape[0]
    experts = router.shape[0]

    def body(act_ref, in_ref, old_ref, gain_ref, router_ref, route_ref, out_ref, mix_ref, new_ref):
        route = route_ref[...]
        added = exact_mix(old_ref[...], in_ref[...].reshape(blocks * PAD, width))
        mixed = (act_ref[...].astype(jnp.float32) + added).astype(jnp.bfloat16)
        mix_ref[...] = mixed
        hidden = row_norm(mixed.astype(jnp.float32), gain_ref[...])
        picks, first = padded_picks(route, experts)
        out_ref[...] = (
            pick_rows(picks, hidden).astype(jnp.bfloat16).reshape(blocks, PAD, width)
        )
        new_ref[...] = gate_weights(hidden, router_ref[...], route, picks, first)

    return pl.pallas_call(
        body,
        in_specs=[whole_spec()] * 6,
        out_specs=[whole_spec()] * 3,
        out_shape=[
            jax.ShapeDtypeStruct((blocks, PAD, width), jnp.bfloat16),
            jax.ShapeDtypeStruct((rows, width), jnp.bfloat16),
            jax.ShapeDtypeStruct((blocks * PAD, rows), jnp.float32),
        ],
        compiler_params=pltpu.CompilerParams(vmem_limit_bytes=4 << 20),
        name="middle",
    )(activations, arrived, weights, gain.reshape(1, width), router, routes)


def finish(mixed, arrived, weights):
    rows, width = mixed.shape

    def body(mix_ref, in_ref, weight_ref, out_ref):
        added = exact_mix(weight_ref[...], in_ref[...].reshape(-1, width))
        out_ref[...] = (mix_ref[...].astype(jnp.float32) + added).astype(jnp.bfloat16)

    return pl.pallas_call(
        body,
        in_specs=[whole_spec()] * 3,
        out_specs=whole_spec(),
        out_shape=jax.ShapeDtypeStruct((rows, width), jnp.bfloat16),
        compiler_params=pltpu.CompilerParams(vmem_limit_bytes=4 << 20),
        name="finish",
    )(mixed, arrived, weights)


def feedforward(arrived, gate_piece, down_piece):
    blocks, _, width = arrived.shape
    count = blocks * CAP
    units = down_piece.shape[0]
    tile = FF_TILE
    steps = units // tile
    slots = 4

    def body(in_ref, gate_ref, down_ref, out_ref, gates, ups, downs, sems):
        def copies(step):
            slot = step % slots
            return [
                pltpu.make_async_copy(
                    gate_ref.at[:, pl.ds(step * tile, tile)], gates.at[slot], sems.at[slot, 0]
                ),
                pltpu.make_async_copy(
                    gate_ref.at[:, pl.ds(units + step * tile, tile)],
                    ups.at[slot],
                    sems.at[slot, 1],
                ),
                pltpu.make_async_copy(
                    down_ref.at[pl.ds(step * tile, tile), :], downs.at[slot], sems.at[slot, 2]
                ),
            ]

        for step in range(slots):
            for one in copies(step):
                one.start()
        rows = compact(in_ref[...].reshape(blocks * PAD, width)).astype(jnp.bfloat16)
        total = jnp.zeros((count, width), jnp.float32)
        for step in range(steps):
            slot = step % slots
            gate_copy, up_copy, down_copy = copies(step)
            gate_copy.wait()
            gate = jnp.dot(rows, gates[slot], preferred_element_type=jnp.float32)
            up_copy.wait()
            up = jnp.dot(rows, ups[slot], preferred_element_type=jnp.float32)
            active = (gate / (1.0 + jnp.exp(-gate)) * up).astype(jnp.bfloat16)
            down_copy.wait()
            total = total + jnp.dot(active, downs[slot], preferred_element_type=jnp.float32)
            if step + slots < steps:
                for one in copies(step + slots):
                    one.start()
        out_ref[...] = (
            spread(total.astype(jnp.bfloat16)).astype(jnp.bfloat16).reshape(blocks, PAD, width)
        )

    return pl.pallas_call(
        body,
        in_specs=[whole_spec(), any_spec(), any_spec()],
        out_specs=whole_spec(),
        out_shape=jax.ShapeDtypeStruct(arrived.shape, jnp.bfloat16),
        scratch_shapes=[
            pltpu.VMEM((slots, width, tile), jnp.bfloat16),
            pltpu.VMEM((slots, width, tile), jnp.bfloat16),
            pltpu.VMEM((slots, tile, width), jnp.bfloat16),
            pltpu.SemaphoreType.DMA((slots, 3)),
        ],
        compiler_params=pltpu.CompilerParams(vmem_limit_bytes=32 << 20),
        name="feedforward",
    )(arrived, *in_hbm(gate_piece, down_piece))


def local_heads(
    activations,
    cache_entries,
    cache_lengths,
    attention_gain,
    feedforward_gain,
    key_value_weight,
    attention_router,
    attention_routes,
    query_weight,
    output_weight,
    feedforward_router,
    feedforward_routes,
    gate_up,
    down_weight,
):
    tok_count = lax.axis_size("tok")
    req_count = lax.axis_size("req")
    tok_index = lax.axis_index("tok")
    req_index = lax.axis_index("req")
    query_rows, width = activations.shape[1:]

    attn_routes = attention_routes[0].T
    ffn_routes = feedforward_routes[0].T
    place = jnp.stack([cache_lengths[0], req_index, tok_index])
    message, attn_weights = prepare(
        activations[0], attention_gain, attention_router.T, attn_routes, tok_count
    )
    arrived = swap_all(message, "tok")
    own_block, near, *turned, weight_held = cache_split(
        cache_entries[0], key_value_weight, place, attn_weights
    )
    turned = [
        permute(turned[turn - 1], "tok", [(one, one ^ (2 * turn)) for one in range(tok_count)])
        for turn in range(1, 4)
    ]
    pair = [(one, one ^ 1) for one in range(tok_count)]
    sibling = permute(key_value_weight, "tok", pair)
    mine = own_tokens(arrived, [sibling], tok_count, width)
    tokens = [mine] + [
        permute(mine, "req", [(one, one ^ turn) for one in range(req_count)])
        for turn in range(1, req_count)
    ]
    parts = key_value_parts(tokens, weight_held, sibling, place, turned)
    projected = query_project(arrived, query_weight[0], parts[:1], tok_count)
    parts = [parts[0]] + [
        permute(parts[turn], "tok", [(one, one ^ (2 * turn)) for one in range(tok_count)])
        for turn in range(1, 4)
    ]
    projected, *gate = lax.optimization_barrier((projected, *parts[1:], *turned))
    parts[1:], turned = gate[:3], gate[3:]
    sums = key_value_sum(parts, place, projected)
    queries = swap_all(projected, "tok")
    relayed = permute(cache_relay(near, turned), "tok", pair)
    fresh_blocks = []
    for turn in range(4):
        pairs = []
        for one in range(req_count * tok_count):
            r, t = one // tok_count, one % tok_count
            dest = ((r // 2) * 2 + t % 2) ^ turn
            pairs.append((one, dest * tok_count + 4 * (r % 2) + t // 2))
        fresh_blocks.append(permute(sums[turn], ("req", "tok"), pairs))
    attended = attention(queries, place, fresh_blocks, own_block, turned, relayed)
    attended = swap_all(attended, "tok")
    parts_out, new_keys_values = output_project(attended, output_weight[0], query_rows)
    output_back = swap_all(parts_out, "tok")
    ffn_send, mixed_rows, ffn_weights = middle(
        activations[0],
        output_back,
        attn_weights,
        feedforward_gain,
        feedforward_router.T,
        ffn_routes,
    )
    received = swap_all(ffn_send, "tok")
    expert_parts = feedforward(received, gate_up[0], down_weight[0])
    expert_back = swap_all(expert_parts, "tok")
    layer_output = finish(mixed_rows, expert_back, ffn_weights)
    return (layer_output[None], new_keys_values[None])


def solution(mesh):
    placed = (
        P("req", "tok", None),
        P("req", "tok", None),
        P("req"),
        P(),
        P(),
        P("tok", "req"),
        P(),
        P("req", "tok", None),
        P("tok", None, None),
        P("tok", None, None),
        P(),
        P("req", "tok", None),
        P("tok", None, None),
        P("tok", None, None),
    )
    sizes = dict(mesh.shape)
    by_heads = sizes["tok"] == 8 and sizes["req"] == 4
    return jax.shard_map(
        local_heads if by_heads else local,
        mesh=mesh,
        in_specs=placed,
        out_specs=(P("req", "tok", None), P("req", "tok", None)),
        check_vma=False,
    )
```

```python
import math

import jax
import jax.numpy as jnp
from jax import lax
from jax.experimental import pallas as pl
from jax.experimental.pallas import tpu as pltpu
from jax.sharding import PartitionSpec as P

HEADS = 16
HEAD_DIM = 128
CAP = 6


def normed(values, gain):
    scale_rows = lax.rsqrt(jnp.mean(values * values, axis=-1, keepdims=True) + 1e-06)
    return values * scale_rows * gain


def slot_matrix(routes, experts, capacity):
    row_count, top_count = routes.shape
    labels = jnp.arange(experts, dtype=jnp.int32)
    onehot = (routes.reshape(row_count * top_count, 1) == labels[None, :]).astype(jnp.int32)
    before = jnp.cumsum(onehot, axis=0) - onehot
    within = jnp.sum(before * onehot, axis=1)
    placed = routes.reshape(row_count * top_count) * capacity + within
    columns = jnp.arange(experts * capacity, dtype=jnp.int32)
    return (placed[:, None] == columns[None, :]).astype(jnp.float32)


def router_gates(hidden, router, routes):
    logits = jnp.dot(hidden, router, preferred_element_type=jnp.float32)
    picked = jnp.take_along_axis(logits, routes, axis=1)
    return jax.nn.sigmoid(2.0 * picked - jnp.sum(picked, axis=1, keepdims=True))


def token_matrices(pair_slots, gates, top_count):
    row_count = gates.shape[0]
    per_token = pair_slots.reshape(row_count, top_count, -1)
    picked = jnp.sum(per_token, axis=1)
    weighted = jnp.sum(per_token * gates[:, :, None], axis=1)
    return (picked, weighted)


def spread_slots(slot_rows, experts, groups, capacity):
    feat_width = slot_rows.shape[-1]
    shaped = slot_rows.reshape(experts, 1, capacity, feat_width)
    return jnp.broadcast_to(shaped, (experts, groups, capacity, feat_width)).reshape(
        experts * groups, capacity, feat_width
    )


def head_groups(rows, experts, groups, group_width):
    row_count = rows.shape[0]
    shaped = (
        rows.reshape(row_count, 2, groups, group_width)
        .transpose(2, 0, 1, 3)
        .reshape(groups, row_count, 2 * group_width)
    )
    return jnp.broadcast_to(shaped[None], (experts, groups, row_count, 2 * group_width)).reshape(
        experts * groups, row_count, 2 * group_width
    )


def group_sum(received, experts, groups, capacity):
    feat_width = received.shape[-1]
    summed = jnp.sum(
        received.reshape(experts, groups, capacity, feat_width).astype(jnp.float32), axis=1
    )
    return summed.reshape(experts * capacity, feat_width)


def expert_feedforward(received, gate_piece, down_piece):
    units = down_piece.shape[0]
    projected = jnp.einsum("scd,df->scf", received, gate_piece, preferred_element_type=jnp.float32)
    active = (jax.nn.silu(projected[..., :units]) * projected[..., units:]).astype(jnp.bfloat16)
    return jnp.einsum("scf,fd->scd", active, down_piece, preferred_element_type=jnp.float32).astype(
        jnp.bfloat16
    )


def local(
    activations,
    cache_entries,
    cache_lengths,
    attention_gain,
    feedforward_gain,
    key_value_weight,
    attention_router,
    attention_routes,
    query_weight,
    output_weight,
    feedforward_router,
    feedforward_routes,
    gate_up,
    down_weight,
):
    tok_count = lax.axis_size("tok")
    tok_index = lax.axis_index("tok")
    experts = attention_router.shape[1]
    groups = tok_count // experts
    query_rows = activations.shape[1]
    cache_rows = cache_entries.shape[1]
    top_count = attention_routes.shape[2]
    model_width = activations.shape[2]
    head_count = HEADS // groups
    group_width = head_count * HEAD_DIM
    block_span = cache_rows + query_rows
    score_scale = 1.0 / math.sqrt(HEAD_DIM)
    cache_part = cache_entries[0]
    residual_in = activations[0].astype(jnp.float32)
    hidden = normed(residual_in, attention_gain).astype(jnp.bfloat16)
    stacked = lax.all_gather(hidden, "req", axis=0, tiled=True)
    projected_part = jnp.dot(
        stacked,
        lax.all_gather(key_value_weight, "tok", axis=0, tiled=True),
        preferred_element_type=jnp.float32,
    )
    new_keys_values = lax.all_to_all(
        projected_part.astype(jnp.bfloat16), "req", split_axis=0, concat_axis=1, tiled=True
    )
    combined = jnp.concatenate([cache_part, new_keys_values], axis=0)
    group_keys = lax.all_to_all(
        head_groups(combined, experts, groups, group_width),
        "tok",
        split_axis=0,
        concat_axis=0,
        tiled=True,
    )
    attn_routes = attention_routes[0]
    attn_pairs = slot_matrix(attn_routes, experts, CAP)
    attn_gate = router_gates(hidden, attention_router, attn_routes)
    attn_pick, attn_weights = token_matrices(attn_pairs, attn_gate, top_count)
    slot_inputs = jnp.dot(
        attn_pick.T.astype(jnp.bfloat16), hidden, preferred_element_type=jnp.float32
    ).astype(jnp.bfloat16)
    token_place = tok_index * query_rows + jnp.arange(query_rows, dtype=jnp.int32)
    slot_place = jnp.sum(attn_pick.astype(jnp.int32) * token_place[:, None], axis=0)
    query_send = spread_slots(slot_inputs, experts, groups, CAP)
    place_send = jnp.broadcast_to(
        slot_place.reshape(experts, 1, CAP), (experts, groups, CAP)
    ).reshape(tok_count, CAP)
    length = cache_lengths[0]
    source = jnp.arange(tok_count, dtype=jnp.int32).reshape(groups, experts, 1)
    offset = jnp.arange(block_span, dtype=jnp.int32).reshape(1, 1, block_span)
    turn_shape = (groups, experts * block_span)
    cached = jnp.broadcast_to(offset < cache_rows, (groups, experts, block_span)).reshape(
        turn_shape
    )
    cache_usable = (source * cache_rows + offset < length).reshape(turn_shape)
    fresh_place = (source * query_rows + offset - cache_rows).reshape(turn_shape)
    key_turns = group_keys.reshape(groups, experts * block_span, 2, head_count, HEAD_DIM)
    slot_rows = lax.all_to_all(query_send, "tok", split_axis=0, concat_axis=0, tiled=True)
    slot_places = lax.all_to_all(place_send, "tok", split_axis=0, concat_axis=0, tiled=True)
    items = slot_rows.shape[1]
    query_three = (
        jnp.einsum("scd,df->scf", slot_rows, query_weight[0], preferred_element_type=jnp.float32)
        .astype(jnp.bfloat16)
        .reshape(tok_count * items, head_count, HEAD_DIM)
    )
    query_place = slot_places.reshape(tok_count * items)

    def one_turn(state_in, turn_data):
        row_max, row_sums, weighted = state_in
        keys_values, cached_turn, usable_turn, place_turn = turn_data
        usable = jnp.where(
            cached_turn[None, :], usable_turn[None, :], place_turn[None, :] <= query_place[:, None]
        )[None]
        scores = (
            jnp.einsum(
                "phd,khd->hpk", query_three, keys_values[:, 0], preferred_element_type=jnp.float32
            )
            * score_scale
        )
        scores = jnp.where(usable, scores, -1e30)
        new_max = jnp.maximum(row_max, jnp.max(scores, axis=-1))
        weights = jnp.where(usable, jnp.exp(scores - new_max[..., None]), 0.0).astype(jnp.bfloat16)
        factor = jnp.exp(row_max - new_max)
        row_sums = row_sums * factor + jnp.sum(weights.astype(jnp.float32), axis=-1)
        weighted = weighted * factor[..., None] + jnp.einsum(
            "hpk,khd->hpd", weights, keys_values[:, 1], preferred_element_type=jnp.float32
        )
        return ((new_max, row_sums, weighted), None)

    query_total = tok_count * items
    initial = (
        jnp.full((head_count, query_total), -1e30, jnp.float32),
        jnp.zeros((head_count, query_total), jnp.float32),
        jnp.zeros((head_count, query_total, HEAD_DIM), jnp.float32),
    )
    final_state, _ = lax.scan(one_turn, initial, (key_turns, cached, cache_usable, fresh_place))
    row_max, row_sums, weighted = final_state
    attended = (
        (weighted / row_sums[..., None])
        .astype(jnp.bfloat16)
        .transpose(1, 0, 2)
        .reshape(tok_count, items, group_width)
    )
    parts = jnp.einsum(
        "scf,fd->scd", attended, output_weight[0], preferred_element_type=jnp.float32
    ).astype(jnp.bfloat16)
    output_back = lax.all_to_all(parts, "tok", split_axis=0, concat_axis=0, tiled=True)
    output_sums = group_sum(output_back, experts, groups, CAP)
    mixed_rows = (
        residual_in + jnp.dot(attn_weights, output_sums, precision=lax.Precision.HIGHEST)
    ).astype(jnp.bfloat16)
    hidden_two = normed(mixed_rows.astype(jnp.float32), feedforward_gain).astype(jnp.bfloat16)
    ffn_routes = feedforward_routes[0]
    ffn_pairs = slot_matrix(ffn_routes, experts, CAP)
    ffn_gate = router_gates(hidden_two, feedforward_router, ffn_routes)
    ffn_pick, ffn_weights = token_matrices(ffn_pairs, ffn_gate, top_count)
    every_rows, every_routes = (
        lax.all_gather(hidden_two, "tok", axis=0, tiled=True),
        lax.all_gather(ffn_routes, "tok", axis=0, tiled=True),
    )
    routes_all = every_routes.reshape(tok_count, query_rows, top_count)

    def source_slots(routes_block):
        return slot_matrix(routes_block, experts, CAP)

    per_source = jax.vmap(source_slots)(routes_all)
    per_token = jnp.sum(per_source.reshape(tok_count, query_rows, top_count, experts, CAP), axis=2)
    expert_mask = (jnp.arange(experts, dtype=jnp.int32) == tok_index // groups).astype(jnp.float32)
    picked = jnp.einsum("sqec,e->sqc", per_token, expert_mask)
    received = jnp.einsum(
        "sqc,sqd->scd",
        picked.astype(jnp.bfloat16),
        every_rows.reshape(tok_count, query_rows, model_width),
        preferred_element_type=jnp.float32,
    ).astype(jnp.bfloat16)
    expert_parts = expert_feedforward(received, gate_up[0], down_weight[0])
    expert_back = lax.all_to_all(expert_parts, "tok", split_axis=0, concat_axis=0, tiled=True)
    expert_sums = group_sum(expert_back, experts, groups, CAP)
    layer_output = (
        mixed_rows.astype(jnp.float32)
        + jnp.dot(ffn_weights, expert_sums, precision=lax.Precision.HIGHEST)
    ).astype(jnp.bfloat16)
    return (layer_output[None], new_keys_values[None])


PAD = 8
LANES = 128
FF_TILE = 512
WIRE = 4


def column_stream(source, buffers, sems, tile):
    return [
        pltpu.make_async_copy(
            source.at[:, pl.ds(step * tile, tile)], buffers.at[step], sems.at[step]
        )
        for step in range(buffers.shape[0])
    ]


def permute(values, axis, pairs):
    return lax.ppermute(values, axis, pairs)


def swap_all(values, axis):
    return lax.all_to_all(values, axis, split_axis=0, concat_axis=0, tiled=True)


def whole_spec():
    return pl.BlockSpec(memory_space=pltpu.VMEM)


def index_spec():
    return pl.BlockSpec(memory_space=pltpu.SMEM)


def iota(shape, axis):
    return lax.broadcasted_iota(jnp.int32, shape, axis)


def any_spec():
    return pl.BlockSpec(memory_space=pl.ANY)


def in_hbm(*arrays):
    return [pltpu.with_memory_space_constraint(one, pltpu.HBM) for one in arrays]


def in_vmem(*arrays):
    return [pltpu.with_memory_space_constraint(one, pltpu.VMEM) for one in arrays]


def load_all(pairs, sems):
    copies = [
        pltpu.make_async_copy(source, target, sems.at[number])
        for number, (source, target) in enumerate(pairs)
    ]
    for one in copies:
        one.start()
    for one in copies:
        one.wait()


def padded_picks(routes, experts, height):
    row_count = routes.shape[1]
    row = iota((experts * height, row_count), 0)
    expert, slot = row // height, row % height
    first, second = routes[0:1, :] == expert, routes[1:2, :] == expert
    named = jnp.where(first, 1.0, 0.0) + jnp.where(second, 1.0, 0.0)
    earlier = (iota((row_count, row_count), 0) < iota((row_count, row_count), 1)).astype(
        jnp.bfloat16
    )
    before = jnp.dot(
        named.astype(jnp.bfloat16), earlier, preferred_element_type=jnp.float32
    ).astype(jnp.int32)
    here = (before == slot) & (slot < CAP)
    return named * here.astype(jnp.float32), first


def gate_weights(hidden, router, routes, picks, first):
    logits = lax.dot_general(
        router, hidden, (((1,), (1,)), ((), ())), preferred_element_type=jnp.float32
    )
    label = iota(logits.shape, 0)
    one = jnp.sum(jnp.where(routes[0:1, :] == label, logits, 0.0), axis=0, keepdims=True)
    two = jnp.sum(jnp.where(routes[1:2, :] == label, logits, 0.0), axis=0, keepdims=True)
    gate_one = 1.0 / (1.0 + jnp.exp(two - one))
    gate_two = 1.0 / (1.0 + jnp.exp(one - two))
    return picks * jnp.where(first, gate_one, gate_two)


def row_norm(values, gain):
    mean = jnp.mean(values * values, axis=-1, keepdims=True)
    return (values * lax.rsqrt(mean + 1e-06) * gain).astype(jnp.bfloat16)


def pick_rows(picks, rows):
    return jnp.dot(picks.astype(jnp.bfloat16), rows, preferred_element_type=jnp.float32)


def compact(rows):
    count = rows.shape[0] // PAD * CAP
    one, two = iota((count, rows.shape[0]), 0), iota((count, rows.shape[0]), 1)
    chosen = ((one // CAP) * PAD + one % CAP == two).astype(jnp.bfloat16)
    return jnp.dot(chosen, rows, preferred_element_type=jnp.float32)


def wire_order(blocks, columns):
    total = blocks * columns * CAP
    row = iota((total, total), 0)
    block, column, slot = row // (columns * CAP), row // CAP % columns, row % CAP
    return (column * (blocks * CAP) + block * CAP + slot == iota((total, total), 1)).astype(
        jnp.bfloat16
    )


def pack(pieces, blocks):
    columns, span = len(pieces), pieces[0].shape[1]
    stacked = jnp.concatenate(pieces, axis=0)
    moved = jnp.dot(wire_order(blocks, columns), stacked, preferred_element_type=jnp.float32)
    return moved.reshape(blocks, columns * CAP, span).astype(jnp.bfloat16)


def split_columns(rows):
    span = rows.shape[1] // WIRE
    return [rows[:, step * span : (step + 1) * span] for step in range(WIRE)]


def unpack(values):
    blocks, height, span = values.shape
    columns = height // CAP
    flat = values.astype(jnp.float32).reshape(blocks * height, span).astype(jnp.bfloat16)
    moved = lax.dot_general(
        wire_order(blocks, columns),
        flat,
        (((0,), (0,)), ((), ())),
        preferred_element_type=jnp.float32,
    ).astype(jnp.bfloat16)
    rows = blocks * CAP
    return jnp.concatenate(
        [moved[step * rows : (step + 1) * rows] for step in range(columns)], axis=1
    )


def exact_mix(weights, rows):
    high = weights.astype(jnp.bfloat16)
    rest = weights - high.astype(jnp.float32)
    middle = rest.astype(jnp.bfloat16)
    low = (rest - middle.astype(jnp.float32)).astype(jnp.bfloat16)
    count = weights.shape[1]
    stacked = lax.dot_general(
        jnp.concatenate([high, middle, low], axis=1),
        rows,
        (((0,), (0,)), ((), ())),
        preferred_element_type=jnp.float32,
    )
    return stacked[:count] + (stacked[count : 2 * count] + stacked[2 * count :])


def prepare(activations, gain, router, routes, tok_count):
    rows, width = activations.shape
    experts = router.shape[0]
    span = width // tok_count
    half = rows // 2
    per_row = width // (2 * span)

    def body(
        act_in, gain_in, router_in, route_in, out_ref, weight_ref,
        act_ref, gain_ref, router_ref, route_ref, wide, copy, sems,
    ):
        load_all(
            [
                (act_in, act_ref),
                (gain_in, gain_ref),
                (router_in, router_ref),
                (route_in, route_ref),
            ],
            sems,
        )
        route = route_ref[...]
        hidden = row_norm(act_ref[...].astype(jnp.float32), gain_ref[...])
        picks, _ = padded_picks(route, experts, PAD)
        wide[...] = pick_rows(picks, hidden)
        copy[...] = hidden.astype(jnp.float32)
        for dest in range(tok_count):
            chip, core = dest // 2, dest % 2
            for place in range(half):
                row = dest * PAD + CAP + place // per_row
                for side in range(2):
                    column = (place % per_row) * 2 * span + side * span
                    source = (2 * chip + (core ^ side)) * span
                    wide[row : row + 1, column : column + span] = copy[
                        core * half + place : core * half + place + 1, source : source + span
                    ]
        out_ref[:, :, :width] = wide[...].astype(jnp.bfloat16).reshape(tok_count, PAD, width)
        number = iota((rows, LANES), 0).astype(jnp.float32).astype(jnp.bfloat16)
        out_ref[:, :, width:] = (
            pick_rows(picks, number).astype(jnp.bfloat16).reshape(tok_count, PAD, LANES)
        )
        narrow, first = padded_picks(route, experts, CAP)
        weight_ref[...] = gate_weights(hidden, router_ref[...], route, narrow, first)

    return pl.pallas_call(
        body,
        in_specs=[any_spec()] * 4,
        out_specs=[whole_spec()] * 2,
        out_shape=[
            jax.ShapeDtypeStruct((tok_count, PAD, width + LANES), jnp.bfloat16),
            jax.ShapeDtypeStruct((tok_count * CAP, rows), jnp.float32),
        ],
        scratch_shapes=[
            pltpu.VMEM((rows, width), activations.dtype),
            pltpu.VMEM((1, width), gain.dtype),
            pltpu.VMEM(router.shape, router.dtype),
            pltpu.VMEM(routes.shape, routes.dtype),
            pltpu.VMEM((tok_count * PAD, width), jnp.float32),
            pltpu.VMEM((rows, width), jnp.float32),
            pltpu.SemaphoreType.DMA((4,)),
        ],
        compiler_params=pltpu.CompilerParams(vmem_limit_bytes=4 << 20),
        name="prepare",
    )(*in_hbm(activations, gain.reshape(1, width), router, routes))


def cache_split(cache_part, side, place, after):
    rows, width = cache_part.shape
    count = 8
    span = width // 2 // count

    def body(index_ref, cache_ref, side_ref, after_ref, *refs):
        outs, side_out, sems = refs[:5], refs[5], refs[6]
        pairs = []
        for number in range(count):
            turn, side = number // 2, number % 2
            out, base = (outs[turn + 1], side * rows) if turn else (outs[side], 0)
            start = pl.multiple_of((index_ref[2] ^ number) * span, span)
            for kind in range(2):
                pairs.append(
                    (
                        cache_ref.at[:, pl.ds(kind * (width // 2) + start, span)],
                        out.at[base : base + rows, kind * span : (kind + 1) * span],
                    )
                )
        pairs.append((side_ref, side_out))
        load_all(pairs, sems)

    shapes = [(rows, 2 * span)] * 2 + [(2 * rows, 2 * span)] * 3
    return pl.pallas_call(
        body,
        in_specs=[index_spec()] + [any_spec()] * 3,
        out_specs=[whole_spec()] * 6,
        out_shape=[jax.ShapeDtypeStruct(one, cache_part.dtype) for one in shapes]
        + [pltpu.VMEM(side.shape, side.dtype)],
        scratch_shapes=[pltpu.SemaphoreType.DMA((2 * count + 1,))],
        compiler_params=pltpu.CompilerParams(vmem_limit_bytes=4 << 20),
        name="cache_split",
    )(place, *in_hbm(cache_part, side), after)


def cache_relay(near, turned):
    rows, width = near.shape

    def body(near_ref, *refs):
        out_ref = refs[-1]
        out_ref[:rows, :] = near_ref[...]
        for turn in range(1, 4):
            out_ref[turn * rows : (turn + 1) * rows, :] = refs[turn - 1][rows:, :]

    return pl.pallas_call(
        body,
        in_specs=[whole_spec()] * 4,
        out_specs=whole_spec(),
        out_shape=jax.ShapeDtypeStruct((4 * rows, width), near.dtype),
        compiler_params=pltpu.CompilerParams(vmem_limit_bytes=3 << 20),
        name="cache_relay",
    )(near, *turned)


def own_tokens(arrived, after, tok_count, width):
    span = width // tok_count
    per_row = width // (2 * span)
    extra = PAD - CAP

    def body(in_ref, *rest):
        out_ref, wide = rest[len(after) :]
        for source in range(tok_count):
            rows = in_ref[source, :, :width].astype(jnp.float32)
            for part in range(extra):
                for place in range(per_row):
                    row = source * extra * per_row + part * per_row + place
                    wide[row : row + 1, :] = rows[
                        CAP + part : CAP + part + 1, place * 2 * span : (place + 1) * 2 * span
                    ]
        out_ref[...] = wide[...].astype(jnp.bfloat16)

    count = tok_count * extra * per_row
    return pl.pallas_call(
        body,
        in_specs=[whole_spec()] + [any_spec()] * len(after),
        out_specs=whole_spec(),
        out_shape=jax.ShapeDtypeStruct((count, 2 * span), jnp.bfloat16),
        scratch_shapes=[pltpu.VMEM((count, 2 * span), jnp.float32)],
        compiler_params=pltpu.CompilerParams(vmem_limit_bytes=4 << 20),
        name="own_tokens",
    )(arrived, *after)


def query_project(arrived, weight, after, tok_count):
    width = weight.shape[0]
    span = width // tok_count
    slots = tok_count * CAP
    height = slots + PAD
    tile = 2 * span
    steps = width // tile

    def body(in_ref, weight_ref, *rest):
        out_ref, held, sems = rest[len(after) :]
        copies = column_stream(weight_ref, held, sems, tile)
        for one in copies:
            one.start()
        every = compact(in_ref[...].reshape(tok_count * PAD, width + LANES))
        rows = every[:, :width].astype(jnp.bfloat16)
        local = every[:, width : width + LANES]
        mine = iota(local.shape, 0)
        placed = local + ((mine // CAP) * (2 * PAD)).astype(jnp.float32)
        placed = jnp.where(mine == iota(local.shape, 1), placed, 0.0)
        line = jnp.broadcast_to(jnp.sum(placed, axis=0, keepdims=True), (PAD, LANES))
        line = jnp.concatenate([line] * (span // LANES), axis=1).astype(jnp.bfloat16)
        for step in range(steps):
            copies[step].wait()
            query = jnp.dot(rows, held[step], preferred_element_type=jnp.float32).astype(
                jnp.bfloat16
            )
            for one in range(tile // span):
                place = step * (tile // span) + one
                out_ref[place, :slots, :] = query[:, one * span : (one + 1) * span]
                out_ref[place, slots:, :] = line
    return pl.pallas_call(
        body,
        in_specs=[whole_spec(), any_spec()] + [any_spec()] * len(after),
        out_specs=whole_spec(),
        out_shape=jax.ShapeDtypeStruct((tok_count, height, span), jnp.bfloat16),
        scratch_shapes=[
            pltpu.VMEM((steps, width, tile), jnp.bfloat16),
            pltpu.SemaphoreType.DMA((steps,)),
        ],
        compiler_params=pltpu.CompilerParams(vmem_limit_bytes=14 << 20),
        cost_estimate=pl.CostEstimate(flops=0, transcendentals=0, bytes_accessed=40 << 20),
        name="query_project",
    )(arrived, *in_hbm(weight), *after)


def key_value_parts(tokens, weight, sibling, place, after):
    rows, depth = tokens[0].shape
    half = depth // 2
    quarter = weight.shape[1] // 4
    count = len(tokens)

    def body(place_ref, *refs):
        token_refs, weight_ref, sibling_ref = refs[:count], refs[count], refs[count + 1]
        outs = refs[count + 2 + len(after) :]
        stacked = jnp.concatenate([one[...] for one in token_refs], axis=0)
        for turn in range(4):
            start = pl.multiple_of(((place_ref[2] // 2) ^ turn) * quarter, quarter)
            part = jnp.dot(
                stacked[:, :half],
                weight_ref[:, pl.ds(start, quarter)],
                preferred_element_type=jnp.float32,
            ) + jnp.dot(
                stacked[:, half:],
                sibling_ref[:, pl.ds(start, quarter)],
                preferred_element_type=jnp.float32,
            )
            outs[turn][...] = part.astype(outs[turn].dtype)

    shapes = [
        jax.ShapeDtypeStruct((count * rows, quarter), jnp.float32 if turn == 0 else jnp.bfloat16)
        for turn in range(4)
    ]
    return pl.pallas_call(
        body,
        in_specs=[index_spec()] + [whole_spec()] * (count + 2) + [any_spec()] * len(after),
        out_specs=[whole_spec()] * 4,
        out_shape=shapes,
        compiler_params=pltpu.CompilerParams(vmem_limit_bytes=8 << 20),
        name="key_value_parts",
    )(place, *tokens, weight, sibling, *after)


def key_value_sum(parts, place, after):
    rows, quarter = parts[0].shape
    block = rows // 4

    def body(place_ref, *refs):
        ins, outs = refs[:4], refs[5:]
        req = place_ref[1]
        source = (req // 2) * 2 + place_ref[2] % 2
        for turn in range(4):
            start = pl.multiple_of((req ^ source ^ turn) * block, block)
            total = ins[0][pl.ds(start, block), :]
            for one in ins[1:]:
                total = total + one[pl.ds(start, block), :].astype(jnp.float32)
            outs[turn][...] = total.astype(jnp.bfloat16)

    return pl.pallas_call(
        body,
        in_specs=[index_spec()] + [whole_spec()] * 4 + [any_spec()],
        out_specs=[whole_spec()] * 4,
        out_shape=[jax.ShapeDtypeStruct((block, quarter), jnp.bfloat16)] * 4,
        compiler_params=pltpu.CompilerParams(vmem_limit_bytes=4 << 20),
        name="key_value_sum",
    )(place, *parts, after)


def attention(message, scalars, fresh_blocks, own, turned, relayed):
    blocks, _, span = message.shape
    heads = span // HEAD_DIM
    slots = blocks * CAP
    fresh_rows = fresh_blocks[0].shape[0]
    half = fresh_rows // blocks
    cache_rows = own.shape[0]
    scale = 1.0 / math.sqrt(HEAD_DIM)
    contract = (((1,), (1,)), ((), ()))

    def body(scalar_ref, in_ref, *refs):
        fresh_refs, own_ref, turned_refs, relay_ref = refs[:4], refs[4], refs[5:8], refs[8]
        out_ref = refs[9]
        limit, req, tok = scalar_ref[0], scalar_ref[1], scalar_ref[2]
        pieces = []
        for source in range(4):
            picked = fresh_refs[3][...]
            for turn in range(3):
                picked = jnp.where((req ^ source) == turn, fresh_refs[turn][...], picked)
            pieces.append(picked)
        new_keys = jnp.concatenate(pieces[:2], axis=0)
        new_values = jnp.concatenate(pieces[2:], axis=0)
        key_row = iota((1, blocks * cache_rows), 1)
        key_block = key_row // cache_rows
        key_source = ((key_block % 4) * 2 + key_block // 4) ^ tok
        cache_usable = key_source * cache_rows + key_row % cache_rows < limit
        new_row = iota((1, 2 * fresh_rows), 1)
        within = new_row % fresh_rows
        new_place = (within // half) * (2 * half) + (new_row // fresh_rows) * half + within % half
        places = []
        for expert in range(blocks):
            line = in_ref[expert, slots:, :LANES].astype(jnp.float32)[0:1]
            chosen = iota((slots, LANES), 0) == iota((slots, LANES), 1)
            places.append(jnp.sum(jnp.where(chosen, line, 0.0), axis=1, keepdims=True))
        new_usable = new_place <= jnp.concatenate(places, axis=0).astype(jnp.int32)
        flat = in_ref[:, :slots, :].reshape(blocks * slots, span)
        cached = [own_ref] + [one.at[:cache_rows] for one in turned_refs] + [relay_ref]
        keys = jnp.concatenate([one[:, :span] for one in cached], axis=0)
        values = jnp.concatenate([one[:, span:] for one in cached], axis=0)
        for head in range(heads):
            cols = slice(head * HEAD_DIM, (head + 1) * HEAD_DIM)
            query = flat[:, cols]
            first = lax.dot_general(
                query, keys[:, cols], contract, preferred_element_type=jnp.float32
            )
            second = lax.dot_general(
                query, new_keys[:, cols], contract, preferred_element_type=jnp.float32
            )
            first = jnp.where(cache_usable, first * scale, -1e30)
            second = jnp.where(new_usable, second * scale, -1e30)
            top = jnp.maximum(
                jnp.max(first, axis=-1, keepdims=True), jnp.max(second, axis=-1, keepdims=True)
            )
            first = jnp.exp(first - top).astype(jnp.bfloat16)
            second = jnp.exp(second - top).astype(jnp.bfloat16)
            sums = jnp.sum(first.astype(jnp.float32), axis=-1, keepdims=True) + jnp.sum(
                second.astype(jnp.float32), axis=-1, keepdims=True
            )
            mixed = jnp.dot(first, values[:, cols], preferred_element_type=jnp.float32) + jnp.dot(
                second, new_values[:, cols], preferred_element_type=jnp.float32
            )
            out_ref[:, :slots, cols] = (
                (mixed / sums).astype(jnp.bfloat16).reshape(blocks, slots, HEAD_DIM)
            )
        for kind in range(2):
            for part in range(2):
                start = slots + kind * 2 * half + part * half
                out_ref[:, start : start + half, :] = pieces[2 * kind + part].reshape(
                    blocks, half, span
                )

    return pl.pallas_call(
        body,
        in_specs=[index_spec()] + [whole_spec()] * 10,
        out_specs=whole_spec(),
        out_shape=jax.ShapeDtypeStruct((blocks, slots + 4 * half, span), jnp.bfloat16),
        compiler_params=pltpu.CompilerParams(vmem_limit_bytes=14 << 20),
        name="attention",
    )(scalars, message, *fresh_blocks, own, *turned, relayed)


def output_project(arrived, weight, query_rows):
    blocks, height, span = arrived.shape
    slots = blocks * CAP
    width = weight.shape[1]
    tile = width // WIRE

    def body(in_ref, weight_ref, out_ref, fresh_ref, held, sems):
        copies = column_stream(weight_ref, held, sems, tile)
        for one in copies:
            one.start()
        rows, pieces = [], []
        for block in range(blocks):
            cols = slice(block * span, (block + 1) * span)
            rows.append(in_ref[block, :slots, :])
            fresh_ref[:, cols] = in_ref[block, slots : slots + query_rows, :]
            fresh_ref[:, block * span + width : (block + 1) * span + width] = in_ref[
                block, slots + query_rows :, :
            ]
        rows = jnp.concatenate(rows, axis=1)
        for step in range(width // tile):
            copies[step].wait()
            part = jnp.dot(rows, held[step], preferred_element_type=jnp.float32)
            pieces.append(part.astype(jnp.bfloat16))
        out_ref[...] = pack(pieces, blocks)

    return pl.pallas_call(
        body,
        in_specs=[whole_spec(), any_spec()],
        out_specs=[whole_spec()] * 2,
        out_shape=[
            jax.ShapeDtypeStruct((blocks, WIRE * CAP, tile), jnp.bfloat16),
            jax.ShapeDtypeStruct((query_rows, 2 * width), jnp.bfloat16),
        ],
        scratch_shapes=[
            pltpu.VMEM((width // tile, blocks * span, tile), jnp.bfloat16),
            pltpu.SemaphoreType.DMA((width // tile,)),
        ],
        compiler_params=pltpu.CompilerParams(vmem_limit_bytes=14 << 20),
        name="output_project",
    )(arrived, *in_hbm(weight))


def middle(activations, arrived, weights, gain, router, routes):
    rows, width = activations.shape
    blocks = arrived.shape[0]
    experts = router.shape[0]

    def body(act_ref, in_ref, old_ref, gain_ref, router_ref, route_ref, out_ref, mix_ref, new_ref):
        route = route_ref[...]
        added = exact_mix(old_ref[...], unpack(in_ref[...]))
        mixed = (act_ref[...].astype(jnp.float32) + added).astype(jnp.bfloat16)
        mix_ref[...] = mixed
        hidden = row_norm(mixed.astype(jnp.float32), gain_ref[...])
        picks, first = padded_picks(route, experts, CAP)
        out_ref[...] = pack(split_columns(pick_rows(picks, hidden).astype(jnp.bfloat16)), blocks)
        new_ref[...] = gate_weights(hidden, router_ref[...], route, picks, first)

    return pl.pallas_call(
        body,
        in_specs=[whole_spec()] * 6,
        out_specs=[whole_spec()] * 3,
        out_shape=[
            jax.ShapeDtypeStruct(arrived.shape, jnp.bfloat16),
            jax.ShapeDtypeStruct((rows, width), jnp.bfloat16),
            jax.ShapeDtypeStruct((blocks * CAP, rows), jnp.float32),
        ],
        compiler_params=pltpu.CompilerParams(vmem_limit_bytes=4 << 20),
        name="middle",
    )(activations, arrived, weights, gain.reshape(1, width), router, routes)


def finish(mixed, arrived, weights):
    rows, width = mixed.shape

    def body(mix_ref, in_ref, weight_ref, out_ref):
        added = exact_mix(weight_ref[...], unpack(in_ref[...]))
        out_ref[...] = (mix_ref[...].astype(jnp.float32) + added).astype(jnp.bfloat16)

    return pl.pallas_call(
        body,
        in_specs=[whole_spec()] * 3,
        out_specs=whole_spec(),
        out_shape=jax.ShapeDtypeStruct((rows, width), jnp.bfloat16),
        compiler_params=pltpu.CompilerParams(vmem_limit_bytes=4 << 20),
        name="finish",
    )(mixed, arrived, weights)


def feedforward(arrived, gate_piece, down_piece):
    blocks, width = arrived.shape[0], down_piece.shape[1]
    count = blocks * CAP
    units = down_piece.shape[0]
    tile = FF_TILE
    steps = units // tile
    slots = 4

    def body(in_ref, gate_ref, down_ref, out_ref, gates, ups, downs, sems):
        def copies(step):
            slot = step % slots
            return [
                pltpu.make_async_copy(
                    gate_ref.at[:, pl.ds(step * tile, tile)], gates.at[slot], sems.at[slot, 0]
                ),
                pltpu.make_async_copy(
                    gate_ref.at[:, pl.ds(units + step * tile, tile)],
                    ups.at[slot],
                    sems.at[slot, 1],
                ),
                pltpu.make_async_copy(
                    down_ref.at[pl.ds(step * tile, tile), :], downs.at[slot], sems.at[slot, 2]
                ),
            ]

        for step in range(slots):
            for one in copies(step):
                one.start()
        rows = unpack(in_ref[...])
        total = jnp.zeros((count, width), jnp.float32)
        for step in range(steps):
            slot = step % slots
            gate_copy, up_copy, down_copy = copies(step)
            gate_copy.wait()
            gate = jnp.dot(rows, gates[slot], preferred_element_type=jnp.float32)
            up_copy.wait()
            up = jnp.dot(rows, ups[slot], preferred_element_type=jnp.float32)
            active = (gate / (1.0 + jnp.exp(-gate)) * up).astype(jnp.bfloat16)
            down_copy.wait()
            total = total + jnp.dot(active, downs[slot], preferred_element_type=jnp.float32)
            if step + slots < steps:
                for one in copies(step + slots):
                    one.start()
        out_ref[...] = pack(split_columns(total.astype(jnp.bfloat16)), blocks)

    return pl.pallas_call(
        body,
        in_specs=[whole_spec(), any_spec(), any_spec()],
        out_specs=whole_spec(),
        out_shape=jax.ShapeDtypeStruct(arrived.shape, jnp.bfloat16),
        scratch_shapes=[
            pltpu.VMEM((slots, width, tile), jnp.bfloat16),
            pltpu.VMEM((slots, width, tile), jnp.bfloat16),
            pltpu.VMEM((slots, tile, width), jnp.bfloat16),
            pltpu.SemaphoreType.DMA((slots, 3)),
        ],
        compiler_params=pltpu.CompilerParams(vmem_limit_bytes=32 << 20),
        name="feedforward",
    )(arrived, *in_hbm(gate_piece, down_piece))


def local_heads(
    activations,
    cache_entries,
    cache_lengths,
    attention_gain,
    feedforward_gain,
    key_value_weight,
    attention_router,
    attention_routes,
    query_weight,
    output_weight,
    feedforward_router,
    feedforward_routes,
    gate_up,
    down_weight,
):
    tok_count = lax.axis_size("tok")
    req_count = lax.axis_size("req")
    tok_index = lax.axis_index("tok")
    req_index = lax.axis_index("req")
    query_rows, width = activations.shape[1:]

    attn_routes = attention_routes[0].T
    ffn_routes = feedforward_routes[0].T
    place = jnp.stack([cache_lengths[0], req_index, tok_index])
    message, attn_weights = prepare(
        activations[0], attention_gain, attention_router.T, attn_routes, tok_count
    )
    arrived = swap_all(message, "tok")
    own_block, near, *turned, weight_held = cache_split(
        cache_entries[0], key_value_weight, place, attn_weights
    )
    turned = [
        permute(turned[turn - 1], "tok", [(one, one ^ (2 * turn)) for one in range(tok_count)])
        for turn in range(1, 4)
    ]
    pair = [(one, one ^ 1) for one in range(tok_count)]
    sibling = permute(key_value_weight, "tok", pair)
    mine = own_tokens(arrived, [sibling], tok_count, width)
    tokens = [mine] + [
        permute(mine, "req", [(one, one ^ turn) for one in range(req_count)])
        for turn in range(1, req_count)
    ]
    parts = key_value_parts(tokens, weight_held, sibling, place, turned)
    projected = query_project(arrived, query_weight[0], parts[:1], tok_count)
    parts = [parts[0]] + [
        permute(parts[turn], "tok", [(one, one ^ (2 * turn)) for one in range(tok_count)])
        for turn in range(1, 4)
    ]
    projected, *gate = lax.optimization_barrier((projected, *parts[1:], *turned))
    parts[1:], turned = gate[:3], gate[3:]
    sums = key_value_sum(parts, place, projected)
    queries = swap_all(projected, "tok")
    relayed = permute(cache_relay(near, turned), "tok", pair)
    fresh_blocks = []
    for turn in range(4):
        pairs = []
        for one in range(req_count * tok_count):
            r, t = one // tok_count, one % tok_count
            dest = ((r // 2) * 2 + t % 2) ^ turn
            pairs.append((one, dest * tok_count + 4 * (r % 2) + t // 2))
        fresh_blocks.append(permute(sums[turn], ("req", "tok"), pairs))
    attended = attention(queries, place, fresh_blocks, own_block, turned, relayed)
    attended = swap_all(attended, "tok")
    parts_out, new_keys_values = output_project(attended, output_weight[0], query_rows)
    output_back = swap_all(parts_out, "tok")
    ffn_send, mixed_rows, ffn_weights = middle(
        activations[0],
        output_back,
        attn_weights,
        feedforward_gain,
        feedforward_router.T,
        ffn_routes,
    )
    received = swap_all(ffn_send, "tok")
    expert_parts = feedforward(received, gate_up[0], down_weight[0])
    expert_back = swap_all(expert_parts, "tok")
    layer_output = finish(mixed_rows, expert_back, ffn_weights)
    return (layer_output[None], new_keys_values[None])


def solution(mesh):
    placed = (
        P("req", "tok", None),
        P("req", "tok", None),
        P("req"),
        P(),
        P(),
        P("tok", "req"),
        P(),
        P("req", "tok", None),
        P("tok", None, None),
        P("tok", None, None),
        P(),
        P("req", "tok", None),
        P("tok", None, None),
        P("tok", None, None),
    )
    sizes = dict(mesh.shape)
    by_heads = sizes["tok"] == 8 and sizes["req"] == 4
    return jax.shard_map(
        local_heads if by_heads else local,
        mesh=mesh,
        in_specs=placed,
        out_specs=(P("req", "tok", None), P("req", "tok", None)),
        check_vma=False,
    )
```

```python
import math

import jax
import jax.numpy as jnp
from jax import lax
from jax.experimental import pallas as pl
from jax.experimental.pallas import tpu as pltpu
from jax.sharding import PartitionSpec as P

HEADS = 16
HEAD_DIM = 128
CAP = 6


def normed(values, gain):
    scale_rows = lax.rsqrt(jnp.mean(values * values, axis=-1, keepdims=True) + 1e-06)
    return values * scale_rows * gain


def slot_matrix(routes, experts, capacity):
    row_count, top_count = routes.shape
    labels = jnp.arange(experts, dtype=jnp.int32)
    onehot = (routes.reshape(row_count * top_count, 1) == labels[None, :]).astype(jnp.int32)
    before = jnp.cumsum(onehot, axis=0) - onehot
    within = jnp.sum(before * onehot, axis=1)
    placed = routes.reshape(row_count * top_count) * capacity + within
    columns = jnp.arange(experts * capacity, dtype=jnp.int32)
    return (placed[:, None] == columns[None, :]).astype(jnp.float32)


def router_gates(hidden, router, routes):
    logits = jnp.dot(hidden, router, preferred_element_type=jnp.float32)
    picked = jnp.take_along_axis(logits, routes, axis=1)
    return jax.nn.sigmoid(2.0 * picked - jnp.sum(picked, axis=1, keepdims=True))


def token_matrices(pair_slots, gates, top_count):
    row_count = gates.shape[0]
    per_token = pair_slots.reshape(row_count, top_count, -1)
    picked = jnp.sum(per_token, axis=1)
    weighted = jnp.sum(per_token * gates[:, :, None], axis=1)
    return (picked, weighted)


def spread_slots(slot_rows, experts, groups, capacity):
    feat_width = slot_rows.shape[-1]
    shaped = slot_rows.reshape(experts, 1, capacity, feat_width)
    return jnp.broadcast_to(shaped, (experts, groups, capacity, feat_width)).reshape(
        experts * groups, capacity, feat_width
    )


def head_groups(rows, experts, groups, group_width):
    row_count = rows.shape[0]
    shaped = (
        rows.reshape(row_count, 2, groups, group_width)
        .transpose(2, 0, 1, 3)
        .reshape(groups, row_count, 2 * group_width)
    )
    return jnp.broadcast_to(shaped[None], (experts, groups, row_count, 2 * group_width)).reshape(
        experts * groups, row_count, 2 * group_width
    )


def group_sum(received, experts, groups, capacity):
    feat_width = received.shape[-1]
    summed = jnp.sum(
        received.reshape(experts, groups, capacity, feat_width).astype(jnp.float32), axis=1
    )
    return summed.reshape(experts * capacity, feat_width)


def expert_feedforward(received, gate_piece, down_piece):
    units = down_piece.shape[0]
    projected = jnp.einsum("scd,df->scf", received, gate_piece, preferred_element_type=jnp.float32)
    active = (jax.nn.silu(projected[..., :units]) * projected[..., units:]).astype(jnp.bfloat16)
    return jnp.einsum("scf,fd->scd", active, down_piece, preferred_element_type=jnp.float32).astype(
        jnp.bfloat16
    )


def local(
    activations,
    cache_entries,
    cache_lengths,
    attention_gain,
    feedforward_gain,
    key_value_weight,
    attention_router,
    attention_routes,
    query_weight,
    output_weight,
    feedforward_router,
    feedforward_routes,
    gate_up,
    down_weight,
):
    tok_count = lax.axis_size("tok")
    tok_index = lax.axis_index("tok")
    experts = attention_router.shape[1]
    groups = tok_count // experts
    query_rows = activations.shape[1]
    cache_rows = cache_entries.shape[1]
    top_count = attention_routes.shape[2]
    model_width = activations.shape[2]
    head_count = HEADS // groups
    group_width = head_count * HEAD_DIM
    block_span = cache_rows + query_rows
    score_scale = 1.0 / math.sqrt(HEAD_DIM)
    cache_part = cache_entries[0]
    residual_in = activations[0].astype(jnp.float32)
    hidden = normed(residual_in, attention_gain).astype(jnp.bfloat16)
    stacked = lax.all_gather(hidden, "req", axis=0, tiled=True)
    projected_part = jnp.dot(
        stacked,
        lax.all_gather(key_value_weight, "tok", axis=0, tiled=True),
        preferred_element_type=jnp.float32,
    )
    new_keys_values = lax.all_to_all(
        projected_part.astype(jnp.bfloat16), "req", split_axis=0, concat_axis=1, tiled=True
    )
    combined = jnp.concatenate([cache_part, new_keys_values], axis=0)
    group_keys = lax.all_to_all(
        head_groups(combined, experts, groups, group_width),
        "tok",
        split_axis=0,
        concat_axis=0,
        tiled=True,
    )
    attn_routes = attention_routes[0]
    attn_pairs = slot_matrix(attn_routes, experts, CAP)
    attn_gate = router_gates(hidden, attention_router, attn_routes)
    attn_pick, attn_weights = token_matrices(attn_pairs, attn_gate, top_count)
    slot_inputs = jnp.dot(
        attn_pick.T.astype(jnp.bfloat16), hidden, preferred_element_type=jnp.float32
    ).astype(jnp.bfloat16)
    token_place = tok_index * query_rows + jnp.arange(query_rows, dtype=jnp.int32)
    slot_place = jnp.sum(attn_pick.astype(jnp.int32) * token_place[:, None], axis=0)
    query_send = spread_slots(slot_inputs, experts, groups, CAP)
    place_send = jnp.broadcast_to(
        slot_place.reshape(experts, 1, CAP), (experts, groups, CAP)
    ).reshape(tok_count, CAP)
    length = cache_lengths[0]
    source = jnp.arange(tok_count, dtype=jnp.int32).reshape(groups, experts, 1)
    offset = jnp.arange(block_span, dtype=jnp.int32).reshape(1, 1, block_span)
    turn_shape = (groups, experts * block_span)
    cached = jnp.broadcast_to(offset < cache_rows, (groups, experts, block_span)).reshape(
        turn_shape
    )
    cache_usable = (source * cache_rows + offset < length).reshape(turn_shape)
    fresh_place = (source * query_rows + offset - cache_rows).reshape(turn_shape)
    key_turns = group_keys.reshape(groups, experts * block_span, 2, head_count, HEAD_DIM)
    slot_rows = lax.all_to_all(query_send, "tok", split_axis=0, concat_axis=0, tiled=True)
    slot_places = lax.all_to_all(place_send, "tok", split_axis=0, concat_axis=0, tiled=True)
    items = slot_rows.shape[1]
    query_three = (
        jnp.einsum("scd,df->scf", slot_rows, query_weight[0], preferred_element_type=jnp.float32)
        .astype(jnp.bfloat16)
        .reshape(tok_count * items, head_count, HEAD_DIM)
    )
    query_place = slot_places.reshape(tok_count * items)

    def one_turn(state_in, turn_data):
        row_max, row_sums, weighted = state_in
        keys_values, cached_turn, usable_turn, place_turn = turn_data
        usable = jnp.where(
            cached_turn[None, :], usable_turn[None, :], place_turn[None, :] <= query_place[:, None]
        )[None]
        scores = (
            jnp.einsum(
                "phd,khd->hpk", query_three, keys_values[:, 0], preferred_element_type=jnp.float32
            )
            * score_scale
        )
        scores = jnp.where(usable, scores, -1e30)
        new_max = jnp.maximum(row_max, jnp.max(scores, axis=-1))
        weights = jnp.where(usable, jnp.exp(scores - new_max[..., None]), 0.0).astype(jnp.bfloat16)
        factor = jnp.exp(row_max - new_max)
        row_sums = row_sums * factor + jnp.sum(weights.astype(jnp.float32), axis=-1)
        weighted = weighted * factor[..., None] + jnp.einsum(
            "hpk,khd->hpd", weights, keys_values[:, 1], preferred_element_type=jnp.float32
        )
        return ((new_max, row_sums, weighted), None)

    query_total = tok_count * items
    initial = (
        jnp.full((head_count, query_total), -1e30, jnp.float32),
        jnp.zeros((head_count, query_total), jnp.float32),
        jnp.zeros((head_count, query_total, HEAD_DIM), jnp.float32),
    )
    final_state, _ = lax.scan(one_turn, initial, (key_turns, cached, cache_usable, fresh_place))
    row_max, row_sums, weighted = final_state
    attended = (
        (weighted / row_sums[..., None])
        .astype(jnp.bfloat16)
        .transpose(1, 0, 2)
        .reshape(tok_count, items, group_width)
    )
    parts = jnp.einsum(
        "scf,fd->scd", attended, output_weight[0], preferred_element_type=jnp.float32
    ).astype(jnp.bfloat16)
    output_back = lax.all_to_all(parts, "tok", split_axis=0, concat_axis=0, tiled=True)
    output_sums = group_sum(output_back, experts, groups, CAP)
    mixed_rows = (
        residual_in + jnp.dot(attn_weights, output_sums, precision=lax.Precision.HIGHEST)
    ).astype(jnp.bfloat16)
    hidden_two = normed(mixed_rows.astype(jnp.float32), feedforward_gain).astype(jnp.bfloat16)
    ffn_routes = feedforward_routes[0]
    ffn_pairs = slot_matrix(ffn_routes, experts, CAP)
    ffn_gate = router_gates(hidden_two, feedforward_router, ffn_routes)
    ffn_pick, ffn_weights = token_matrices(ffn_pairs, ffn_gate, top_count)
    every_rows, every_routes = (
        lax.all_gather(hidden_two, "tok", axis=0, tiled=True),
        lax.all_gather(ffn_routes, "tok", axis=0, tiled=True),
    )
    routes_all = every_routes.reshape(tok_count, query_rows, top_count)

    def source_slots(routes_block):
        return slot_matrix(routes_block, experts, CAP)

    per_source = jax.vmap(source_slots)(routes_all)
    per_token = jnp.sum(per_source.reshape(tok_count, query_rows, top_count, experts, CAP), axis=2)
    expert_mask = (jnp.arange(experts, dtype=jnp.int32) == tok_index // groups).astype(jnp.float32)
    picked = jnp.einsum("sqec,e->sqc", per_token, expert_mask)
    received = jnp.einsum(
        "sqc,sqd->scd",
        picked.astype(jnp.bfloat16),
        every_rows.reshape(tok_count, query_rows, model_width),
        preferred_element_type=jnp.float32,
    ).astype(jnp.bfloat16)
    expert_parts = expert_feedforward(received, gate_up[0], down_weight[0])
    expert_back = lax.all_to_all(expert_parts, "tok", split_axis=0, concat_axis=0, tiled=True)
    expert_sums = group_sum(expert_back, experts, groups, CAP)
    layer_output = (
        mixed_rows.astype(jnp.float32)
        + jnp.dot(ffn_weights, expert_sums, precision=lax.Precision.HIGHEST)
    ).astype(jnp.bfloat16)
    return (layer_output[None], new_keys_values[None])


PAD = 8
LANES = 128
FF_TILE = 512
WIRE = 4


def column_stream(source, buffers, sems, tile):
    count = buffers.shape[0]
    skipped = source.shape[1] // tile - count
    return [
        pltpu.make_async_copy(
            source.at[:, pl.ds((skipped + step) * tile, tile)], buffers.at[step], sems.at[step]
        )
        for step in range(count)
    ]


def permute(values, axis, pairs):
    return lax.ppermute(values, axis, pairs)


def swap_all(values, axis):
    return lax.all_to_all(values, axis, split_axis=0, concat_axis=0, tiled=True)


def whole_spec():
    return pl.BlockSpec(memory_space=pltpu.VMEM)


def index_spec():
    return pl.BlockSpec(memory_space=pltpu.SMEM)


def iota(shape, axis):
    return lax.broadcasted_iota(jnp.int32, shape, axis)


def any_spec():
    return pl.BlockSpec(memory_space=pl.ANY)


def in_hbm(*arrays):
    return [pltpu.with_memory_space_constraint(one, pltpu.HBM) for one in arrays]


def in_vmem(*arrays):
    return [pltpu.with_memory_space_constraint(one, pltpu.VMEM) for one in arrays]


def load_all(pairs, sems):
    copies = [
        pltpu.make_async_copy(source, target, sems.at[number])
        for number, (source, target) in enumerate(pairs)
    ]
    for one in copies:
        one.start()
    for one in copies:
        one.wait()


def padded_picks(routes, experts, height):
    row_count = routes.shape[1]
    row = iota((experts * height, row_count), 0)
    expert, slot = row // height, row % height
    first, second = routes[0:1, :] == expert, routes[1:2, :] == expert
    named = jnp.where(first, 1.0, 0.0) + jnp.where(second, 1.0, 0.0)
    earlier = (iota((row_count, row_count), 0) < iota((row_count, row_count), 1)).astype(
        jnp.bfloat16
    )
    before = jnp.dot(
        named.astype(jnp.bfloat16), earlier, preferred_element_type=jnp.float32
    ).astype(jnp.int32)
    here = (before == slot) & (slot < CAP)
    return named * here.astype(jnp.float32), first


def gate_weights(hidden, router, routes, picks, first):
    logits = lax.dot_general(
        router, hidden, (((1,), (1,)), ((), ())), preferred_element_type=jnp.float32
    )
    label = iota(logits.shape, 0)
    one = jnp.sum(jnp.where(routes[0:1, :] == label, logits, 0.0), axis=0, keepdims=True)
    two = jnp.sum(jnp.where(routes[1:2, :] == label, logits, 0.0), axis=0, keepdims=True)
    gate_one = 1.0 / (1.0 + jnp.exp(two - one))
    gate_two = 1.0 / (1.0 + jnp.exp(one - two))
    return picks * jnp.where(first, gate_one, gate_two)


def row_norm(values, gain):
    mean = jnp.mean(values * values, axis=-1, keepdims=True)
    return (values * lax.rsqrt(mean + 1e-06) * gain).astype(jnp.bfloat16)


def pick_rows(picks, rows):
    return jnp.dot(picks.astype(jnp.bfloat16), rows, preferred_element_type=jnp.float32)


def compact(rows):
    count = rows.shape[0] // PAD * CAP
    one, two = iota((count, rows.shape[0]), 0), iota((count, rows.shape[0]), 1)
    chosen = ((one // CAP) * PAD + one % CAP == two).astype(jnp.bfloat16)
    return jnp.dot(chosen, rows, preferred_element_type=jnp.float32)


def wire_order(blocks, columns):
    total = blocks * columns * CAP
    row = iota((total, total), 0)
    block, column, slot = row // (columns * CAP), row // CAP % columns, row % CAP
    return (column * (blocks * CAP) + block * CAP + slot == iota((total, total), 1)).astype(
        jnp.bfloat16
    )


def pack(pieces, blocks):
    columns, span = len(pieces), pieces[0].shape[1]
    stacked = jnp.concatenate(pieces, axis=0)
    moved = jnp.dot(wire_order(blocks, columns), stacked, preferred_element_type=jnp.float32)
    return moved.reshape(blocks, columns * CAP, span).astype(jnp.bfloat16)


def split_columns(rows):
    span = rows.shape[1] // WIRE
    return [rows[:, step * span : (step + 1) * span] for step in range(WIRE)]


def unpack(values):
    blocks, height, span = values.shape
    columns = height // CAP
    flat = values.astype(jnp.float32).reshape(blocks * height, span).astype(jnp.bfloat16)
    moved = lax.dot_general(
        wire_order(blocks, columns),
        flat,
        (((0,), (0,)), ((), ())),
        preferred_element_type=jnp.float32,
    ).astype(jnp.bfloat16)
    rows = blocks * CAP
    return jnp.concatenate(
        [moved[step * rows : (step + 1) * rows] for step in range(columns)], axis=1
    )


def exact_mix(weights, rows):
    high = weights.astype(jnp.bfloat16)
    rest = weights - high.astype(jnp.float32)
    middle = rest.astype(jnp.bfloat16)
    low = (rest - middle.astype(jnp.float32)).astype(jnp.bfloat16)
    count = weights.shape[1]
    stacked = lax.dot_general(
        jnp.concatenate([high, middle, low], axis=1),
        rows,
        (((0,), (0,)), ((), ())),
        preferred_element_type=jnp.float32,
    )
    return stacked[:count] + (stacked[count : 2 * count] + stacked[2 * count :])


def prepare(activations, gain, router, routes, tok_count):
    rows, width = activations.shape
    experts = router.shape[0]
    span = width // tok_count
    half = rows // 2
    per_row = width // (2 * span)

    def body(
        act_in, gain_in, router_in, route_in, out_ref, weight_ref,
        act_ref, gain_ref, router_ref, route_ref, wide, copy, sems,
    ):
        load_all(
            [
                (act_in, act_ref),
                (gain_in, gain_ref),
                (router_in, router_ref),
                (route_in, route_ref),
            ],
            sems,
        )
        route = route_ref[...]
        hidden = row_norm(act_ref[...].astype(jnp.float32), gain_ref[...])
        picks, _ = padded_picks(route, experts, PAD)
        wide[...] = pick_rows(picks, hidden)
        copy[...] = hidden.astype(jnp.float32)
        for dest in range(tok_count):
            chip, core = dest // 2, dest % 2
            for place in range(half):
                row = dest * PAD + CAP + place // per_row
                for side in range(2):
                    column = (place % per_row) * 2 * span + side * span
                    source = (2 * chip + (core ^ side)) * span
                    wide[row : row + 1, column : column + span] = copy[
                        core * half + place : core * half + place + 1, source : source + span
                    ]
        out_ref[:, :, :width] = wide[...].astype(jnp.bfloat16).reshape(tok_count, PAD, width)
        number = iota((rows, LANES), 0).astype(jnp.float32).astype(jnp.bfloat16)
        out_ref[:, :, width:] = (
            pick_rows(picks, number).astype(jnp.bfloat16).reshape(tok_count, PAD, LANES)
        )
        narrow, first = padded_picks(route, experts, CAP)
        weight_ref[...] = gate_weights(hidden, router_ref[...], route, narrow, first)

    return pl.pallas_call(
        body,
        in_specs=[any_spec()] * 4,
        out_specs=[whole_spec()] * 2,
        out_shape=[
            jax.ShapeDtypeStruct((tok_count, PAD, width + LANES), jnp.bfloat16),
            jax.ShapeDtypeStruct((tok_count * CAP, rows), jnp.float32),
        ],
        scratch_shapes=[
            pltpu.VMEM((rows, width), activations.dtype),
            pltpu.VMEM((1, width), gain.dtype),
            pltpu.VMEM(router.shape, router.dtype),
            pltpu.VMEM(routes.shape, routes.dtype),
            pltpu.VMEM((tok_count * PAD, width), jnp.float32),
            pltpu.VMEM((rows, width), jnp.float32),
            pltpu.SemaphoreType.DMA((4,)),
        ],
        compiler_params=pltpu.CompilerParams(vmem_limit_bytes=4 << 20),
        name="prepare",
    )(*in_hbm(activations, gain.reshape(1, width), router, routes))


def cache_split(cache_part, side, place, after):
    rows, width = cache_part.shape
    count = 8
    span = width // 2 // count

    def body(index_ref, cache_ref, side_ref, after_ref, *refs):
        outs, side_out, sems = refs[:5], refs[5], refs[6]
        pairs = []
        for number in range(count):
            turn, side = number // 2, number % 2
            out, base = (outs[turn + 1], side * rows) if turn else (outs[side], 0)
            start = pl.multiple_of((index_ref[2] ^ number) * span, span)
            for kind in range(2):
                pairs.append(
                    (
                        cache_ref.at[:, pl.ds(kind * (width // 2) + start, span)],
                        out.at[base : base + rows, kind * span : (kind + 1) * span],
                    )
                )
        pairs.append((side_ref, side_out))
        load_all(pairs, sems)

    shapes = [(rows, 2 * span)] * 2 + [(2 * rows, 2 * span)] * 3
    return pl.pallas_call(
        body,
        in_specs=[index_spec()] + [any_spec()] * 3,
        out_specs=[whole_spec()] * 6,
        out_shape=[jax.ShapeDtypeStruct(one, cache_part.dtype) for one in shapes]
        + [pltpu.VMEM(side.shape, side.dtype)],
        scratch_shapes=[pltpu.SemaphoreType.DMA((2 * count + 1,))],
        compiler_params=pltpu.CompilerParams(vmem_limit_bytes=4 << 20),
        name="cache_split",
    )(place, *in_hbm(cache_part, side), after)


def cache_relay(near, turned):
    rows, width = near.shape

    def body(near_ref, *refs):
        out_ref = refs[-1]
        out_ref[:rows, :] = near_ref[...]
        for turn in range(1, 4):
            out_ref[turn * rows : (turn + 1) * rows, :] = refs[turn - 1][rows:, :]

    return pl.pallas_call(
        body,
        in_specs=[whole_spec()] * 4,
        out_specs=whole_spec(),
        out_shape=jax.ShapeDtypeStruct((4 * rows, width), near.dtype),
        compiler_params=pltpu.CompilerParams(vmem_limit_bytes=3 << 20),
        name="cache_relay",
    )(near, *turned)


def own_tokens(arrived, after, tok_count, width):
    span = width // tok_count
    per_row = width // (2 * span)
    extra = PAD - CAP

    def body(in_ref, *rest):
        out_ref, wide = rest[len(after) :]
        for source in range(tok_count):
            rows = in_ref[source, :, :width].astype(jnp.float32)
            for part in range(extra):
                for place in range(per_row):
                    row = source * extra * per_row + part * per_row + place
                    wide[row : row + 1, :] = rows[
                        CAP + part : CAP + part + 1, place * 2 * span : (place + 1) * 2 * span
                    ]
        out_ref[...] = wide[...].astype(jnp.bfloat16)

    count = tok_count * extra * per_row
    return pl.pallas_call(
        body,
        in_specs=[whole_spec()] + [any_spec()] * len(after),
        out_specs=whole_spec(),
        out_shape=jax.ShapeDtypeStruct((count, 2 * span), jnp.bfloat16),
        scratch_shapes=[pltpu.VMEM((count, 2 * span), jnp.float32)],
        compiler_params=pltpu.CompilerParams(vmem_limit_bytes=4 << 20),
        name="own_tokens",
    )(arrived, *after)


def query_project(arrived, weight, after, tok_count):
    width = weight.shape[0]
    span = width // tok_count
    slots = tok_count * CAP
    height = slots + PAD
    tile = 2 * span
    steps = width // tile

    def body(in_ref, weight_ref, *rest):
        out_ref, held, sems = rest[len(after) :]
        copies = column_stream(weight_ref, held, sems, tile)
        for one in copies:
            one.start()
        every = compact(in_ref[...].reshape(tok_count * PAD, width + LANES))
        rows = every[:, :width].astype(jnp.bfloat16)
        local = every[:, width : width + LANES]
        mine = iota(local.shape, 0)
        placed = local + ((mine // CAP) * (2 * PAD)).astype(jnp.float32)
        placed = jnp.where(mine == iota(local.shape, 1), placed, 0.0)
        line = jnp.broadcast_to(jnp.sum(placed, axis=0, keepdims=True), (PAD, LANES))
        line = jnp.concatenate([line] * (span // LANES), axis=1).astype(jnp.bfloat16)
        for step in range(steps):
            copies[step].wait()
            query = jnp.dot(rows, held[step], preferred_element_type=jnp.float32).astype(
                jnp.bfloat16
            )
            for one in range(tile // span):
                place = step * (tile // span) + one
                out_ref[place, :slots, :] = query[:, one * span : (one + 1) * span]
                out_ref[place, slots:, :] = line
    return pl.pallas_call(
        body,
        in_specs=[whole_spec(), any_spec()] + [any_spec()] * len(after),
        out_specs=whole_spec(),
        out_shape=jax.ShapeDtypeStruct((tok_count, height, span), jnp.bfloat16),
        scratch_shapes=[
            pltpu.VMEM((steps, width, tile), jnp.bfloat16),
            pltpu.SemaphoreType.DMA((steps,)),
        ],
        compiler_params=pltpu.CompilerParams(vmem_limit_bytes=14 << 20),
        cost_estimate=pl.CostEstimate(flops=0, transcendentals=0, bytes_accessed=40 << 20),
        name="query_project",
    )(arrived, *in_hbm(weight), *after)


def key_value_parts(tokens, weight, sibling, place, after):
    rows, depth = tokens[0].shape
    half = depth // 2
    quarter = weight.shape[1] // 4
    count = len(tokens)

    def body(place_ref, *refs):
        token_refs, weight_ref, sibling_ref = refs[:count], refs[count], refs[count + 1]
        outs = refs[count + 2 + len(after) :]
        stacked = jnp.concatenate([one[...] for one in token_refs], axis=0)
        for turn in range(4):
            start = pl.multiple_of(((place_ref[2] // 2) ^ turn) * quarter, quarter)
            part = jnp.dot(
                stacked[:, :half],
                weight_ref[:, pl.ds(start, quarter)],
                preferred_element_type=jnp.float32,
            ) + jnp.dot(
                stacked[:, half:],
                sibling_ref[:, pl.ds(start, quarter)],
                preferred_element_type=jnp.float32,
            )
            outs[turn][...] = part.astype(outs[turn].dtype)

    shapes = [
        jax.ShapeDtypeStruct((count * rows, quarter), jnp.float32 if turn == 0 else jnp.bfloat16)
        for turn in range(4)
    ]
    return pl.pallas_call(
        body,
        in_specs=[index_spec()] + [whole_spec()] * (count + 2) + [any_spec()] * len(after),
        out_specs=[whole_spec()] * 4,
        out_shape=shapes,
        compiler_params=pltpu.CompilerParams(vmem_limit_bytes=8 << 20),
        name="key_value_parts",
    )(place, *tokens, weight, sibling, *after)


def key_value_sum(parts, place, after):
    rows, quarter = parts[0].shape
    block = rows // 4

    def body(place_ref, *refs):
        ins, outs = refs[:4], refs[5:]
        req = place_ref[1]
        source = (req // 2) * 2 + place_ref[2] % 2
        for turn in range(4):
            start = pl.multiple_of((req ^ source ^ turn) * block, block)
            total = ins[0][pl.ds(start, block), :]
            for one in ins[1:]:
                total = total + one[pl.ds(start, block), :].astype(jnp.float32)
            outs[turn][...] = total.astype(jnp.bfloat16)

    return pl.pallas_call(
        body,
        in_specs=[index_spec()] + [whole_spec()] * 4 + [any_spec()],
        out_specs=[whole_spec()] * 4,
        out_shape=[jax.ShapeDtypeStruct((block, quarter), jnp.bfloat16)] * 4,
        compiler_params=pltpu.CompilerParams(vmem_limit_bytes=4 << 20),
        name="key_value_sum",
    )(place, *parts, after)


def attention(message, scalars, fresh_blocks, own, turned, relayed, weight):
    blocks, _, span = message.shape
    heads = span // HEAD_DIM
    slots = blocks * CAP
    fresh_rows = fresh_blocks[0].shape[0]
    half = fresh_rows // blocks
    cache_rows = own.shape[0]
    scale = 1.0 / math.sqrt(HEAD_DIM)
    contract = (((1,), (1,)), ((), ()))
    tile = weight.shape[1] // WIRE

    def body(scalar_ref, in_ref, *refs):
        fresh_refs, own_ref, turned_refs, relay_ref = refs[:4], refs[4], refs[5:8], refs[8]
        weight_ref, out_ref, held_ref, sem = refs[9:]
        fetch = pltpu.make_async_copy(weight_ref.at[:, pl.ds(0, tile)], held_ref, sem)
        fetch.start()
        limit, req, tok = scalar_ref[0], scalar_ref[1], scalar_ref[2]
        pieces = []
        for source in range(4):
            picked = fresh_refs[3][...]
            for turn in range(3):
                picked = jnp.where((req ^ source) == turn, fresh_refs[turn][...], picked)
            pieces.append(picked)
        new_keys = jnp.concatenate(pieces[:2], axis=0)
        new_values = jnp.concatenate(pieces[2:], axis=0)
        key_row = iota((1, blocks * cache_rows), 1)
        key_block = key_row // cache_rows
        key_source = ((key_block % 4) * 2 + key_block // 4) ^ tok
        cache_usable = key_source * cache_rows + key_row % cache_rows < limit
        new_row = iota((1, 2 * fresh_rows), 1)
        within = new_row % fresh_rows
        new_place = (within // half) * (2 * half) + (new_row // fresh_rows) * half + within % half
        places = []
        for expert in range(blocks):
            line = in_ref[expert, slots:, :LANES].astype(jnp.float32)[0:1]
            chosen = iota((slots, LANES), 0) == iota((slots, LANES), 1)
            places.append(jnp.sum(jnp.where(chosen, line, 0.0), axis=1, keepdims=True))
        new_usable = new_place <= jnp.concatenate(places, axis=0).astype(jnp.int32)
        flat = in_ref[:, :slots, :].reshape(blocks * slots, span)
        cached = [own_ref] + [one.at[:cache_rows] for one in turned_refs] + [relay_ref]
        keys = jnp.concatenate([one[:, :span] for one in cached], axis=0)
        values = jnp.concatenate([one[:, span:] for one in cached], axis=0)
        for head in range(heads):
            cols = slice(head * HEAD_DIM, (head + 1) * HEAD_DIM)
            query = flat[:, cols]
            first = lax.dot_general(
                query, keys[:, cols], contract, preferred_element_type=jnp.float32
            )
            second = lax.dot_general(
                query, new_keys[:, cols], contract, preferred_element_type=jnp.float32
            )
            first = jnp.where(cache_usable, first * scale, -1e30)
            second = jnp.where(new_usable, second * scale, -1e30)
            top = jnp.maximum(
                jnp.max(first, axis=-1, keepdims=True), jnp.max(second, axis=-1, keepdims=True)
            )
            first = jnp.exp(first - top).astype(jnp.bfloat16)
            second = jnp.exp(second - top).astype(jnp.bfloat16)
            sums = jnp.sum(first.astype(jnp.float32), axis=-1, keepdims=True) + jnp.sum(
                second.astype(jnp.float32), axis=-1, keepdims=True
            )
            mixed = jnp.dot(first, values[:, cols], preferred_element_type=jnp.float32) + jnp.dot(
                second, new_values[:, cols], preferred_element_type=jnp.float32
            )
            out_ref[:, :slots, cols] = (
                (mixed / sums).astype(jnp.bfloat16).reshape(blocks, slots, HEAD_DIM)
            )
        for kind in range(2):
            for part in range(2):
                start = slots + kind * 2 * half + part * half
                out_ref[:, start : start + half, :] = pieces[2 * kind + part].reshape(
                    blocks, half, span
                )
        fetch.wait()

    return pl.pallas_call(
        body,
        in_specs=[index_spec()] + [whole_spec()] * 10 + [any_spec()],
        out_specs=[whole_spec()] * 2,
        out_shape=[
            jax.ShapeDtypeStruct((blocks, slots + 4 * half, span), jnp.bfloat16),
            pltpu.VMEM((weight.shape[0], tile), jnp.bfloat16),
        ],
        scratch_shapes=[pltpu.SemaphoreType.DMA(())],
        compiler_params=pltpu.CompilerParams(vmem_limit_bytes=14 << 20),
        name="attention",
    )(scalars, message, *fresh_blocks, own, *turned, relayed, *in_hbm(weight))


def output_project(arrived, weight, ready, query_rows):
    blocks, height, span = arrived.shape
    slots = blocks * CAP
    width = weight.shape[1]
    tile = width // WIRE

    def body(in_ref, weight_ref, ready_ref, out_ref, fresh_ref, held, sems):
        copies = column_stream(weight_ref, held, sems, tile)
        for one in copies:
            one.start()
        rows, pieces = [], []
        for block in range(blocks):
            cols = slice(block * span, (block + 1) * span)
            rows.append(in_ref[block, :slots, :])
            fresh_ref[:, cols] = in_ref[block, slots : slots + query_rows, :]
            fresh_ref[:, block * span + width : (block + 1) * span + width] = in_ref[
                block, slots + query_rows :, :
            ]
        rows = jnp.concatenate(rows, axis=1)
        for step in range(width // tile):
            if step:
                copies[step - 1].wait()
            tile_weight = held[step - 1] if step else ready_ref[...]
            part = jnp.dot(rows, tile_weight, preferred_element_type=jnp.float32)
            pieces.append(part.astype(jnp.bfloat16))
        out_ref[...] = pack(pieces, blocks)

    return pl.pallas_call(
        body,
        in_specs=[whole_spec(), any_spec(), whole_spec()],
        out_specs=[whole_spec()] * 2,
        out_shape=[
            jax.ShapeDtypeStruct((blocks, WIRE * CAP, tile), jnp.bfloat16),
            jax.ShapeDtypeStruct((query_rows, 2 * width), jnp.bfloat16),
        ],
        scratch_shapes=[
            pltpu.VMEM((width // tile - 1, blocks * span, tile), jnp.bfloat16),
            pltpu.SemaphoreType.DMA((width // tile - 1,)),
        ],
        compiler_params=pltpu.CompilerParams(vmem_limit_bytes=14 << 20),
        name="output_project",
    )(arrived, *in_hbm(weight), *in_vmem(ready))


def middle(activations, arrived, weights, gain, router, routes, gate_piece):
    rows, width = activations.shape
    blocks = arrived.shape[0]
    experts = router.shape[0]

    def body(
        act_ref, in_ref, old_ref, gain_ref, router_ref, route_ref, gate_ref,
        out_ref, mix_ref, new_ref, held_ref, sem,
    ):
        fetch = pltpu.make_async_copy(gate_ref.at[:, pl.ds(0, FF_TILE)], held_ref, sem)
        fetch.start()
        route = route_ref[...]
        added = exact_mix(old_ref[...], unpack(in_ref[...]))
        mixed = (act_ref[...].astype(jnp.float32) + added).astype(jnp.bfloat16)
        mix_ref[...] = mixed
        hidden = row_norm(mixed.astype(jnp.float32), gain_ref[...])
        picks, first = padded_picks(route, experts, CAP)
        out_ref[...] = pack(split_columns(pick_rows(picks, hidden).astype(jnp.bfloat16)), blocks)
        new_ref[...] = gate_weights(hidden, router_ref[...], route, picks, first)
        fetch.wait()

    return pl.pallas_call(
        body,
        in_specs=[whole_spec()] * 6 + [any_spec()],
        out_specs=[whole_spec()] * 4,
        out_shape=[
            jax.ShapeDtypeStruct(arrived.shape, jnp.bfloat16),
            jax.ShapeDtypeStruct((rows, width), jnp.bfloat16),
            jax.ShapeDtypeStruct((blocks * CAP, rows), jnp.float32),
            pltpu.VMEM((width, FF_TILE), jnp.bfloat16),
        ],
        scratch_shapes=[pltpu.SemaphoreType.DMA(())],
        compiler_params=pltpu.CompilerParams(vmem_limit_bytes=4 << 20),
        name="middle",
    )(activations, arrived, weights, gain.reshape(1, width), router, routes, *in_hbm(gate_piece))


def finish(mixed, arrived, weights):
    rows, width = mixed.shape

    def body(mix_ref, in_ref, weight_ref, out_ref):
        added = exact_mix(weight_ref[...], unpack(in_ref[...]))
        out_ref[...] = (mix_ref[...].astype(jnp.float32) + added).astype(jnp.bfloat16)

    return pl.pallas_call(
        body,
        in_specs=[whole_spec()] * 3,
        out_specs=whole_spec(),
        out_shape=jax.ShapeDtypeStruct((rows, width), jnp.bfloat16),
        compiler_params=pltpu.CompilerParams(vmem_limit_bytes=4 << 20),
        name="finish",
    )(mixed, arrived, weights)


def feedforward(arrived, gate_piece, down_piece, ready):
    blocks, width = arrived.shape[0], down_piece.shape[1]
    count = blocks * CAP
    units = down_piece.shape[0]
    tile = FF_TILE
    steps = units // tile
    slots = 4

    def body(in_ref, gate_ref, down_ref, ready_ref, out_ref, gates, ups, downs, sems):
        def copies(step):
            slot = step % slots
            return [
                pltpu.make_async_copy(
                    gate_ref.at[:, pl.ds(step * tile, tile)], gates.at[slot], sems.at[slot, 0]
                ),
                pltpu.make_async_copy(
                    gate_ref.at[:, pl.ds(units + step * tile, tile)],
                    ups.at[slot],
                    sems.at[slot, 1],
                ),
                pltpu.make_async_copy(
                    down_ref.at[pl.ds(step * tile, tile), :], downs.at[slot], sems.at[slot, 2]
                ),
            ]

        for step in range(slots):
            for one in copies(step)[0 if step else 1 :]:
                one.start()
        rows = unpack(in_ref[...])
        total = jnp.zeros((count, width), jnp.float32)
        for step in range(steps):
            slot = step % slots
            gate_copy, up_copy, down_copy = copies(step)
            if step:
                gate_copy.wait()
            gate_tile = gates[slot] if step else ready_ref[...]
            gate = jnp.dot(rows, gate_tile, preferred_element_type=jnp.float32)
            up_copy.wait()
            up = jnp.dot(rows, ups[slot], preferred_element_type=jnp.float32)
            active = (gate / (1.0 + jnp.exp(-gate)) * up).astype(jnp.bfloat16)
            down_copy.wait()
            total = total + jnp.dot(active, downs[slot], preferred_element_type=jnp.float32)
            if step + slots < steps:
                for one in copies(step + slots):
                    one.start()
        out_ref[...] = pack(split_columns(total.astype(jnp.bfloat16)), blocks)

    return pl.pallas_call(
        body,
        in_specs=[whole_spec(), any_spec(), any_spec(), whole_spec()],
        out_specs=whole_spec(),
        out_shape=jax.ShapeDtypeStruct(arrived.shape, jnp.bfloat16),
        scratch_shapes=[
            pltpu.VMEM((slots, width, tile), jnp.bfloat16),
            pltpu.VMEM((slots, width, tile), jnp.bfloat16),
            pltpu.VMEM((slots, tile, width), jnp.bfloat16),
            pltpu.SemaphoreType.DMA((slots, 3)),
        ],
        compiler_params=pltpu.CompilerParams(vmem_limit_bytes=32 << 20),
        name="feedforward",
    )(arrived, *in_hbm(gate_piece, down_piece), *in_vmem(ready))


def local_heads(
    activations,
    cache_entries,
    cache_lengths,
    attention_gain,
    feedforward_gain,
    key_value_weight,
    attention_router,
    attention_routes,
    query_weight,
    output_weight,
    feedforward_router,
    feedforward_routes,
    gate_up,
    down_weight,
):
    tok_count = lax.axis_size("tok")
    req_count = lax.axis_size("req")
    tok_index = lax.axis_index("tok")
    req_index = lax.axis_index("req")
    query_rows, width = activations.shape[1:]

    attn_routes = attention_routes[0].T
    ffn_routes = feedforward_routes[0].T
    place = jnp.stack([cache_lengths[0], req_index, tok_index])
    message, attn_weights = prepare(
        activations[0], attention_gain, attention_router.T, attn_routes, tok_count
    )
    arrived = swap_all(message, "tok")
    own_block, near, *turned, weight_held = cache_split(
        cache_entries[0], key_value_weight, place, attn_weights
    )
    turned = [
        permute(turned[turn - 1], "tok", [(one, one ^ (2 * turn)) for one in range(tok_count)])
        for turn in range(1, 4)
    ]
    pair = [(one, one ^ 1) for one in range(tok_count)]
    sibling = permute(key_value_weight, "tok", pair)
    mine = own_tokens(arrived, [sibling], tok_count, width)
    tokens = [mine] + [
        permute(mine, "req", [(one, one ^ turn) for one in range(req_count)])
        for turn in range(1, req_count)
    ]
    parts = key_value_parts(tokens, weight_held, sibling, place, turned)
    projected = query_project(arrived, query_weight[0], parts[:1], tok_count)
    parts = [parts[0]] + [
        permute(parts[turn], "tok", [(one, one ^ (2 * turn)) for one in range(tok_count)])
        for turn in range(1, 4)
    ]
    projected, *gate = lax.optimization_barrier((projected, *parts[1:], *turned))
    parts[1:], turned = gate[:3], gate[3:]
    sums = key_value_sum(parts, place, projected)
    queries = swap_all(projected, "tok")
    relayed = permute(cache_relay(near, turned), "tok", pair)
    fresh_blocks = []
    for turn in range(4):
        pairs = []
        for one in range(req_count * tok_count):
            r, t = one // tok_count, one % tok_count
            dest = ((r // 2) * 2 + t % 2) ^ turn
            pairs.append((one, dest * tok_count + 4 * (r % 2) + t // 2))
        fresh_blocks.append(permute(sums[turn], ("req", "tok"), pairs))
    attended, output_ready = attention(
        queries, place, fresh_blocks, own_block, turned, relayed, output_weight[0]
    )
    attended = swap_all(attended, "tok")
    parts_out, new_keys_values = output_project(
        attended, output_weight[0], output_ready, query_rows
    )
    output_back = swap_all(parts_out, "tok")
    ffn_send, mixed_rows, ffn_weights, gate_ready = middle(
        activations[0],
        output_back,
        attn_weights,
        feedforward_gain,
        feedforward_router.T,
        ffn_routes,
        gate_up[0],
    )
    received = swap_all(ffn_send, "tok")
    expert_parts = feedforward(received, gate_up[0], down_weight[0], gate_ready)
    expert_back = swap_all(expert_parts, "tok")
    layer_output = finish(mixed_rows, expert_back, ffn_weights)
    return (layer_output[None], new_keys_values[None])


def solution(mesh):
    placed = (
        P("req", "tok", None),
        P("req", "tok", None),
        P("req"),
        P(),
        P(),
        P("tok", "req"),
        P(),
        P("req", "tok", None),
        P("tok", None, None),
        P("tok", None, None),
        P(),
        P("req", "tok", None),
        P("tok", None, None),
        P("tok", None, None),
    )
    sizes = dict(mesh.shape)
    by_heads = sizes["tok"] == 8 and sizes["req"] == 4
    return jax.shard_map(
        local_heads if by_heads else local,
        mesh=mesh,
        in_specs=placed,
        out_specs=(P("req", "tok", None), P("req", "tok", None)),
        check_vma=False,
    )
```

```python
import math

import jax
import jax.numpy as jnp
from jax import lax
from jax.experimental import pallas as pl
from jax.experimental.pallas import tpu as pltpu
from jax.sharding import PartitionSpec as P

HEADS = 16
HEAD_DIM = 128
CAP = 6


def normed(values, gain):
    scale_rows = lax.rsqrt(jnp.mean(values * values, axis=-1, keepdims=True) + 1e-06)
    return values * scale_rows * gain


def slot_matrix(routes, experts, capacity):
    row_count, top_count = routes.shape
    labels = jnp.arange(experts, dtype=jnp.int32)
    onehot = (routes.reshape(row_count * top_count, 1) == labels[None, :]).astype(jnp.int32)
    before = jnp.cumsum(onehot, axis=0) - onehot
    within = jnp.sum(before * onehot, axis=1)
    placed = routes.reshape(row_count * top_count) * capacity + within
    columns = jnp.arange(experts * capacity, dtype=jnp.int32)
    return (placed[:, None] == columns[None, :]).astype(jnp.float32)


def router_gates(hidden, router, routes):
    logits = jnp.dot(hidden, router, preferred_element_type=jnp.float32)
    picked = jnp.take_along_axis(logits, routes, axis=1)
    return jax.nn.sigmoid(2.0 * picked - jnp.sum(picked, axis=1, keepdims=True))


def token_matrices(pair_slots, gates, top_count):
    row_count = gates.shape[0]
    per_token = pair_slots.reshape(row_count, top_count, -1)
    picked = jnp.sum(per_token, axis=1)
    weighted = jnp.sum(per_token * gates[:, :, None], axis=1)
    return (picked, weighted)


def spread_slots(slot_rows, experts, groups, capacity):
    feat_width = slot_rows.shape[-1]
    shaped = slot_rows.reshape(experts, 1, capacity, feat_width)
    return jnp.broadcast_to(shaped, (experts, groups, capacity, feat_width)).reshape(
        experts * groups, capacity, feat_width
    )


def head_groups(rows, experts, groups, group_width):
    row_count = rows.shape[0]
    shaped = (
        rows.reshape(row_count, 2, groups, group_width)
        .transpose(2, 0, 1, 3)
        .reshape(groups, row_count, 2 * group_width)
    )
    return jnp.broadcast_to(shaped[None], (experts, groups, row_count, 2 * group_width)).reshape(
        experts * groups, row_count, 2 * group_width
    )


def group_sum(received, experts, groups, capacity):
    feat_width = received.shape[-1]
    summed = jnp.sum(
        received.reshape(experts, groups, capacity, feat_width).astype(jnp.float32), axis=1
    )
    return summed.reshape(experts * capacity, feat_width)


def expert_feedforward(received, gate_piece, down_piece):
    units = down_piece.shape[0]
    projected = jnp.einsum("scd,df->scf", received, gate_piece, preferred_element_type=jnp.float32)
    active = (jax.nn.silu(projected[..., :units]) * projected[..., units:]).astype(jnp.bfloat16)
    return jnp.einsum("scf,fd->scd", active, down_piece, preferred_element_type=jnp.float32).astype(
        jnp.bfloat16
    )


def local(
    activations,
    cache_entries,
    cache_lengths,
    attention_gain,
    feedforward_gain,
    key_value_weight,
    attention_router,
    attention_routes,
    query_weight,
    output_weight,
    feedforward_router,
    feedforward_routes,
    gate_up,
    down_weight,
):
    tok_count = lax.axis_size("tok")
    tok_index = lax.axis_index("tok")
    experts = attention_router.shape[1]
    groups = tok_count // experts
    query_rows = activations.shape[1]
    cache_rows = cache_entries.shape[1]
    top_count = attention_routes.shape[2]
    model_width = activations.shape[2]
    head_count = HEADS // groups
    group_width = head_count * HEAD_DIM
    block_span = cache_rows + query_rows
    score_scale = 1.0 / math.sqrt(HEAD_DIM)
    cache_part = cache_entries[0]
    residual_in = activations[0].astype(jnp.float32)
    hidden = normed(residual_in, attention_gain).astype(jnp.bfloat16)
    stacked = lax.all_gather(hidden, "req", axis=0, tiled=True)
    projected_part = jnp.dot(
        stacked,
        lax.all_gather(key_value_weight, "tok", axis=0, tiled=True),
        preferred_element_type=jnp.float32,
    )
    new_keys_values = lax.all_to_all(
        projected_part.astype(jnp.bfloat16), "req", split_axis=0, concat_axis=1, tiled=True
    )
    combined = jnp.concatenate([cache_part, new_keys_values], axis=0)
    group_keys = lax.all_to_all(
        head_groups(combined, experts, groups, group_width),
        "tok",
        split_axis=0,
        concat_axis=0,
        tiled=True,
    )
    attn_routes = attention_routes[0]
    attn_pairs = slot_matrix(attn_routes, experts, CAP)
    attn_gate = router_gates(hidden, attention_router, attn_routes)
    attn_pick, attn_weights = token_matrices(attn_pairs, attn_gate, top_count)
    slot_inputs = jnp.dot(
        attn_pick.T.astype(jnp.bfloat16), hidden, preferred_element_type=jnp.float32
    ).astype(jnp.bfloat16)
    token_place = tok_index * query_rows + jnp.arange(query_rows, dtype=jnp.int32)
    slot_place = jnp.sum(attn_pick.astype(jnp.int32) * token_place[:, None], axis=0)
    query_send = spread_slots(slot_inputs, experts, groups, CAP)
    place_send = jnp.broadcast_to(
        slot_place.reshape(experts, 1, CAP), (experts, groups, CAP)
    ).reshape(tok_count, CAP)
    length = cache_lengths[0]
    source = jnp.arange(tok_count, dtype=jnp.int32).reshape(groups, experts, 1)
    offset = jnp.arange(block_span, dtype=jnp.int32).reshape(1, 1, block_span)
    turn_shape = (groups, experts * block_span)
    cached = jnp.broadcast_to(offset < cache_rows, (groups, experts, block_span)).reshape(
        turn_shape
    )
    cache_usable = (source * cache_rows + offset < length).reshape(turn_shape)
    fresh_place = (source * query_rows + offset - cache_rows).reshape(turn_shape)
    key_turns = group_keys.reshape(groups, experts * block_span, 2, head_count, HEAD_DIM)
    slot_rows = lax.all_to_all(query_send, "tok", split_axis=0, concat_axis=0, tiled=True)
    slot_places = lax.all_to_all(place_send, "tok", split_axis=0, concat_axis=0, tiled=True)
    items = slot_rows.shape[1]
    query_three = (
        jnp.einsum("scd,df->scf", slot_rows, query_weight[0], preferred_element_type=jnp.float32)
        .astype(jnp.bfloat16)
        .reshape(tok_count * items, head_count, HEAD_DIM)
    )
    query_place = slot_places.reshape(tok_count * items)

    def one_turn(state_in, turn_data):
        row_max, row_sums, weighted = state_in
        keys_values, cached_turn, usable_turn, place_turn = turn_data
        usable = jnp.where(
            cached_turn[None, :], usable_turn[None, :], place_turn[None, :] <= query_place[:, None]
        )[None]
        scores = (
            jnp.einsum(
                "phd,khd->hpk", query_three, keys_values[:, 0], preferred_element_type=jnp.float32
            )
            * score_scale
        )
        scores = jnp.where(usable, scores, -1e30)
        new_max = jnp.maximum(row_max, jnp.max(scores, axis=-1))
        weights = jnp.where(usable, jnp.exp(scores - new_max[..., None]), 0.0).astype(jnp.bfloat16)
        factor = jnp.exp(row_max - new_max)
        row_sums = row_sums * factor + jnp.sum(weights.astype(jnp.float32), axis=-1)
        weighted = weighted * factor[..., None] + jnp.einsum(
            "hpk,khd->hpd", weights, keys_values[:, 1], preferred_element_type=jnp.float32
        )
        return ((new_max, row_sums, weighted), None)

    query_total = tok_count * items
    initial = (
        jnp.full((head_count, query_total), -1e30, jnp.float32),
        jnp.zeros((head_count, query_total), jnp.float32),
        jnp.zeros((head_count, query_total, HEAD_DIM), jnp.float32),
    )
    final_state, _ = lax.scan(one_turn, initial, (key_turns, cached, cache_usable, fresh_place))
    row_max, row_sums, weighted = final_state
    attended = (
        (weighted / row_sums[..., None])
        .astype(jnp.bfloat16)
        .transpose(1, 0, 2)
        .reshape(tok_count, items, group_width)
    )
    parts = jnp.einsum(
        "scf,fd->scd", attended, output_weight[0], preferred_element_type=jnp.float32
    ).astype(jnp.bfloat16)
    output_back = lax.all_to_all(parts, "tok", split_axis=0, concat_axis=0, tiled=True)
    output_sums = group_sum(output_back, experts, groups, CAP)
    mixed_rows = (
        residual_in + jnp.dot(attn_weights, output_sums, precision=lax.Precision.HIGHEST)
    ).astype(jnp.bfloat16)
    hidden_two = normed(mixed_rows.astype(jnp.float32), feedforward_gain).astype(jnp.bfloat16)
    ffn_routes = feedforward_routes[0]
    ffn_pairs = slot_matrix(ffn_routes, experts, CAP)
    ffn_gate = router_gates(hidden_two, feedforward_router, ffn_routes)
    ffn_pick, ffn_weights = token_matrices(ffn_pairs, ffn_gate, top_count)
    every_rows, every_routes = (
        lax.all_gather(hidden_two, "tok", axis=0, tiled=True),
        lax.all_gather(ffn_routes, "tok", axis=0, tiled=True),
    )
    routes_all = every_routes.reshape(tok_count, query_rows, top_count)

    def source_slots(routes_block):
        return slot_matrix(routes_block, experts, CAP)

    per_source = jax.vmap(source_slots)(routes_all)
    per_token = jnp.sum(per_source.reshape(tok_count, query_rows, top_count, experts, CAP), axis=2)
    expert_mask = (jnp.arange(experts, dtype=jnp.int32) == tok_index // groups).astype(jnp.float32)
    picked = jnp.einsum("sqec,e->sqc", per_token, expert_mask)
    received = jnp.einsum(
        "sqc,sqd->scd",
        picked.astype(jnp.bfloat16),
        every_rows.reshape(tok_count, query_rows, model_width),
        preferred_element_type=jnp.float32,
    ).astype(jnp.bfloat16)
    expert_parts = expert_feedforward(received, gate_up[0], down_weight[0])
    expert_back = lax.all_to_all(expert_parts, "tok", split_axis=0, concat_axis=0, tiled=True)
    expert_sums = group_sum(expert_back, experts, groups, CAP)
    layer_output = (
        mixed_rows.astype(jnp.float32)
        + jnp.dot(ffn_weights, expert_sums, precision=lax.Precision.HIGHEST)
    ).astype(jnp.bfloat16)
    return (layer_output[None], new_keys_values[None])


PAD = 8
LANES = 128
FF_TILE = 512
WIRE = 4


def column_stream(source, buffers, sems, tile):
    return [
        pltpu.make_async_copy(
            source.at[:, pl.ds(step * tile, tile)], buffers.at[step], sems.at[step]
        )
        for step in range(buffers.shape[0])
    ]


def permute(values, axis, pairs):
    return lax.ppermute(values, axis, pairs)


def swap_all(values, axis):
    return lax.all_to_all(values, axis, split_axis=0, concat_axis=0, tiled=True)


def whole_spec():
    return pl.BlockSpec(memory_space=pltpu.VMEM)


def index_spec():
    return pl.BlockSpec(memory_space=pltpu.SMEM)


def iota(shape, axis):
    return lax.broadcasted_iota(jnp.int32, shape, axis)


def any_spec():
    return pl.BlockSpec(memory_space=pl.ANY)


def in_hbm(*arrays):
    return [pltpu.with_memory_space_constraint(one, pltpu.HBM) for one in arrays]


def in_vmem(*arrays):
    return [pltpu.with_memory_space_constraint(one, pltpu.VMEM) for one in arrays]


def load_all(pairs, sems):
    copies = [
        pltpu.make_async_copy(source, target, sems.at[number])
        for number, (source, target) in enumerate(pairs)
    ]
    for one in copies:
        one.start()
    for one in copies:
        one.wait()


def padded_picks(routes, experts, height):
    row_count = routes.shape[1]
    row = iota((experts * height, row_count), 0)
    expert, slot = row // height, row % height
    first, second = routes[0:1, :] == expert, routes[1:2, :] == expert
    named = jnp.where(first, 1.0, 0.0) + jnp.where(second, 1.0, 0.0)
    earlier = (iota((row_count, row_count), 0) < iota((row_count, row_count), 1)).astype(
        jnp.bfloat16
    )
    before = jnp.dot(
        named.astype(jnp.bfloat16), earlier, preferred_element_type=jnp.float32
    ).astype(jnp.int32)
    here = (before == slot) & (slot < CAP)
    return named * here.astype(jnp.float32), first


def gate_weights(hidden, router, routes, picks, first):
    logits = lax.dot_general(
        router, hidden, (((1,), (1,)), ((), ())), preferred_element_type=jnp.float32
    )
    label = iota(logits.shape, 0)
    one = jnp.sum(jnp.where(routes[0:1, :] == label, logits, 0.0), axis=0, keepdims=True)
    two = jnp.sum(jnp.where(routes[1:2, :] == label, logits, 0.0), axis=0, keepdims=True)
    gate_one = 1.0 / (1.0 + jnp.exp(two - one))
    gate_two = 1.0 / (1.0 + jnp.exp(one - two))
    return picks * jnp.where(first, gate_one, gate_two)


def row_norm(values, gain):
    mean = jnp.mean(values * values, axis=-1, keepdims=True)
    return (values * lax.rsqrt(mean + 1e-06) * gain).astype(jnp.bfloat16)


def pick_rows(picks, rows):
    return jnp.dot(picks.astype(jnp.bfloat16), rows, preferred_element_type=jnp.float32)


def compact(rows):
    count = rows.shape[0] // PAD * CAP
    one, two = iota((count, rows.shape[0]), 0), iota((count, rows.shape[0]), 1)
    chosen = ((one // CAP) * PAD + one % CAP == two).astype(jnp.bfloat16)
    return jnp.dot(chosen, rows, preferred_element_type=jnp.float32)


def wire_order(blocks, columns):
    total = blocks * columns * CAP
    row = iota((total, total), 0)
    block, column, slot = row // (columns * CAP), row // CAP % columns, row % CAP
    return (column * (blocks * CAP) + block * CAP + slot == iota((total, total), 1)).astype(
        jnp.bfloat16
    )


def pack(pieces, blocks):
    columns, span = len(pieces), pieces[0].shape[1]
    stacked = jnp.concatenate(pieces, axis=0)
    moved = jnp.dot(wire_order(blocks, columns), stacked, preferred_element_type=jnp.float32)
    return moved.reshape(blocks, columns * CAP, span).astype(jnp.bfloat16)


def split_columns(rows):
    span = rows.shape[1] // WIRE
    return [rows[:, step * span : (step + 1) * span] for step in range(WIRE)]


def unpack(values):
    blocks, height, span = values.shape
    columns = height // CAP
    flat = values.astype(jnp.float32).reshape(blocks * height, span).astype(jnp.bfloat16)
    moved = lax.dot_general(
        wire_order(blocks, columns),
        flat,
        (((0,), (0,)), ((), ())),
        preferred_element_type=jnp.float32,
    ).astype(jnp.bfloat16)
    rows = blocks * CAP
    return jnp.concatenate(
        [moved[step * rows : (step + 1) * rows] for step in range(columns)], axis=1
    )


def exact_mix(weights, rows):
    high = weights.astype(jnp.bfloat16)
    rest = weights - high.astype(jnp.float32)
    middle = rest.astype(jnp.bfloat16)
    low = (rest - middle.astype(jnp.float32)).astype(jnp.bfloat16)
    count = weights.shape[1]
    stacked = lax.dot_general(
        jnp.concatenate([high, middle, low], axis=1),
        rows,
        (((0,), (0,)), ((), ())),
        preferred_element_type=jnp.float32,
    )
    return stacked[:count] + (stacked[count : 2 * count] + stacked[2 * count :])


def prepare(activations, gain, router, routes, tok_count):
    rows, width = activations.shape
    experts = router.shape[0]
    span = width // tok_count
    half = rows // 2
    per_row = width // (2 * span)

    def body(
        act_in, gain_in, router_in, route_in, out_ref, weight_ref,
        act_ref, gain_ref, router_ref, route_ref, wide, copy, sems,
    ):
        load_all(
            [
                (act_in, act_ref),
                (gain_in, gain_ref),
                (router_in, router_ref),
                (route_in, route_ref),
            ],
            sems,
        )
        route = route_ref[...]
        hidden = row_norm(act_ref[...].astype(jnp.float32), gain_ref[...])
        picks, _ = padded_picks(route, experts, PAD)
        wide[...] = pick_rows(picks, hidden)
        copy[...] = hidden.astype(jnp.float32)
        for dest in range(tok_count):
            chip, core = dest // 2, dest % 2
            for place in range(half):
                row = dest * PAD + CAP + place // per_row
                for side in range(2):
                    column = (place % per_row) * 2 * span + side * span
                    source = (2 * chip + (core ^ side)) * span
                    wide[row : row + 1, column : column + span] = copy[
                        core * half + place : core * half + place + 1, source : source + span
                    ]
        out_ref[:, :, :width] = wide[...].astype(jnp.bfloat16).reshape(tok_count, PAD, width)
        number = iota((rows, LANES), 0).astype(jnp.float32).astype(jnp.bfloat16)
        out_ref[:, :, width:] = (
            pick_rows(picks, number).astype(jnp.bfloat16).reshape(tok_count, PAD, LANES)
        )
        narrow, first = padded_picks(route, experts, CAP)
        weight_ref[...] = gate_weights(hidden, router_ref[...], route, narrow, first)

    return pl.pallas_call(
        body,
        in_specs=[any_spec()] * 4,
        out_specs=[whole_spec()] * 2,
        out_shape=[
            jax.ShapeDtypeStruct((tok_count, PAD, width + LANES), jnp.bfloat16),
            jax.ShapeDtypeStruct((tok_count * CAP, rows), jnp.float32),
        ],
        scratch_shapes=[
            pltpu.VMEM((rows, width), activations.dtype),
            pltpu.VMEM((1, width), gain.dtype),
            pltpu.VMEM(router.shape, router.dtype),
            pltpu.VMEM(routes.shape, routes.dtype),
            pltpu.VMEM((tok_count * PAD, width), jnp.float32),
            pltpu.VMEM((rows, width), jnp.float32),
            pltpu.SemaphoreType.DMA((4,)),
        ],
        compiler_params=pltpu.CompilerParams(vmem_limit_bytes=4 << 20),
        name="prepare",
    )(*in_hbm(activations, gain.reshape(1, width), router, routes))


def cache_split(cache_part, side, place, after):
    rows, width = cache_part.shape
    count = 8
    span = width // 2 // count

    def body(index_ref, cache_ref, side_ref, after_ref, *refs):
        outs, side_out, sems = refs[:5], refs[5], refs[6]
        pairs = []
        for number in range(count):
            turn, side = number // 2, number % 2
            out, base = (outs[turn + 1], side * rows) if turn else (outs[side], 0)
            start = pl.multiple_of((index_ref[2] ^ number) * span, span)
            for kind in range(2):
                pairs.append(
                    (
                        cache_ref.at[:, pl.ds(kind * (width // 2) + start, span)],
                        out.at[base : base + rows, kind * span : (kind + 1) * span],
                    )
                )
        pairs.append((side_ref, side_out))
        load_all(pairs, sems)

    shapes = [(rows, 2 * span)] * 2 + [(2 * rows, 2 * span)] * 3
    return pl.pallas_call(
        body,
        in_specs=[index_spec()] + [any_spec()] * 3,
        out_specs=[whole_spec()] * 6,
        out_shape=[jax.ShapeDtypeStruct(one, cache_part.dtype) for one in shapes]
        + [pltpu.VMEM(side.shape, side.dtype)],
        scratch_shapes=[pltpu.SemaphoreType.DMA((2 * count + 1,))],
        compiler_params=pltpu.CompilerParams(vmem_limit_bytes=4 << 20),
        name="cache_split",
    )(place, *in_hbm(cache_part, side), after)


def cache_relay(near, turned, after):
    rows, width = near.shape

    def body(near_ref, *refs):
        out_ref = refs[-1]
        out_ref[:rows, :] = near_ref[...]
        for turn in range(1, 4):
            out_ref[turn * rows : (turn + 1) * rows, :] = refs[turn - 1][rows:, :]

    return pl.pallas_call(
        body,
        in_specs=[whole_spec()] * 4 + [any_spec()],
        out_specs=whole_spec(),
        out_shape=jax.ShapeDtypeStruct((4 * rows, width), near.dtype),
        compiler_params=pltpu.CompilerParams(vmem_limit_bytes=3 << 20),
        name="cache_relay",
    )(near, *turned, after)


def own_tokens(arrived, after, tok_count, width):
    span = width // tok_count
    per_row = width // (2 * span)
    extra = PAD - CAP

    def body(in_ref, *rest):
        out_ref, wide = rest[len(after) :]
        for source in range(tok_count):
            rows = in_ref[source, :, :width].astype(jnp.float32)
            for part in range(extra):
                for place in range(per_row):
                    row = source * extra * per_row + part * per_row + place
                    wide[row : row + 1, :] = rows[
                        CAP + part : CAP + part + 1, place * 2 * span : (place + 1) * 2 * span
                    ]
        out_ref[...] = wide[...].astype(jnp.bfloat16)

    count = tok_count * extra * per_row
    return pl.pallas_call(
        body,
        in_specs=[whole_spec()] + [any_spec()] * len(after),
        out_specs=whole_spec(),
        out_shape=jax.ShapeDtypeStruct((count, 2 * span), jnp.bfloat16),
        scratch_shapes=[pltpu.VMEM((count, 2 * span), jnp.float32)],
        compiler_params=pltpu.CompilerParams(vmem_limit_bytes=4 << 20),
        name="own_tokens",
    )(arrived, *after)


def query_project(arrived, weight, after, tok_count):
    width = weight.shape[0]
    span = width // tok_count
    slots = tok_count * CAP
    height = slots + PAD
    tile = 2 * span
    steps = width // tile

    def body(in_ref, weight_ref, *rest):
        out_ref, held, sems = rest[len(after) :]
        copies = column_stream(weight_ref, held, sems, tile)
        for one in copies:
            one.start()
        every = compact(in_ref[...].reshape(tok_count * PAD, width + LANES))
        rows = every[:, :width].astype(jnp.bfloat16)
        local = every[:, width : width + LANES]
        mine = iota(local.shape, 0)
        placed = local + ((mine // CAP) * (2 * PAD)).astype(jnp.float32)
        placed = jnp.where(mine == iota(local.shape, 1), placed, 0.0)
        line = jnp.broadcast_to(jnp.sum(placed, axis=0, keepdims=True), (PAD, LANES))
        line = jnp.concatenate([line] * (span // LANES), axis=1).astype(jnp.bfloat16)
        for step in range(steps):
            copies[step].wait()
            query = jnp.dot(rows, held[step], preferred_element_type=jnp.float32).astype(
                jnp.bfloat16
            )
            for one in range(tile // span):
                place = step * (tile // span) + one
                out_ref[place, :slots, :] = query[:, one * span : (one + 1) * span]
                out_ref[place, slots:, :] = line
    return pl.pallas_call(
        body,
        in_specs=[whole_spec(), any_spec()] + [any_spec()] * len(after),
        out_specs=whole_spec(),
        out_shape=jax.ShapeDtypeStruct((tok_count, height, span), jnp.bfloat16),
        scratch_shapes=[
            pltpu.VMEM((steps, width, tile), jnp.bfloat16),
            pltpu.SemaphoreType.DMA((steps,)),
        ],
        compiler_params=pltpu.CompilerParams(vmem_limit_bytes=14 << 20),
        cost_estimate=pl.CostEstimate(flops=0, transcendentals=0, bytes_accessed=40 << 20),
        name="query_project",
    )(arrived, *in_hbm(weight), *after)


def key_value_parts(tokens, weight, sibling, place, after):
    rows, depth = tokens[0].shape
    half = depth // 2
    quarter = weight.shape[1] // 4
    count = len(tokens)

    def body(place_ref, *refs):
        token_refs, weight_ref, sibling_ref = refs[:count], refs[count], refs[count + 1]
        outs = refs[count + 2 + len(after) :]
        stacked = jnp.concatenate([one[...] for one in token_refs], axis=0)
        for turn in range(4):
            start = pl.multiple_of(((place_ref[2] // 2) ^ turn) * quarter, quarter)
            part = jnp.dot(
                stacked[:, :half],
                weight_ref[:, pl.ds(start, quarter)],
                preferred_element_type=jnp.float32,
            ) + jnp.dot(
                stacked[:, half:],
                sibling_ref[:, pl.ds(start, quarter)],
                preferred_element_type=jnp.float32,
            )
            outs[turn][...] = part.astype(outs[turn].dtype)

    shapes = [
        jax.ShapeDtypeStruct((count * rows, quarter), jnp.float32 if turn == 0 else jnp.bfloat16)
        for turn in range(4)
    ]
    return pl.pallas_call(
        body,
        in_specs=[index_spec()] + [whole_spec()] * (count + 2) + [any_spec()] * len(after),
        out_specs=[whole_spec()] * 4,
        out_shape=shapes,
        compiler_params=pltpu.CompilerParams(vmem_limit_bytes=8 << 20),
        name="key_value_parts",
    )(place, *tokens, weight, sibling, *after)


def key_value_sum(parts, place, after):
    rows, quarter = parts[0].shape
    block = rows // 4

    def body(place_ref, *refs):
        ins, outs = refs[:4], refs[5:]
        req = place_ref[1]
        source = (req // 2) * 2 + place_ref[2] % 2
        for turn in range(4):
            start = pl.multiple_of((req ^ source ^ turn) * block, block)
            total = ins[0][pl.ds(start, block), :]
            for one in ins[1:]:
                total = total + one[pl.ds(start, block), :].astype(jnp.float32)
            outs[turn][...] = total.astype(jnp.bfloat16)

    return pl.pallas_call(
        body,
        in_specs=[index_spec()] + [whole_spec()] * 4 + [any_spec()],
        out_specs=[whole_spec()] * 4,
        out_shape=[jax.ShapeDtypeStruct((block, quarter), jnp.bfloat16)] * 4,
        compiler_params=pltpu.CompilerParams(vmem_limit_bytes=4 << 20),
        name="key_value_sum",
    )(place, *parts, after)


def attention(message, scalars, fresh_blocks, own, turned, relayed):
    blocks, _, span = message.shape
    heads = span // HEAD_DIM
    slots = blocks * CAP
    fresh_rows = fresh_blocks[0].shape[0]
    half = fresh_rows // blocks
    cache_rows = own.shape[0]
    scale = 1.0 / math.sqrt(HEAD_DIM)
    contract = (((1,), (1,)), ((), ()))

    def body(scalar_ref, in_ref, *refs):
        fresh_refs, own_ref, turned_refs, relay_ref = refs[:4], refs[4], refs[5:8], refs[8]
        out_ref = refs[9]
        limit, req, tok = scalar_ref[0], scalar_ref[1], scalar_ref[2]
        pieces = []
        for source in range(4):
            picked = fresh_refs[3][...]
            for turn in range(3):
                picked = jnp.where((req ^ source) == turn, fresh_refs[turn][...], picked)
            pieces.append(picked)
        new_keys = jnp.concatenate(pieces[:2], axis=0)
        new_values = jnp.concatenate(pieces[2:], axis=0)
        key_row = iota((1, blocks * cache_rows), 1)
        key_block = key_row // cache_rows
        key_source = ((key_block % 4) * 2 + key_block // 4) ^ tok
        cache_usable = key_source * cache_rows + key_row % cache_rows < limit
        new_row = iota((1, 2 * fresh_rows), 1)
        within = new_row % fresh_rows
        new_place = (within // half) * (2 * half) + (new_row // fresh_rows) * half + within % half
        places = []
        for expert in range(blocks):
            line = in_ref[expert, slots:, :LANES].astype(jnp.float32)[0:1]
            chosen = iota((slots, LANES), 0) == iota((slots, LANES), 1)
            places.append(jnp.sum(jnp.where(chosen, line, 0.0), axis=1, keepdims=True))
        new_usable = new_place <= jnp.concatenate(places, axis=0).astype(jnp.int32)
        flat = in_ref[:, :slots, :].reshape(blocks * slots, span)
        cached = [own_ref] + [one.at[:cache_rows] for one in turned_refs] + [relay_ref]
        keys = jnp.concatenate([one[:, :span] for one in cached], axis=0)
        values = jnp.concatenate([one[:, span:] for one in cached], axis=0)
        for head in range(heads):
            cols = slice(head * HEAD_DIM, (head + 1) * HEAD_DIM)
            query = flat[:, cols]
            first = lax.dot_general(
                query, keys[:, cols], contract, preferred_element_type=jnp.float32
            )
            second = lax.dot_general(
                query, new_keys[:, cols], contract, preferred_element_type=jnp.float32
            )
            first = jnp.where(cache_usable, first * scale, -1e30)
            second = jnp.where(new_usable, second * scale, -1e30)
            top = jnp.maximum(
                jnp.max(first, axis=-1, keepdims=True), jnp.max(second, axis=-1, keepdims=True)
            )
            first = jnp.exp(first - top).astype(jnp.bfloat16)
            second = jnp.exp(second - top).astype(jnp.bfloat16)
            sums = jnp.sum(first.astype(jnp.float32), axis=-1, keepdims=True) + jnp.sum(
                second.astype(jnp.float32), axis=-1, keepdims=True
            )
            mixed = jnp.dot(first, values[:, cols], preferred_element_type=jnp.float32) + jnp.dot(
                second, new_values[:, cols], preferred_element_type=jnp.float32
            )
            out_ref[:, :slots, cols] = (
                (mixed / sums).astype(jnp.bfloat16).reshape(blocks, slots, HEAD_DIM)
            )
        for kind in range(2):
            for part in range(2):
                start = slots + kind * 2 * half + part * half
                out_ref[:, start : start + half, :] = pieces[2 * kind + part].reshape(
                    blocks, half, span
                )

    return pl.pallas_call(
        body,
        in_specs=[index_spec()] + [whole_spec()] * 10,
        out_specs=whole_spec(),
        out_shape=jax.ShapeDtypeStruct((blocks, slots + 4 * half, span), jnp.bfloat16),
        compiler_params=pltpu.CompilerParams(vmem_limit_bytes=14 << 20),
        name="attention",
    )(scalars, message, *fresh_blocks, own, *turned, relayed)


def output_project(arrived, weight, query_rows):
    blocks, height, span = arrived.shape
    slots = blocks * CAP
    width = weight.shape[1]
    tile = width // WIRE

    def body(in_ref, weight_ref, out_ref, fresh_ref, held, sems):
        copies = column_stream(weight_ref, held, sems, tile)
        for one in copies:
            one.start()
        rows, pieces = [], []
        for block in range(blocks):
            cols = slice(block * span, (block + 1) * span)
            rows.append(in_ref[block, :slots, :])
            fresh_ref[:, cols] = in_ref[block, slots : slots + query_rows, :]
            fresh_ref[:, block * span + width : (block + 1) * span + width] = in_ref[
                block, slots + query_rows :, :
            ]
        rows = jnp.concatenate(rows, axis=1)
        for step in range(width // tile):
            copies[step].wait()
            part = jnp.dot(rows, held[step], preferred_element_type=jnp.float32)
            pieces.append(part.astype(jnp.bfloat16))
        out_ref[...] = pack(pieces, blocks)

    return pl.pallas_call(
        body,
        in_specs=[whole_spec(), any_spec()],
        out_specs=[whole_spec()] * 2,
        out_shape=[
            jax.ShapeDtypeStruct((blocks, WIRE * CAP, tile), jnp.bfloat16),
            jax.ShapeDtypeStruct((query_rows, 2 * width), jnp.bfloat16),
        ],
        scratch_shapes=[
            pltpu.VMEM((width // tile, blocks * span, tile), jnp.bfloat16),
            pltpu.SemaphoreType.DMA((width // tile,)),
        ],
        compiler_params=pltpu.CompilerParams(vmem_limit_bytes=14 << 20),
        name="output_project",
    )(arrived, *in_hbm(weight))


def middle(activations, arrived, weights, gain, router, routes):
    rows, width = activations.shape
    blocks = arrived.shape[0]
    experts = router.shape[0]

    def body(act_ref, in_ref, old_ref, gain_ref, router_ref, route_ref, out_ref, mix_ref, new_ref):
        route = route_ref[...]
        added = exact_mix(old_ref[...], unpack(in_ref[...]))
        mixed = (act_ref[...].astype(jnp.float32) + added).astype(jnp.bfloat16)
        mix_ref[...] = mixed
        hidden = row_norm(mixed.astype(jnp.float32), gain_ref[...])
        picks, first = padded_picks(route, experts, CAP)
        out_ref[...] = pack(split_columns(pick_rows(picks, hidden).astype(jnp.bfloat16)), blocks)
        new_ref[...] = gate_weights(hidden, router_ref[...], route, picks, first)

    return pl.pallas_call(
        body,
        in_specs=[whole_spec()] * 6,
        out_specs=[whole_spec()] * 3,
        out_shape=[
            jax.ShapeDtypeStruct(arrived.shape, jnp.bfloat16),
            jax.ShapeDtypeStruct((rows, width), jnp.bfloat16),
            jax.ShapeDtypeStruct((blocks * CAP, rows), jnp.float32),
        ],
        compiler_params=pltpu.CompilerParams(vmem_limit_bytes=4 << 20),
        name="middle",
    )(activations, arrived, weights, gain.reshape(1, width), router, routes)


def finish(mixed, arrived, weights):
    rows, width = mixed.shape

    def body(mix_ref, in_ref, weight_ref, out_ref):
        added = exact_mix(weight_ref[...], unpack(in_ref[...]))
        out_ref[...] = (mix_ref[...].astype(jnp.float32) + added).astype(jnp.bfloat16)

    return pl.pallas_call(
        body,
        in_specs=[whole_spec()] * 3,
        out_specs=whole_spec(),
        out_shape=jax.ShapeDtypeStruct((rows, width), jnp.bfloat16),
        compiler_params=pltpu.CompilerParams(vmem_limit_bytes=4 << 20),
        name="finish",
    )(mixed, arrived, weights)


def feedforward(arrived, gate_piece, down_piece):
    blocks, width = arrived.shape[0], down_piece.shape[1]
    count = blocks * CAP
    units = down_piece.shape[0]
    tile = FF_TILE
    steps = units // tile
    slots = 4

    def body(in_ref, gate_ref, down_ref, out_ref, gates, ups, downs, sems):
        def copies(step):
            slot = step % slots
            return [
                pltpu.make_async_copy(
                    gate_ref.at[:, pl.ds(step * tile, tile)], gates.at[slot], sems.at[slot, 0]
                ),
                pltpu.make_async_copy(
                    gate_ref.at[:, pl.ds(units + step * tile, tile)],
                    ups.at[slot],
                    sems.at[slot, 1],
                ),
                pltpu.make_async_copy(
                    down_ref.at[pl.ds(step * tile, tile), :], downs.at[slot], sems.at[slot, 2]
                ),
            ]

        for step in range(slots):
            for one in copies(step):
                one.start()
        rows = unpack(in_ref[...])
        total = jnp.zeros((count, width), jnp.float32)
        for step in range(steps):
            slot = step % slots
            gate_copy, up_copy, down_copy = copies(step)
            gate_copy.wait()
            gate = jnp.dot(rows, gates[slot], preferred_element_type=jnp.float32)
            up_copy.wait()
            up = jnp.dot(rows, ups[slot], preferred_element_type=jnp.float32)
            active = (gate / (1.0 + jnp.exp(-gate)) * up).astype(jnp.bfloat16)
            down_copy.wait()
            total = total + jnp.dot(active, downs[slot], preferred_element_type=jnp.float32)
            if step + slots < steps:
                for one in copies(step + slots):
                    one.start()
        out_ref[...] = pack(split_columns(total.astype(jnp.bfloat16)), blocks)

    return pl.pallas_call(
        body,
        in_specs=[whole_spec(), any_spec(), any_spec()],
        out_specs=whole_spec(),
        out_shape=jax.ShapeDtypeStruct(arrived.shape, jnp.bfloat16),
        scratch_shapes=[
            pltpu.VMEM((slots, width, tile), jnp.bfloat16),
            pltpu.VMEM((slots, width, tile), jnp.bfloat16),
            pltpu.VMEM((slots, tile, width), jnp.bfloat16),
            pltpu.SemaphoreType.DMA((slots, 3)),
        ],
        compiler_params=pltpu.CompilerParams(vmem_limit_bytes=32 << 20),
        name="feedforward",
    )(arrived, *in_hbm(gate_piece, down_piece))


def local_heads(
    activations,
    cache_entries,
    cache_lengths,
    attention_gain,
    feedforward_gain,
    key_value_weight,
    attention_router,
    attention_routes,
    query_weight,
    output_weight,
    feedforward_router,
    feedforward_routes,
    gate_up,
    down_weight,
):
    tok_count = lax.axis_size("tok")
    req_count = lax.axis_size("req")
    tok_index = lax.axis_index("tok")
    req_index = lax.axis_index("req")
    query_rows, width = activations.shape[1:]

    attn_routes = attention_routes[0].T
    ffn_routes = feedforward_routes[0].T
    place = jnp.stack([cache_lengths[0], req_index, tok_index])
    message, attn_weights = prepare(
        activations[0], attention_gain, attention_router.T, attn_routes, tok_count
    )
    arrived = swap_all(message, "tok")
    own_block, near, *turned, weight_held = cache_split(
        cache_entries[0], key_value_weight, place, attn_weights
    )
    turned = [
        permute(turned[turn - 1], "tok", [(one, one ^ (2 * turn)) for one in range(tok_count)])
        for turn in range(1, 4)
    ]
    pair = [(one, one ^ 1) for one in range(tok_count)]
    sibling = permute(key_value_weight, "tok", pair)
    mine = own_tokens(arrived, [sibling], tok_count, width)
    tokens = [mine] + [
        permute(mine, "req", [(one, one ^ turn) for one in range(req_count)])
        for turn in range(1, req_count)
    ]
    parts = key_value_parts(tokens, weight_held, sibling, place, turned)
    projected = query_project(arrived, query_weight[0], parts[:1], tok_count)
    parts = [parts[0]] + [
        permute(parts[turn], "tok", [(one, one ^ (2 * turn)) for one in range(tok_count)])
        for turn in range(1, 4)
    ]
    projected, *gate = lax.optimization_barrier((projected, *parts[1:], *turned))
    parts[1:], turned = gate[:3], gate[3:]
    sums = key_value_sum(parts, place, projected)
    queries = swap_all(projected, "tok")
    relayed = permute(cache_relay(near, turned, sums[0]), "tok", pair)
    fresh_blocks = []
    for turn in range(4):
        pairs = []
        for one in range(req_count * tok_count):
            r, t = one // tok_count, one % tok_count
            dest = ((r // 2) * 2 + t % 2) ^ turn
            pairs.append((one, dest * tok_count + 4 * (r % 2) + t // 2))
        fresh_blocks.append(permute(sums[turn], ("req", "tok"), pairs))
    attended = attention(queries, place, fresh_blocks, own_block, turned, relayed)
    attended = swap_all(attended, "tok")
    parts_out, new_keys_values = output_project(attended, output_weight[0], query_rows)
    output_back = swap_all(parts_out, "tok")
    ffn_send, mixed_rows, ffn_weights = middle(
        activations[0],
        output_back,
        attn_weights,
        feedforward_gain,
        feedforward_router.T,
        ffn_routes,
    )
    received = swap_all(ffn_send, "tok")
    expert_parts = feedforward(received, gate_up[0], down_weight[0])
    expert_back = swap_all(expert_parts, "tok")
    layer_output = finish(mixed_rows, expert_back, ffn_weights)
    return (layer_output[None], new_keys_values[None])


def solution(mesh):
    placed = (
        P("req", "tok", None),
        P("req", "tok", None),
        P("req"),
        P(),
        P(),
        P("tok", "req"),
        P(),
        P("req", "tok", None),
        P("tok", None, None),
        P("tok", None, None),
        P(),
        P("req", "tok", None),
        P("tok", None, None),
        P("tok", None, None),
    )
    sizes = dict(mesh.shape)
    by_heads = sizes["tok"] == 8 and sizes["req"] == 4
    return jax.shard_map(
        local_heads if by_heads else local,
        mesh=mesh,
        in_specs=placed,
        out_specs=(P("req", "tok", None), P("req", "tok", None)),
        check_vma=False,
    )
```
